32 devices in a mesh: dp: 8 (over z, core), fsdp: 4 (over y, x).
Axes of the slice: x: 2, y: 2, z: 4, core: 2. Of those that a mesh axis runs over, the one named last changes fastest.
Arguments:
- tokens: bfloat16 [32, 1024, 768], P(('dp', 'fsdp')), may hold values from -6 to 6
- lengths: int32 [32], P(('dp', 'fsdp')), may hold values from 1 to 1024, as said below
- keep_attn: int32 [32, 1024, 768], P(('dp', 'fsdp')), may hold values 0 or 1
- keep_ffn: int32 [32, 1024, 768], P(('dp', 'fsdp')), may hold values 0 or 1
- partners: int32 [32], replicated, may hold values from 0 to 31, as said below
- out_cot: bfloat16 [32, 1024, 768], P(('dp', 'fsdp')), may hold values from -6 to 6
- w_qkv: bfloat16 [768, 2304], P(('dp', 'fsdp')), may hold values from -0.21875 to 0.21875
- b_qv: bfloat16 [1536], P(('dp', 'fsdp')), may hold values from -3 to 3
- w_out: bfloat16 [768, 768], P(('dp', 'fsdp')), may hold values from -6 to 6
- b_out: bfloat16 [768], P(('dp', 'fsdp')), may hold values from -3 to 3
- ln1_gain: bfloat16 [768], P(('dp', 'fsdp')), may hold values from 0.099609375 to 1.8984375
- ln1_bias: bfloat16 [768], P(('dp', 'fsdp')), may hold values from -3 to 3
- w_up: bfloat16 [768, 3072], P(('dp', 'fsdp')), may hold values from -0.21875 to 0.21875
- b_up: bfloat16 [3072], P(('dp', 'fsdp')), may hold values from -3 to 3
- w_down: bfloat16 [3072, 768], P(('dp', 'fsdp')), may hold values from -0.109375 to 0.109375
- b_down: bfloat16 [768], P(('dp', 'fsdp')), may hold values from -3 to 3
- ln2_gain: bfloat16 [768], P(('dp', 'fsdp')), may hold values from 0.099609375 to 1.8984375
- ln2_bias: bfloat16 [768], P(('dp', 'fsdp')), may hold values from -3 to 3
- w_pool: bfloat16 [768, 768], P(('dp', 'fsdp')), may hold values from -0.21875 to 0.21875
- b_pool: bfloat16 [768], P(('dp', 'fsdp')), may hold values from -3 to 3
Outputs:
- layer_out: bfloat16 [32, 1024, 768], P(('dp', 'fsdp'))
- tokens_grad: bfloat16 [32, 1024, 768], P(('dp', 'fsdp'))
- grad_w_qkv: float32 [768, 2304], P(('dp', 'fsdp'))
- grad_b_qv: float32 [1536], P(('dp', 'fsdp'))
- grad_w_out: float32 [768, 768], P(('dp', 'fsdp'))
- grad_b_out: float32 [768], P(('dp', 'fsdp'))
- grad_ln1_gain: float32 [768], P(('dp', 'fsdp'))
- grad_ln1_bias: float32 [768], P(('dp', 'fsdp'))
- grad_w_up: float32 [768, 3072], P(('dp', 'fsdp'))
- grad_b_up: float32 [3072], P(('dp', 'fsdp'))
- grad_w_down: float32 [3072, 768], P(('dp', 'fsdp'))
- grad_b_down: float32 [768], P(('dp', 'fsdp'))
- grad_ln2_gain: float32 [768], P(('dp', 'fsdp'))
- grad_ln2_bias: float32 [768], P(('dp', 'fsdp'))
- grad_w_pool: float32 [768, 768], P(('dp', 'fsdp'))
- grad_b_pool: float32 [768], P(('dp', 'fsdp'))
- loss: float32 [], replicated
The draws below stay inside these ranges and needn't reach their ends.
Inputs may be any that keep to these rules, and one draw needn't show every extreme that they name: partners[partners[i]] = i and partners[i] != i: the 32 views form 32 / 2 pairs. lengths[partners[i]] = lengths[i]; the longest view has exactly 1024 live tokens.
All inputs are finite; a program needn't handle non-finite values. No bound on the sum of `keep_attn` or of `keep_ffn` on one device may be relied on, other than what follows from the above.
Results may differ from the reference program's by a relative error of at most 0.029.
Values may be sent and summed in bfloat16 or wider, within the bound.
A program may use at most 256 MiB of HBM per device.

```python
import math
import jax
import jax.numpy as jnp
from jax import lax

D = 768
HEADS = 12
HEAD_DIM = 64
FF = 3072
LENGTH = 1024
BATCH = 32


def pairing(key):
    order = jax.random.permutation(jax.random.fold_in(key, 11), BATCH).astype(jnp.int32)
    firsts = order[0::2]
    seconds = order[1::2]
    pair_lengths = jax.random.randint(jax.random.fold_in(key, 12), (BATCH // 2,), 1, LENGTH + 1).astype(jnp.int32)
    pair_lengths = pair_lengths.at[0].set(LENGTH)
    partner_ids = jnp.zeros((BATCH,), jnp.int32)
    partner_ids = partner_ids.at[firsts].set(seconds)
    partner_ids = partner_ids.at[seconds].set(firsts)
    view_lengths = jnp.zeros((BATCH,), jnp.int32)
    view_lengths = view_lengths.at[firsts].set(pair_lengths)
    view_lengths = view_lengths.at[seconds].set(pair_lengths)
    return (partner_ids, view_lengths)


def draw_partners(key, part):
    return pairing(key)[0]


def draw_lengths(key, part):
    return pairing(key)[1]


def plant(array, key, low, top_value):
    extent = array.shape
    index_at = [jax.random.randint(jax.random.fold_in(key, axis), (), 0, extent[axis]) for axis in range(len(extent))]
    array = array.at[tuple(index_at)].set(low)
    longest = extent.index(max(extent))
    index_at[longest] = (index_at[longest] + 1) % extent[longest]
    return array.at[tuple(index_at)].set(top_value)


def levels(stream_key, dims, shards, least, top_value):
    factor_of, own = 1.0, jax.random.fold_in(stream_key, 6)
    for dim, blocks in shards:
        steps = jnp.exp(jax.random.uniform(jax.random.fold_in(own, dim), (blocks,), jnp.float32, least / len(shards), top_value / len(shards)))
        factor_of = factor_of * jnp.repeat(steps, dims[dim] // blocks).reshape([-1 if axis == dim else 1 for axis in range(len(dims))])
    return factor_of


def bell_draw(rng, dims, scale, reach, split=(), kind=jnp.bfloat16):
    entries = scale * jax.random.normal(rng, dims, jnp.float32)
    if split:
        entries = entries * levels(rng, dims, split, -0.22, 0.18)
    return jnp.clip(entries, -reach, reach).astype(kind)


def setup_inputs(seed: int = 0) -> dict:
    keys = jax.random.split(jax.random.key(seed), 21)
    tokens = bell_draw(keys[0], (BATCH, LENGTH, D), 1.0, 6.0, ((0, 32),))
    lengths = draw_lengths(jax.random.fold_in(keys[20], 71), 0)
    keep_attn = plant((jax.random.randint(keys[2], (BATCH, LENGTH, D), 0, 10) < 9).astype(jnp.int32), jax.random.fold_in(keys[2], 1), 0, 1)
    keep_ffn = plant((jax.random.randint(keys[3], (BATCH, LENGTH, D), 0, 10) < 9).astype(jnp.int32), jax.random.fold_in(keys[3], 1), 0, 1)
    partners = draw_partners(jax.random.fold_in(keys[20], 71), 0)
    out_cot = bell_draw(keys[5], (BATCH, LENGTH, D), 1.0, 6.0, ((0, 32),))
    w_qkv = bell_draw(keys[6], (D, 3 * D), D ** -0.5, 0.21875, ((0, 32),))
    b_qv = bell_draw(keys[7], (2 * D,), 0.5, 3.0, ((0, 32),))
    w_out = bell_draw(keys[8], (D, D), (max(1, 2 * D // LENGTH)) ** -0.5, 6.0, ((0, 32),))
    b_out = bell_draw(keys[9], (D,), 0.5, 3.0, ((0, 32),))
    ln1_gain = jnp.clip(1.0 + 0.18 * jax.random.normal(keys[10], (D,), jnp.float32), 0.099609375, 1.8984375).astype(jnp.bfloat16)
    ln1_bias = bell_draw(keys[11], (D,), 0.5, 3.0, ((0, 32),))
    w_up = bell_draw(keys[12], (D, FF), D ** -0.5, 0.21875, ((0, 32),))
    b_up = bell_draw(keys[13], (FF,), 0.5, 3.0, ((0, 32),))
    w_down = bell_draw(keys[14], (FF, D), FF ** -0.5, 0.109375, ((0, 32),))
    b_down = bell_draw(keys[15], (D,), 0.5, 3.0, ((0, 32),))
    ln2_gain = jnp.clip(1.0 + 0.18 * jax.random.normal(keys[16], (D,), jnp.float32), 0.099609375, 1.8984375).astype(jnp.bfloat16)
    ln2_bias = bell_draw(keys[17], (D,), 0.5, 3.0, ((0, 32),))
    w_pool = bell_draw(keys[18], (D, D), D ** -0.5, 0.21875, ((0, 32),))
    b_pool = bell_draw(keys[19], (D,), 0.5, 3.0, ((0, 32),))
    return dict(tokens=tokens, lengths=lengths, keep_attn=keep_attn, keep_ffn=keep_ffn, partners=partners, out_cot=out_cot, w_qkv=w_qkv, b_qv=b_qv, w_out=w_out, b_out=b_out, ln1_gain=ln1_gain, ln1_bias=ln1_bias, w_up=w_up, b_up=b_up, w_down=w_down, b_down=b_down, ln2_gain=ln2_gain, ln2_bias=ln2_bias, w_pool=w_pool, b_pool=b_pool)


@jax.custom_vjp
def low(v):
    return lax.optimization_barrier(v.astype(jnp.bfloat16)).astype(jnp.float32)

@jax.custom_vjp
def low_back(v):
    return v

def low_keep(v):
    return (low(v), None)

def low_pass(kept, grad):
    return (grad,)

def back_keep(v):
    return (v, None)

def back_low(kept, grad):
    return (low(grad),)
low.defvjp(low_keep, low_pass)
low_back.defvjp(back_keep, back_low)
full_accuracy_setting = lax.Precision.HIGHEST
eps_norm = 1e-05
keep_scale = 1.0 / 0.9
logit_divisor = 0.05
neg_fill = -1000000000.0

def layer_norm(values, gain, shift):
    center = values - lax.optimization_barrier(jnp.mean(values, axis=-1, keepdims=True))
    spread = lax.optimization_barrier(jnp.mean(center * center, axis=-1, keepdims=True))
    return center * lax.rsqrt(spread + eps_norm) * gain + shift

def gelu_exact(values):
    return 0.5 * values * (1.0 + lax.erf(values * (1.0 / math.sqrt(2.0))))

def contrast_loss(pooled, partners):
    unit_length_embeddings = pooled * lax.rsqrt(lax.optimization_barrier(jnp.sum(pooled * pooled, axis=1, keepdims=True)) + 1e-06)
    angle_similarity_table = jnp.dot(unit_length_embeddings, unit_length_embeddings.T, precision=full_accuracy_setting) / logit_divisor
    count = pooled.shape[0]
    columns = jnp.arange(count, dtype=jnp.int32)
    others = jnp.where(columns[:, None] == columns[None, :], neg_fill, angle_similarity_table)
    row_max = lax.optimization_barrier(jnp.max(others, axis=1, keepdims=True))
    log_total = row_max[:, 0] + jnp.log(lax.optimization_barrier(jnp.sum(jnp.exp(others - row_max), axis=1)))
    target = lax.optimization_barrier(jnp.sum(jnp.where(partners[:, None] == columns[None, :], angle_similarity_table, 0.0), axis=1))
    return jnp.mean(log_total - target)

def forward_per_group(params, group_tokens, group_keep_attn, group_keep_ffn, group_lengths):
    w_qkv, b_qv, w_out, b_out, ln1_gain, ln1_bias, w_up, b_up, w_down, b_down, ln2_gain, ln2_bias, w_pool, b_pool = params
    group_size = group_tokens.shape[0]
    projected = jnp.einsum('gld,de->gle', group_tokens, w_qkv, precision=full_accuracy_setting)
    query_key_value_bias = jnp.concatenate([b_qv[:D], jnp.zeros((D,), jnp.float32), b_qv[D:]])
    projected = low_back(low(projected + query_key_value_bias))
    shape_four = (group_size, LENGTH, HEADS, HEAD_DIM)
    query_rows = projected[..., :D].reshape(shape_four)
    key_rows = projected[..., D:2 * D].reshape(shape_four)
    value_rows = projected[..., 2 * D:].reshape(shape_four)
    score_scale = 1.0 / math.sqrt(HEAD_DIM)
    raw = jnp.einsum('gqhd,gkhd->ghqk', query_rows, key_rows, precision=full_accuracy_setting) * score_scale
    valid_keys = jnp.arange(LENGTH, dtype=jnp.int32)[None, :] < group_lengths[:, None]
    scores = low_back(jnp.where(valid_keys[:, None, None, :], raw, neg_fill))
    row_max = lax.optimization_barrier(jnp.max(scores, axis=-1, keepdims=True))
    shifted = jnp.exp(scores - row_max)
    probabilities = low(shifted / lax.optimization_barrier(jnp.sum(shifted, axis=-1, keepdims=True)))
    context = jnp.einsum('ghqk,gkhd->gqhd', probabilities, value_rows, precision=full_accuracy_setting)
    context = low_back(low(context.reshape(group_size, LENGTH, D)))
    attended = low_back(jnp.einsum('gld,de->gle', context, w_out, precision=full_accuracy_setting) + b_out)
    first_sum = group_tokens + attended * group_keep_attn
    hidden = layer_norm(first_sum, ln1_gain, ln1_bias)
    up_pre = low_back(jnp.einsum('gld,df->glf', low(hidden), w_up, precision=full_accuracy_setting) + b_up)
    activated = low(gelu_exact(up_pre))
    down_out = low_back(jnp.einsum('glf,fd->gld', activated, w_down, precision=full_accuracy_setting) + b_down)
    second_sum = hidden + down_out * group_keep_ffn
    normed_out = layer_norm(second_sum, ln2_gain, ln2_bias)
    pool_pre = low_back(jnp.dot(low(normed_out[:, 0, :]), w_pool, precision=full_accuracy_setting) + b_pool)
    return (normed_out, jnp.tanh(pool_pre))

def reference(tokens, lengths, keep_attn, keep_ffn, partners, out_cot, w_qkv, b_qv, w_out, b_out, ln1_gain, ln1_bias, w_up, b_up, w_down, b_down, ln2_gain, ln2_bias, w_pool, b_pool):
    params = tuple((weight.astype(jnp.float32) for weight in (w_qkv, b_qv, w_out, b_out, ln1_gain, ln1_bias, w_up, b_up, w_down, b_down, ln2_gain, ln2_bias, w_pool, b_pool)))
    group_size = math.gcd(BATCH, max(1, 4096 // LENGTH))
    group_count = BATCH // group_size
    keep_a = (keep_attn.astype(jnp.float32) * keep_scale).reshape(group_count, group_size, LENGTH, D)
    keep_f = (keep_ffn.astype(jnp.float32) * keep_scale).reshape(group_count, group_size, LENGTH, D)
    group_lengths = lengths.reshape(group_count, group_size)

    def forward(word_embedding_entries, weights):

        def one_group(inputs_one):
            return forward_per_group(weights, inputs_one[0], inputs_one[1], inputs_one[2], inputs_one[3])
        outputs, pooled = lax.map(jax.checkpoint(one_group), (word_embedding_entries.reshape(group_count, group_size, LENGTH, D), keep_a, keep_f, group_lengths))
        return (outputs.reshape(BATCH, LENGTH, D), contrast_loss(pooled.reshape(BATCH, D), partners))
    (layer_out, loss), pullback = jax.vjp(forward, tokens.astype(jnp.float32), params)
    token_grad, grads = pullback((out_cot.astype(jnp.float32), jnp.asarray(BATCH, jnp.float32)))
    return (layer_out.astype(jnp.bfloat16), token_grad.astype(jnp.bfloat16), grads[0], grads[1], grads[2], grads[3], grads[4], grads[5], grads[6], grads[7], grads[8], grads[9], grads[10], grads[11], grads[12], grads[13], loss)
```

```python
import functools
import math

import jax
import jax.numpy as jnp
from jax import lax
from jax.experimental import pallas as pl
from jax.experimental.pallas import tpu as pltpu
from jax.sharding import PartitionSpec as P

HEAD_DIM = 64
LANES = 128
f32, bf16 = jnp.float32, jnp.bfloat16
MESH = pl.DeviceIdType.MESH
AXES = ("dp", "fsdp")
eps_norm = 1e-05
keep_scale = 1.0 / 0.9
logit_divisor = 0.05
neg_fill = -1000000000.0
VMEM_LIMIT = 67043328
DIMS = ("z", "c", "y", "x")
GATHER_ORDERS = (("z", "x", "y", "c"), ("z", "y", "x", "c"))
SCATTER_ORDERS = (("c", "y", "x", "z"), ("c", "x", "y", "z"))
LAG = 2


class Grid:
    def __init__(self, mesh, with_fsdp=True):
        dp, fsdp = mesh.shape["dp"], mesh.shape["fsdp"]
        cores = 2 if dp % 2 == 0 else 1
        side = math.isqrt(fsdp)
        if side * side != fsdp:
            side = fsdp
        self.with_fsdp = with_fsdp
        self.size = {
            "z": dp // cores,
            "c": cores,
            "y": fsdp // side if with_fsdp else 1,
            "x": side if with_fsdp else 1,
        }
        self.shape = tuple(self.size[d] for d in DIMS)
        self.count = math.prod(self.shape)
        self.slots = sum(n - 1 for n in self.shape)

    def me(self):
        dp, fsdp = lax.axis_index("dp"), lax.axis_index("fsdp")
        at = {"z": lax.div(dp, self.size["c"]), "c": lax.rem(dp, self.size["c"])}
        if self.with_fsdp:
            at["y"], at["x"] = lax.div(fsdp, self.size["x"]), lax.rem(fsdp, self.size["x"])
        else:
            at["y"], at["x"] = 0, 0
        return at

    def device(self, at):
        fsdp = at["y"] * self.size["x"] + at["x"] if self.with_fsdp else lax.axis_index("fsdp")
        return (at["z"] * self.size["c"] + at["c"], fsdp)

    def peer(self, at, dim, j):
        other = dict(at)
        other[dim] = lax.rem(at[dim] + j, self.size[dim])
        return other

    def slot(self, dim, j):
        base = 0
        for d in DIMS:
            if d == dim:
                return base + j - 1
            base += self.size[d] - 1

    def order(self, order):
        return tuple(d for d in order if self.size[d] > 1)

    def barrier(self):
        at, sem, count = self.me(), pltpu.get_barrier_semaphore(), 0
        for d in DIMS:
            for j in range(1, self.size[d]):
                pl.semaphore_signal(
                    sem, inc=1, device_id=self.device(self.peer(at, d, j)), device_id_type=MESH
                )
                count += 1
        pl.semaphore_wait(sem, count)


class Gather:
    def __init__(self, grid, pieces, send, recv):
        self.grid, self.send, self.recv, self.at = grid, send, recv, grid.me()
        self.pieces = [(ref, sub, grid.order(order)) for ref, sub, order in pieces]
        self.stages = len(self.pieces[0][2])
        self.steps = len(pieces) + (self.stages - 1) * LAG
        self.now = 0

    def copies(self, i, stage):
        ref, sub, order = self.pieces[i]
        dim, done = order[stage], order[:stage]
        index = tuple(slice(None) if d in done else self.at[d] for d in DIMS)
        view = ref.at[index + sub]
        for j in range(1, self.grid.size[dim]):
            slot = self.grid.slot(dim, j)
            yield pltpu.make_async_remote_copy(
                src_ref=view,
                dst_ref=view,
                send_sem=self.send.at[i, slot],
                recv_sem=self.recv.at[i, slot],
                device_id=self.grid.device(self.grid.peer(self.at, dim, j)),
                device_id_type=MESH,
            )

    def begin(self):
        for i in range(len(self.pieces)):
            for copy in self.copies(i, 0):
                copy.start()

    def run(self, first, last):
        for step in range(first, last):
            for stage in range(self.stages):
                i = step - stage * LAG
                if 0 <= i < len(self.pieces):
                    for copy in self.copies(i, stage):
                        copy.wait_recv()
                    if stage < self.stages - 1:
                        for copy in self.copies(i, stage + 1):
                            copy.start()

    def until(self, i):
        last = max(self.now, min(self.steps, i + 1 + (self.stages - 1) * LAG))
        self.run(self.now, last)
        self.now = last

    def finish(self):
        self.run(self.now, self.steps)
        for i in range(len(self.pieces)):
            for stage in range(self.stages):
                for copy in self.copies(i, stage):
                    copy.wait_send()


class Scatter:
    def __init__(self, grid, pieces, send, recv):
        self.grid, self.send, self.recv, self.at = grid, send, recv, grid.me()
        self.pieces = [(src, sub, grid.order(order), bufs, out) for src, sub, order, bufs, out in pieces]
        self.stages = len(self.pieces[0][2])
        self.steps = len(pieces) + (self.stages - 1) * LAG

    def pick(self, i, stage, where):
        src, sub, order, bufs, _ = self.pieces[i]
        left = tuple(d for d in DIMS if d not in order[:stage])
        index = tuple(where if d == order[stage] else slice(None) for d in left)
        if stage == 0:
            return src.at[index + sub]
        return bufs[stage - 1].at[(0,) + index]

    def copies(self, i, stage):
        _, _, order, bufs, _ = self.pieces[i]
        dim = order[stage]
        for j in range(1, self.grid.size[dim]):
            other = self.grid.peer(self.at, dim, j)
            slot = self.grid.slot(dim, j)
            yield pltpu.make_async_remote_copy(
                src_ref=self.pick(i, stage, other[dim]),
                dst_ref=bufs[stage].at[j - 1],
                send_sem=self.send.at[i, slot],
                recv_sem=self.recv.at[i, slot],
                device_id=self.grid.device(other),
                device_id_type=MESH,
            )

    def begin(self, i):
        for copy in self.copies(i, 0):
            copy.start()

    def run(self, first, last):
        for step in range(first, last):
            for stage in range(self.stages):
                i = step - stage * LAG
                if 0 <= i < len(self.pieces):
                    self.add(i, stage)
                    if stage < self.stages - 1:
                        for copy in self.copies(i, stage + 1):
                            copy.start()

    def add(self, i, stage):
        _, _, order, bufs, out = self.pieces[i]
        for copy in self.copies(i, stage):
            copy.wait_recv()
        buf = bufs[stage]
        total = self.pick(i, stage, self.at[order[stage]])[...].astype(f32)
        for j in range(self.grid.size[order[stage]] - 1):
            total = total + buf[j].astype(f32)
        if stage == self.stages - 1:
            out[...] = total.reshape(out.shape)
        else:
            buf[0] = total.astype(buf.dtype)

    def finish(self):
        for i in range(len(self.pieces)):
            for stage in range(self.stages):
                for copy in self.copies(i, stage):
                    copy.wait_send()


def scatter_buffers(grid, order, rows, columns, dtype):
    shapes, left = [], list(DIMS)
    for d in grid.order(order):
        left.remove(d)
        shapes.append((grid.size[d] - 1,) + tuple(grid.size[e] for e in left) + (rows, columns))
    return [pltpu.VMEM(s, dtype) for s in shapes]


def cuts(total, parts, unit):
    while parts > 1 and total % (parts * unit):
        parts -= 1
    return [(j * (total // parts), total // parts) for j in range(parts)]


def dotg(a, b, ca, cb, precision=None):
    return lax.dot_general(
        a, b, (((ca,), (cb,)), ((), ())), preferred_element_type=f32, precision=precision
    )


def iota(shape, dim):
    return lax.broadcasted_iota(jnp.int32, shape, dim)


def three_parts(x):
    high = x.astype(bf16).astype(f32)
    mid = (x - high).astype(bf16).astype(f32)
    return high, mid, x - high - mid


def spread_vector(rows, n):
    shards, width = rows.shape
    total = shards * n
    place = (iota((width, total), 1) % n == iota((width, total), 0)).astype(f32).astype(bf16)
    wide = dotg(rows, place, 1, 0)
    keep = iota((shards, total), 1) // n == iota((shards, total), 0)
    return jnp.sum(jnp.where(keep, wide, 0.0), axis=0, keepdims=True)


def fold_vector(vector, shards, n, width):
    total = shards * n
    keep = iota((shards, total), 1) // n == iota((shards, total), 0)
    place = (iota((total, width), 0) % n == iota((total, width), 1)).astype(f32)
    return dotg(jnp.where(keep, vector, 0.0), place, 1, 0, lax.Precision.HIGHEST)


def attend(qkv_ref, context_ref, lse_ref, live, pair, block, tick):
    length, width = qkv_ref.shape[0], context_ref.shape[1]

    def col(part):
        return pl.ds(pl.multiple_of(part * width + pair * LANES, LANES), LANES)

    k = qkv_ref[:, col(1)].astype(f32) * (1.0 / math.sqrt(HEAD_DIM))
    v = qkv_ref[:, col(2)].astype(f32)
    lane, row = iota((length, LANES), 1), iota((length, LANES), 0)
    bias = jnp.where(row < live, 0.0, neg_fill)
    keys, values = [], []
    for h in range(2):
        mine, spare = lane // HEAD_DIM == h, HEAD_DIM * (1 - h)
        keys.append(jnp.where(mine, k, jnp.where(lane == spare, bias, 0.0)).astype(bf16))
        values.append(jnp.where(mine, v, 1.0).astype(bf16))
    lane = iota((block, LANES), 1)
    low = lane < HEAD_DIM
    for i in range(length // block):
        rows = slice(i * block, (i + 1) * block)
        q = qkv_ref[rows, col(0)].astype(f32)
        sums, tops = [], []
        for h in range(2):
            spare = HEAD_DIM * (1 - h)
            qh = jnp.where(lane // HEAD_DIM == h, q, jnp.where(lane == spare, 1.0, 0.0))
            scores = dotg(qh.astype(bf16), keys[h], 1, 1)
            top = jnp.max(scores, axis=1, keepdims=True)
            weights = jnp.exp(scores - top).astype(bf16)
            sums.append(dotg(weights, values[h], 1, 0))
            tops.append(top)
        num = jnp.where(low, sums[0], sums[1])
        den = pltpu.roll(jnp.where(low, sums[1], sums[0]), HEAD_DIM, 1)
        out = pl.ds(pl.multiple_of(pair * LANES, LANES), LANES)
        context_ref[rows, out] = (num / den).astype(bf16)
        lse_ref[rows, out] = jnp.where(low, tops[0], tops[1]) + jnp.log(den)
        tick(i)


def gather_plan(grid, shapes):
    plan = [("s", ())]
    every = slice(None)
    for name, parts in (("q", 6), ("o", 2), ("u", 6), ("d", 6), ("p", 2)):
        rows, columns = shapes[name]
        if name == "d":
            plan += [(name, (pl.ds(a, n), every)) for a, n in cuts(rows, parts, 8)]
        else:
            plan += [(name, (every, pl.ds(a, n))) for a, n in cuts(columns, parts, LANES)]
    return [(name, sub, GATHER_ORDERS[i % 2]) for i, (name, sub) in enumerate(plan)]


def forward_kernel(grid, plan, sizes, len_ref, tokens_ref, wq, wo, wu, wd, wp, *refs):
    count = len(sizes)
    small_in, refs = refs[:count], refs[count:]
    (gq, go, gu, gd, gp, qkv_ref, context_ref, lse_ref), refs = refs[:8], refs[8:]
    small_out, (gs, send, recv, own_sem) = refs[:count], refs[count:]
    at = grid.me()
    own = tuple(at[d] for d in DIMS)
    to_own = []
    for i, (src, dst) in enumerate(((wq, gq), (wo, go), (wu, gu), (wd, gd), (wp, gp))):
        to_own.append(pltpu.make_async_copy(src, dst.at[own], own_sem.at[i]))
        to_own[-1].start()
    mine = gs.at[own]
    mine[...] = jnp.zeros(mine.shape, bf16)
    for i, (ref, n) in enumerate(zip(small_in, sizes)):
        mine[i : i + 1, 0:n] = ref[...]
    where = dict(q=gq, o=go, u=gu, d=gd, p=gp, s=gs)
    gather = Gather(grid, [(where[name], sub, order) for name, sub, order in plan], send, recv)
    grid.barrier()
    for copy in to_own:
        copy.wait()
    gather.begin()
    gather.until(0)
    rows = gs[...].reshape((grid.count,) + gs.shape[-2:])
    for i, (ref, n) in enumerate(zip(small_out, sizes)):
        ref[...] = spread_vector(rows[:, i, :], n)
    width = context_ref.shape[1]
    tokens = tokens_ref[...]
    for i, (name, sub, _) in enumerate(plan):
        if name != "q":
            continue
        gather.until(i)
        lo, n = sub[1].start, sub[1].size

        def project(weight, sem):
            copy = pltpu.make_async_copy(gq.at[:, :, :, :, :, pl.ds(lo, n)], weight, sem)
            copy.start()
            copy.wait()
            out = dotg(tokens, weight[...].reshape(-1, n), 1, 0)
            if lo < width:
                out = out + small_out[0][:, lo : lo + n]
            elif lo >= 2 * width:
                out = out + small_out[0][:, lo - width : lo - width + n]
            qkv_ref[:, lo : lo + n] = out.astype(bf16)

        pl.run_scoped(project, pltpu.VMEM(gq.shape[:-1] + (n,), bf16), pltpu.SemaphoreType.DMA)
    pairs, block = width // LANES, min(512, qkv_ref.shape[0])
    blocks = qkv_ref.shape[0] // block
    first, todo, slots = gather.now, gather.steps - gather.now, pairs * blocks
    live = len_ref[0]

    def one_pair(pair, _):
        def tick(i):
            for p in range(pairs):
                t = p * blocks + i

                @pl.when(pair == p)
                def _():
                    gather.run(first + t * todo // slots, first + (t + 1) * todo // slots)

        attend(qkv_ref, context_ref, lse_ref, live, pair, block, tick)
        return 0

    lax.fori_loop(0, pairs, one_pair, 0)
    gather.now = gather.steps
    gather.finish()


def run_forward(grid, length_of, tokens, big, small):
    length, width = tokens.shape
    names = ("q", "o", "u", "d", "p")
    shapes = {k: w.shape for k, w in zip(names, big)}
    sizes = [v.shape[0] for v in small]
    plan = gather_plan(grid, shapes)
    pad = -(-max(sizes) // LANES) * LANES
    vmem, anywhere = pl.BlockSpec(memory_space=pltpu.VMEM), pl.BlockSpec(memory_space=pl.ANY)
    outs = pl.pallas_call(
        functools.partial(forward_kernel, grid, plan, sizes),
        out_shape=[jax.ShapeDtypeStruct(grid.shape + shapes[k], bf16) for k in names]
        + [
            jax.ShapeDtypeStruct((length, 3 * width), bf16),
            jax.ShapeDtypeStruct((length, width), bf16),
            jax.ShapeDtypeStruct((length, width), f32),
        ]
        + [jax.ShapeDtypeStruct((1, grid.count * n), f32) for n in sizes],
        in_specs=[pl.BlockSpec(memory_space=pltpu.SMEM)] + [vmem] * (6 + len(small)),
        out_specs=[anywhere] * 5 + [vmem] * (3 + len(small)),
        scratch_shapes=[
            pltpu.VMEM(grid.shape + (16, pad), bf16),
            pltpu.SemaphoreType.DMA((len(plan), grid.slots)),
            pltpu.SemaphoreType.DMA((len(plan), grid.slots)),
            pltpu.SemaphoreType.DMA((5,)),
        ],
        compiler_params=pltpu.CompilerParams(
            collective_id=0, has_side_effects=True, vmem_limit_bytes=VMEM_LIMIT
        ),
        name="gather_and_attend",
    )(length_of, tokens, *big, *[v.reshape(1, -1) for v in small])
    gathered = [g.reshape(-1, g.shape[-1]) for g in outs[:5]]
    return gathered, outs[5], outs[6], outs[7], outs[8:]


def exchange_kernel(grid, row_ref, all_ref, send, recv):
    at = grid.me()
    all_ref[tuple(at[d] for d in DIMS)] = row_ref[...]
    gather = Gather(grid, [(all_ref, (), GATHER_ORDERS[0])], send, recv)
    grid.barrier()
    gather.begin()
    gather.finish()


def exchange(grid, rows):
    vmem = pl.BlockSpec(memory_space=pltpu.VMEM)
    out = pl.pallas_call(
        functools.partial(exchange_kernel, grid),
        out_shape=jax.ShapeDtypeStruct(grid.shape + rows.shape, rows.dtype),
        in_specs=[vmem],
        out_specs=vmem,
        scratch_shapes=[pltpu.SemaphoreType.DMA((1, grid.slots))] * 2,
        compiler_params=pltpu.CompilerParams(collective_id=1, has_side_effects=True),
        name="exchange",
    )(rows)
    return out.reshape((-1,) + rows.shape)


def attend_back(qkv_ref, context, dcontext, lse, live, pair, block, prep, acc, tick):
    length, width = qkv_ref.shape[0], context.shape[1]
    scale = 1.0 / math.sqrt(HEAD_DIM)
    one = pl.ds(pl.multiple_of(pair * LANES, LANES), LANES)

    def col(part):
        return pl.ds(pl.multiple_of(part * width + pair * LANES, LANES), LANES)

    q, k, v = (qkv_ref[:, col(j)].astype(f32) for j in range(3))
    d = dcontext[:, one].astype(f32)
    lane, row = iota((length, LANES), 1), iota((length, LANES), 0)
    bias = jnp.where(row < live, 0.0, neg_fill)
    both = d * context[:, one].astype(f32)
    total = lse[:, one]
    other = pltpu.roll(total, HEAD_DIM, 1)
    for h in range(2):
        mine, a = lane // HEAD_DIM == h, HEAD_DIM * (1 - h)
        inner = jnp.sum(jnp.where(mine, both, 0.0), axis=1, keepdims=True)
        l0, l1, l2 = three_parts(-other)
        d0, d1, d2 = three_parts(-inner)

        def lanes(base, *extra):
            out = 0.0
            for j, e in reversed(list(enumerate(extra))):
                out = jnp.where(lane == a + j, e, out)
            return jnp.where(mine, base, out).astype(bf16)

        prep[h, 0] = lanes(q * scale, 1.0, l0, l1, l2)
        prep[h, 1] = lanes(k, bias, 1.0, 1.0, 1.0)
        prep[h, 2] = lanes(d, d0, d1, d2)
        prep[h, 3] = lanes(v, 1.0, 1.0, 1.0)
        prep[h, 4] = lanes(q * scale)
        prep[h, 5] = lanes(d)
        prep[h, 6] = lanes(k * scale)
    q_t = (q * scale).T.astype(bf16)
    d_t = d.T.astype(bf16)
    acc[...] = jnp.zeros_like(acc)
    for i in range(length // block):
        rows = slice(i * block, (i + 1) * block)
        dq = jnp.zeros((block, LANES), f32)
        for h in range(2):
            head = slice(h * HEAD_DIM, (h + 1) * HEAD_DIM)
            p = jnp.exp(dotg(prep[h, 0, rows, :], prep[h, 1], 1, 1))
            dp = dotg(prep[h, 2, rows, :], prep[h, 3], 1, 1)
            ds = (p * dp).astype(bf16)
            acc[0, head, :] += dotg(d_t[head, rows], p.astype(bf16), 1, 0)
            acc[1, head, :] += dotg(q_t[head, rows], ds, 1, 0)
            dq = dq + dotg(ds, prep[h, 6], 1, 0)
        qkv_ref[rows, col(0)] = dq.astype(bf16)
        tick(i)
    qkv_ref[:, col(1)] = acc[1].T.astype(bf16)
    qkv_ref[:, col(2)] = acc[0].T.astype(bf16)


def scatter_plan(grid, shapes):
    plan, every = [], slice(None)
    for name, parts in (("d", 6), ("u", 6), ("o", 2), ("q", 9)):
        rows, columns = shapes[name]
        if name == "d":
            plan += [(name, (pl.ds(a, n), every), n, columns) for a, n in cuts(rows, parts, 8)]
        else:
            plan += [(name, (every, pl.ds(a, n)), rows, n) for a, n in cuts(columns, parts, LANES)]
    plan.append(("s", (), 16, shapes["s"]))
    return [(p[0], p[1], SCATTER_ORDERS[i % 2]) + p[2:] for i, p in enumerate(plan)]


def backward_kernel(grid, plan, sizes, len_ref, qkv_hbm, context, dcontext, lse, tokens, first_grad, wq, dd, du, do, *refs):
    count = len(sizes)
    small_in, refs = refs[: count - 1], refs[count - 1 :]
    (rq, ro, ru, rd, rs, tokens_grad), refs = refs[:6], refs[6:]
    (qkv_ref, dq, dsmall, prep, acc, send, recv, sem), bufs = refs[:8], list(refs[8:])
    load = pltpu.make_async_copy(qkv_hbm, qkv_ref, sem)
    load.start()
    sources, results = dict(d=dd, u=du, o=do, q=dq, s=dsmall), dict(d=rd, u=ru, o=ro, q=rq, s=rs)
    pieces = []
    for name, sub, order, _, _ in plan:
        n = len(grid.order(order))
        pieces.append((sources[name], sub, order, bufs[:n], results[name].at[sub] if sub else results[name]))
        bufs = bufs[n:]
    scatter = Scatter(grid, pieces, send, recv)
    names = [p[0] for p in plan]
    ready = names.index("q")
    grid.barrier()
    for i in range(ready):
        scatter.begin(i)
    load.wait()
    length, width = context.shape
    pairs, block = width // LANES, min(256, length)
    blocks = length // block
    slots, live = pairs * blocks, len_ref[0]

    def one_pair(pair, _):
        def tick(i):
            for p in range(pairs):
                t = p * blocks + i

                @pl.when(pair == p)
                def _():
                    scatter.run(t * ready // slots, (t + 1) * ready // slots)

        attend_back(qkv_ref, context, dcontext, lse, live, pair, block, prep, acc, tick)
        return 0

    lax.fori_loop(0, pairs, one_pair, 0)
    step = ready
    for i in range(ready, len(plan) - 1):
        sub = plan[i][1]
        part = dotg(tokens[...], qkv_ref[:, sub[1].start : sub[1].start + sub[1].size], 0, 0)
        dq[:, :, :, :, :, sub[1]] = part.astype(bf16).reshape(grid.shape + (-1, sub[1].size))
        scatter.begin(i)
        if i - 2 >= ready:
            scatter.run(step, step + 1)
            step += 1
    sums = dotg(jnp.ones((8, length), bf16), qkv_ref[...], 1, 0)[0:1]
    vectors = [jnp.concatenate([sums[:, :width], sums[:, 2 * width :]], axis=1)] + [r[...] for r in small_in]
    pad = dsmall.shape[-1]
    dsmall[...] = jnp.zeros_like(dsmall)
    for j, (v, n) in enumerate(zip(vectors, sizes)):
        dsmall[:, :, :, :, j, :] = fold_vector(v, grid.count, n, pad).reshape(grid.shape + (pad,))
    scatter.begin(len(plan) - 1)
    rest = scatter.steps - step
    parts = 4
    rows = length // parts
    for i in range(parts):
        scatter.run(step + i * rest // parts, step + (i + 1) * rest // parts)
        here = slice(i * rows, (i + 1) * rows)
        grad = first_grad[here, :] + dotg(qkv_ref[here, :], wq[...], 1, 1)
        tokens_grad[here, :] = grad.astype(bf16)
    scatter.finish()


def run_backward(grid, length_of, qkv, context, dcontext, lse, tokens, first_grad, wq, big, small, sizes):
    length, width = tokens.shape
    dd, du, do = big
    rows = {k: w.shape[0] // grid.count for k, w in (("d", dd), ("u", du), ("o", do), ("q", wq))}
    columns = {k: w.shape[1] for k, w in (("d", dd), ("u", du), ("o", do), ("q", wq))}
    pad = -(-max(sizes) // LANES) * LANES
    shapes = {k: (rows[k], columns[k]) for k in rows}
    shapes["s"] = pad
    plan = scatter_plan(grid, shapes)
    bufs = []
    for name, _, order, r, c in plan:
        bufs += scatter_buffers(grid, order, r, c, f32 if name == "s" else bf16)
    vmem, anywhere = pl.BlockSpec(memory_space=pltpu.VMEM), pl.BlockSpec(memory_space=pl.ANY)
    return pl.pallas_call(
        functools.partial(backward_kernel, grid, plan, sizes),
        out_shape=[jax.ShapeDtypeStruct(shapes[k], f32) for k in ("q", "o", "u", "d")]
        + [jax.ShapeDtypeStruct((16, pad), f32), jax.ShapeDtypeStruct((length, width), bf16)],
        in_specs=[pl.BlockSpec(memory_space=pltpu.SMEM), anywhere] + [vmem] * (9 + len(small)),
        out_specs=[vmem] * 6,
        scratch_shapes=[
            pltpu.VMEM(qkv.shape, bf16),
            pltpu.VMEM(grid.shape + shapes["q"], bf16),
            pltpu.VMEM(grid.shape + (16, pad), f32),
            pltpu.VMEM((2, 7, length, LANES), bf16),
            pltpu.VMEM((2, LANES, length), f32),
            pltpu.SemaphoreType.DMA((len(plan), grid.slots)),
            pltpu.SemaphoreType.DMA((len(plan), grid.slots)),
            pltpu.SemaphoreType.DMA,
        ]
        + bufs,
        compiler_params=pltpu.CompilerParams(
            collective_id=2, has_side_effects=True, vmem_limit_bytes=VMEM_LIMIT
        ),
        name="attend_back_and_scatter",
    )(
        length_of,
        qkv,
        context,
        dcontext,
        lse,
        tokens,
        first_grad,
        wq,
        *[w.reshape(grid.shape + (-1, w.shape[1])) for w in (dd, du, do)],
        *[v.reshape(1, -1) for v in small],
    )


def layer_norm(values, gain, shift):
    center = values - jnp.mean(values, axis=-1, keepdims=True)
    spread = jnp.mean(center * center, axis=-1, keepdims=True)
    return center * lax.rsqrt(spread + eps_norm) * gain + shift


def gelu_exact(values):
    return 0.5 * values * (1.0 + lax.erf(values * (1.0 / math.sqrt(2.0))))


def contrast_loss(pooled, partners):
    unit = pooled * lax.rsqrt(jnp.sum(pooled * pooled, axis=1, keepdims=True) + 1e-06)
    sims = jnp.dot(unit, unit.T, precision=lax.Precision.HIGHEST) / logit_divisor
    columns = jnp.arange(pooled.shape[0], dtype=jnp.int32)
    others = jnp.where(columns[:, None] == columns[None, :], neg_fill, sims)
    row_max = jnp.max(others, axis=1, keepdims=True)
    log_total = row_max[:, 0] + jnp.log(jnp.sum(jnp.exp(others - row_max), axis=1))
    target = jnp.sum(jnp.where(partners[:, None] == columns[None, :], sims, 0.0), axis=1)
    return jnp.mean(log_total - target)


def dot(a, b):
    return jnp.dot(a, b, preferred_element_type=f32)


def on_device(whole, grid, tokens, lengths, keep_attn, keep_ffn, partners, out_cot, *weights):
    (w_qkv, b_qv, w_out, b_out, ln1_gain, ln1_bias, w_up, b_up, w_down, b_down, ln2_gain, ln2_bias, w_pool, b_pool) = weights
    _, length, width = tokens.shape
    big = [w_qkv, w_out, w_up, w_down, w_pool]
    small = [b_qv, b_out, ln1_gain, ln1_bias, b_up, b_down, ln2_gain, ln2_bias, b_pool]
    shard_rows = w_qkv.shape[0]
    if not grid.with_fsdp:
        big = [lax.all_gather(w, "fsdp", axis=0, tiled=True) for w in big]
        small = [lax.all_gather(v, "fsdp", axis=0, tiled=True) for v in small]
    sizes = [v.shape[0] for v in small]
    rows = tokens.reshape(length, width)
    gathered, qkv, context, lse, vectors = run_forward(grid, lengths, rows, big, small)
    wq, wo, wu, wd, wp = gathered
    v_bout, v_g1, v_b1, v_bup, v_bdown, v_g2, v_b2, v_bpool = vectors[1:]
    keep_a = keep_attn.reshape(length, width).astype(f32) * keep_scale
    keep_f = keep_ffn.reshape(length, width).astype(f32) * keep_scale
    attended = dot(context, wo) + v_bout
    first_sum = rows.astype(f32) + attended * keep_a
    hidden = layer_norm(first_sum, v_g1, v_b1)
    hidden_low = hidden.astype(bf16)
    up_pre = dot(hidden_low, wu) + v_bup
    activated = gelu_exact(up_pre).astype(bf16)
    second_sum = hidden + (dot(activated, wd) + v_bdown) * keep_f
    normed = layer_norm(second_sum, v_g2, v_b2)
    layer_out = normed.astype(bf16)
    cls = normed[0:1].astype(bf16)
    pooled = jnp.tanh(dot(cls, wp) + v_bpool)
    pack = jnp.concatenate([pooled, cls.astype(f32), jnp.zeros((6, width), f32)], axis=0)
    everyone = exchange(whole, pack)
    pooled_all, cls_all = everyone[:, 0, :], everyone[:, 1, :].astype(bf16)
    views = pooled_all.shape[0]
    loss, loss_pull = jax.vjp(functools.partial(contrast_loss, partners=partners), pooled_all)
    (pooled_grad,) = loss_pull(jnp.asarray(views, f32))
    pre_all = (pooled_grad * (1.0 - pooled_all * pooled_all)).astype(bf16)
    here = lax.axis_index(AXES)
    pre_grad = lax.dynamic_slice_in_dim(pre_all, here, 1, 0)
    cls_mine = lax.dynamic_slice_in_dim(cls_all, here * shard_rows, shard_rows, 1)
    pool_weight_grad = lax.dot_general(cls_mine, pre_all, (((0,), (0,)), ((), ())), preferred_element_type=f32)
    pool_bias_all = jnp.sum(pre_all.astype(f32), axis=0)
    pool_bias_grad = lax.dynamic_slice_in_dim(pool_bias_all, here * shard_rows, shard_rows, 0)
    cls_grad = lax.dot_general(pre_grad, wp, (((1,), (1,)), ((), ())), preferred_element_type=f32)
    first_row = jnp.arange(length, dtype=jnp.int32)[:, None] == 0
    out_grad = out_cot.reshape(length, width).astype(f32) + jnp.where(first_row, cls_grad, 0.0)
    _, norm_pull = jax.vjp(layer_norm, second_sum, v_g2, v_b2)
    second_grad, g2_grad, b2_grad = norm_pull(out_grad)
    down_grad = (second_grad * keep_f).astype(bf16)
    down_weight_grad = dot(activated.T, down_grad).astype(bf16)
    _, gelu_pull = jax.vjp(gelu_exact, up_pre)
    (up_grad,) = gelu_pull(lax.dot_general(down_grad, wd, (((1,), (1,)), ((), ())), preferred_element_type=f32))
    up_grad = up_grad.astype(bf16)
    up_weight_grad = dot(hidden_low.T, up_grad).astype(bf16)
    hidden_grad = second_grad + lax.dot_general(up_grad, wu, (((1,), (1,)), ((), ())), preferred_element_type=f32)
    _, first_pull = jax.vjp(layer_norm, first_sum, v_g1, v_b1)
    first_grad, g1_grad, b1_grad = first_pull(hidden_grad)
    attended_grad = (first_grad * keep_a).astype(bf16)
    out_weight_grad = dot(context.T, attended_grad).astype(bf16)
    context_grad = lax.dot_general(attended_grad, wo, (((1,), (1,)), ((), ())), preferred_element_type=f32).astype(bf16)

    def column_sum(x):
        return jnp.sum(x.astype(f32), axis=0)

    vector_grads = [column_sum(attended_grad), g1_grad, b1_grad, column_sum(up_grad), column_sum(down_grad), g2_grad, b2_grad]
    rq, ro, ru, rd, rs, tokens_grad = run_backward(
        grid, lengths, qkv, context, context_grad, lse, rows, first_grad, wq,
        [down_weight_grad, up_weight_grad, out_weight_grad], vector_grads, sizes[:-1],
    )
    owned = [rq, ro, ru, rd] + [rs[j, :n] for j, n in enumerate(sizes[:-1])]
    if not grid.with_fsdp:
        owned = [lax.psum_scatter(g, "fsdp", scatter_dimension=0, tiled=True) for g in owned]
    rq, ro, ru, rd, s_qv, s_out, s_g1, s_b1, s_up, s_down, s_g2, s_b2 = owned
    return (
        layer_out.reshape(tokens.shape), tokens_grad.reshape(tokens.shape), rq, s_qv, ro, s_out, s_g1, s_b1, ru, s_up,
        rd, s_down, s_g2, s_b2, pool_weight_grad, pool_bias_grad, loss,
    )


def solution(mesh):
    rows, vector, matrix = P(AXES, None, None), P(AXES), P(AXES, None)
    weights = (matrix, vector, matrix, vector, vector, vector, matrix, vector, matrix, vector, vector, vector, matrix, vector)
    devices = mesh.shape["dp"] * mesh.shape["fsdp"]

    def step(*args):
        whole = Grid(mesh)
        grid = whole if (args[6].shape[0] // devices) % 8 == 0 else Grid(mesh, False)
        return jax.shard_map(
            functools.partial(on_device, whole, grid),
            mesh=mesh,
            in_specs=(rows, vector, rows, rows, P(), rows) + weights,
            out_specs=(rows, rows) + weights + (P(),),
            check_vma=False,
        )(*args)

    return step
```

```python
import functools
import math

import jax
import jax.numpy as jnp
from jax import lax
from jax.experimental import pallas as pl
from jax.experimental.pallas import tpu as pltpu
from jax.sharding import PartitionSpec as P

HEAD_DIM = 64
LANES = 128
f32, bf16 = jnp.float32, jnp.bfloat16
MESH = pl.DeviceIdType.MESH
AXES = ("dp", "fsdp")
eps_norm = 1e-05
keep_scale = 1.0 / 0.9
logit_divisor = 0.05
neg_fill = -1000000000.0
VMEM_LIMIT = 67043328
DIMS = ("z", "c", "y", "x")
GATHER_ORDERS = (
    ("z", "x", "y", "c"),
    ("x", "z", "y", "c"),
    ("z", "y", "x", "c"),
    ("z", "y", "x", "c"),
    ("y", "z", "x", "c"),
    ("z", "x", "y", "c"),
)
SCATTER_ORDERS = (("c", "y", "x", "z"), ("c", "x", "y", "z"))
LAG = 2


class Grid:
    def __init__(self, mesh, with_fsdp=True):
        dp, fsdp = mesh.shape["dp"], mesh.shape["fsdp"]
        cores = 2 if dp % 2 == 0 else 1
        side = math.isqrt(fsdp)
        if side * side != fsdp:
            side = fsdp
        self.with_fsdp = with_fsdp
        self.size = {
            "z": dp // cores,
            "c": cores,
            "y": fsdp // side if with_fsdp else 1,
            "x": side if with_fsdp else 1,
        }
        self.shape = tuple(self.size[d] for d in DIMS)
        self.count = math.prod(self.shape)
        self.slots = sum(n - 1 for n in self.shape)

    def me(self):
        dp, fsdp = lax.axis_index("dp"), lax.axis_index("fsdp")
        at = {"z": lax.div(dp, self.size["c"]), "c": lax.rem(dp, self.size["c"])}
        if self.with_fsdp:
            at["y"], at["x"] = lax.div(fsdp, self.size["x"]), lax.rem(fsdp, self.size["x"])
        else:
            at["y"], at["x"] = 0, 0
        return at

    def device(self, at):
        fsdp = at["y"] * self.size["x"] + at["x"] if self.with_fsdp else lax.axis_index("fsdp")
        return (at["z"] * self.size["c"] + at["c"], fsdp)

    def peer(self, at, dim, j):
        other = dict(at)
        other[dim] = lax.rem(at[dim] + j, self.size[dim])
        return other

    def slot(self, dim, j):
        base = 0
        for d in DIMS:
            if d == dim:
                return base + j - 1
            base += self.size[d] - 1

    def order(self, order):
        return tuple(d for d in order if self.size[d] > 1)

    def barrier(self):
        at, sem, count = self.me(), pltpu.get_barrier_semaphore(), 0
        for d in DIMS:
            for j in range(1, self.size[d]):
                pl.semaphore_signal(
                    sem, inc=1, device_id=self.device(self.peer(at, d, j)), device_id_type=MESH
                )
                count += 1
        pl.semaphore_wait(sem, count)


class Gather:
    def __init__(self, grid, pieces, send, recv, window=4, lag=3):
        self.grid, self.send, self.recv, self.at = grid, send, recv, grid.me()
        self.pieces = [(ref, sub, grid.order(order)) for ref, sub, order in pieces]
        self.stages, self.window, self.now = len(self.pieces[0][2]), window, 0
        self.events = [
            (step - stage * lag, stage)
            for step in range(len(pieces) + (self.stages - 1) * lag)
            for stage in range(self.stages)
            if 0 <= step - stage * lag < len(pieces)
        ]
        self.whole = [self.events.index((i, self.stages - 1)) + 1 for i in range(len(pieces))]

    def copies(self, i, stage):
        ref, sub, order = self.pieces[i]
        dim, done = order[stage], order[:stage]
        index = tuple(slice(None) if d in done else self.at[d] for d in DIMS)
        view = ref.at[index + sub]
        for j in range(1, self.grid.size[dim]):
            slot = self.grid.slot(dim, j)
            yield pltpu.make_async_remote_copy(
                src_ref=view,
                dst_ref=view,
                send_sem=self.send.at[i, slot],
                recv_sem=self.recv.at[i, slot],
                device_id=self.grid.device(self.grid.peer(self.at, dim, j)),
                device_id_type=MESH,
            )

    def start(self, i, stage):
        for copy in self.copies(i, stage):
            copy.start()

    def begin(self):
        for i in range(min(self.window, len(self.pieces))):
            self.start(i, 0)

    def run(self, first, last):
        for i, stage in self.events[first:last]:
            for copy in self.copies(i, stage):
                copy.wait_recv()
            if stage == 0 and i + self.window < len(self.pieces):
                self.start(i + self.window, 0)
            if stage < self.stages - 1:
                self.start(i, stage + 1)

    def until(self, last):
        self.run(self.now, max(self.now, last))
        self.now = max(self.now, last)

    def finish(self):
        self.until(len(self.events))
        for i in range(len(self.pieces)):
            for stage in range(self.stages):
                for copy in self.copies(i, stage):
                    copy.wait_send()

    def loop(self, count, marks, body):
        marks = [max(self.now, m) for m in marks]
        starts = [self.now] + marks[:-1]

        def step(t, _):
            for k in range(count):
                if marks[k] > starts[k]:

                    @pl.when(t == k)
                    def _():
                        self.run(starts[k], marks[k])

            body(t)
            return 0

        lax.fori_loop(0, count, step, 0)
        self.now = marks[-1]


class Scatter:
    def __init__(self, grid, pieces, send, recv):
        self.grid, self.send, self.recv, self.at = grid, send, recv, grid.me()
        self.pieces = [(src, sub, grid.order(order), bufs, out) for src, sub, order, bufs, out in pieces]
        self.stages = len(self.pieces[0][2])
        self.steps = len(pieces) + (self.stages - 1) * LAG

    def pick(self, i, stage, where):
        src, sub, order, bufs, _ = self.pieces[i]
        left = tuple(d for d in DIMS if d not in order[:stage])
        index = tuple(where if d == order[stage] else slice(None) for d in left)
        if stage == 0:
            return src.at[index + sub]
        return bufs[stage - 1].at[(0,) + index]

    def copies(self, i, stage):
        _, _, order, bufs, _ = self.pieces[i]
        dim = order[stage]
        for j in range(1, self.grid.size[dim]):
            other = self.grid.peer(self.at, dim, j)
            slot = self.grid.slot(dim, j)
            yield pltpu.make_async_remote_copy(
                src_ref=self.pick(i, stage, other[dim]),
                dst_ref=bufs[stage].at[j - 1],
                send_sem=self.send.at[i, slot],
                recv_sem=self.recv.at[i, slot],
                device_id=self.grid.device(other),
                device_id_type=MESH,
            )

    def begin(self, i):
        for copy in self.copies(i, 0):
            copy.start()

    def run(self, first, last):
        for step in range(first, last):
            for stage in range(self.stages):
                i = step - stage * LAG
                if 0 <= i < len(self.pieces):
                    self.add(i, stage)
                    if stage < self.stages - 1:
                        for copy in self.copies(i, stage + 1):
                            copy.start()

    def add(self, i, stage):
        _, _, order, bufs, out = self.pieces[i]
        for copy in self.copies(i, stage):
            copy.wait_recv()
        buf = bufs[stage]
        total = self.pick(i, stage, self.at[order[stage]])[...].astype(f32)
        for j in range(self.grid.size[order[stage]] - 1):
            total = total + buf[j].astype(f32)
        if stage == self.stages - 1:
            out[...] = total.reshape(out.shape)
        else:
            buf[0] = total.astype(buf.dtype)

    def finish(self):
        for i in range(len(self.pieces)):
            for stage in range(self.stages):
                for copy in self.copies(i, stage):
                    copy.wait_send()


def scatter_buffers(grid, order, rows, columns, dtype):
    shapes, left = [], list(DIMS)
    for d in grid.order(order):
        left.remove(d)
        shapes.append((grid.size[d] - 1,) + tuple(grid.size[e] for e in left) + (rows, columns))
    return [pltpu.VMEM(s, dtype) for s in shapes]


def cuts(total, parts, unit):
    while parts > 1 and total % (parts * unit):
        parts -= 1
    return [(j * (total // parts), total // parts) for j in range(parts)]


def dotg(a, b, ca, cb, precision=None):
    return lax.dot_general(
        a, b, (((ca,), (cb,)), ((), ())), preferred_element_type=f32, precision=precision
    )


def iota(shape, dim):
    return lax.broadcasted_iota(jnp.int32, shape, dim)


def three_parts(x):
    high = x.astype(bf16).astype(f32)
    mid = (x - high).astype(bf16).astype(f32)
    return high, mid, x - high - mid


def spread_vector(rows, n):
    shards, width = rows.shape
    total = shards * n
    place = (iota((width, total), 1) % n == iota((width, total), 0)).astype(f32).astype(bf16)
    wide = dotg(rows, place, 1, 0)
    keep = iota((shards, total), 1) // n == iota((shards, total), 0)
    return jnp.sum(jnp.where(keep, wide, 0.0), axis=0, keepdims=True)


def fold_vector(vector, shards, n, width):
    total = shards * n
    keep = iota((shards, total), 1) // n == iota((shards, total), 0)
    place = (iota((total, width), 0) % n == iota((total, width), 1)).astype(f32)
    return dotg(jnp.where(keep, vector, 0.0), place, 1, 0, lax.Precision.HIGHEST)


def attend(qkv_ref, context_ref, lse_ref, live, pair, rows, block):
    length, width = qkv_ref.shape[0], context_ref.shape[1]

    def col(part):
        return pl.ds(pl.multiple_of(part * width + pair * LANES, LANES), LANES)

    k = qkv_ref[:, col(1)].astype(f32) * (1.0 / math.sqrt(HEAD_DIM))
    v = qkv_ref[:, col(2)].astype(f32)
    q = qkv_ref[rows, col(0)].astype(f32)
    lane, row = iota((length, LANES), 1), iota((length, LANES), 0)
    bias = jnp.where(row < live, 0.0, neg_fill)
    few = iota((block, LANES), 1)
    low = few < HEAD_DIM
    sums, tops = [], []
    for h in range(2):
        mine, spare = lane // HEAD_DIM == h, HEAD_DIM * (1 - h)
        keys = jnp.where(mine, k, jnp.where(lane == spare, bias, 0.0)).astype(bf16)
        values = jnp.where(mine, v, 1.0).astype(bf16)
        query = jnp.where(few // HEAD_DIM == h, q, jnp.where(few == spare, 1.0, 0.0)).astype(bf16)
        scores = dotg(query, keys, 1, 1)
        top = jnp.max(scores, axis=1, keepdims=True)
        weights = jnp.exp(scores - top).astype(bf16)
        sums.append(dotg(weights, values, 1, 0))
        tops.append(top)
    num = jnp.where(low, sums[0], sums[1])
    den = pltpu.roll(jnp.where(low, sums[1], sums[0]), HEAD_DIM, 1)
    out = pl.ds(pl.multiple_of(pair * LANES, LANES), LANES)
    context_ref[rows, out] = (num / den).astype(bf16)
    lse_ref[rows, out] = jnp.where(low, tops[0], tops[1]) + jnp.log(den)


def normalize(values):
    center = values - jnp.mean(values, axis=-1, keepdims=True)
    scale = lax.rsqrt(jnp.mean(center * center, axis=-1, keepdims=True) + eps_norm)
    return center * scale, scale


def gather_plan(shapes):
    plan, every = [("s", ())], slice(None)
    for name, unit, parts in (("q", 384, 6), ("o", 384, 2), ("u", 512, 6), ("p", 384, 2), ("d", 256, 3)):
        rows, columns = shapes[name]
        halves = 2 if name == "d" else 1
        for a, n in cuts(columns, parts, LANES):
            for b, m in cuts(rows, halves, 8):
                plan.append((name, (pl.ds(b, m) if halves > 1 else every, pl.ds(a, n))))
    return [(name, sub, GATHER_ORDERS[i % len(GATHER_ORDERS)]) for i, (name, sub) in enumerate(plan)]


def pool_and_loss(views_ref, partners_ref, wp, here, shard_rows, cls_grad, pool_w, pool_b, loss):
    high = lax.Precision.HIGHEST
    rows = views_ref[...].reshape((-1,) + views_ref.shape[-2:])
    pooled, cls = rows[:, 0, :], rows[:, 1, :].astype(bf16)
    views, width = pooled.shape
    scale = lax.rsqrt(jnp.sum(pooled * pooled, axis=1, keepdims=True) + 1e-06)
    unit = pooled * scale
    sims = dotg(unit, unit, 1, 1, high) / logit_divisor
    column, row = iota((views, views), 1), iota((views, views), 0)
    others = jnp.where(row == column, neg_fill, sims)
    top = jnp.max(others, axis=1, keepdims=True)
    weights = jnp.exp(others - top)
    total = jnp.sum(weights, axis=1, keepdims=True)
    partner = column == partners_ref[...]
    target = jnp.sum(jnp.where(partner, sims, 0.0), axis=1, keepdims=True)
    each = top + jnp.log(total) - target
    loss[...] = jnp.broadcast_to(jnp.sum(each, axis=0, keepdims=True) / views, loss.shape)
    pull = weights / total - jnp.where(partner, 1.0, 0.0)
    unit_grad = (dotg(pull, unit, 1, 0, high) + dotg(pull, unit, 0, 0, high)) / logit_divisor
    along = jnp.sum(pooled * unit_grad, axis=1, keepdims=True)
    pooled_grad = scale * unit_grad - pooled * (scale * scale * scale * along)
    pre = (pooled_grad * (1.0 - pooled * pooled)).astype(bf16)
    pre32 = pre.astype(f32)
    mine = jnp.sum(jnp.where(iota((views, width), 0) == here, pre32, 0.0), axis=0, keepdims=True)
    cls_grad[...] = dotg(jnp.broadcast_to(mine, (8, width)).astype(bf16), wp, 1, 1)
    place = iota((width, LANES), 0) == here * shard_rows + iota((width, LANES), 1)
    cls_rows = dotg(cls, place.astype(f32).astype(bf16), 1, 0).astype(bf16)
    pool_w[...] = dotg(cls_rows, pre, 0, 0)[:shard_rows]
    sums = jnp.broadcast_to(jnp.sum(pre32, axis=0, keepdims=True), (8, width))
    pool_b[...] = dotg(sums, place.astype(f32), 1, 0, high)


def forward_kernel(grid, whole, plan, sizes, shard_rows, *refs):
    (len_ref, tokens_ref, partners_ref, keep_a, keep_f, wq, wo, wu, wd, wp), refs = refs[:10], refs[10:]
    count = len(sizes)
    small_in, refs = refs[:count], refs[count:]
    (hq, ho, hu, hd), refs = refs[:4], refs[4:]
    (qkv_ref, context, lse, tokens_t, context_t, hidden_t, norm1, scale1, norm2, scale2, layer_out), refs = refs[:11], refs[11:]
    (act_t, slope, cls_grad, pool_w, pool_b, loss), refs = refs[:6], refs[6:]
    small_out, refs = refs[:count], refs[count:]
    (gq, go, gu, gd, gp, gs, views, keep, hidden, hidden_low, act, act_buf, slope_buf, pack), refs = refs[:14], refs[14:]
    send, recv, view_send, view_recv, own_sem, keep_sem, act_sem, slope_sem, out_sem = refs
    length, width = context.shape
    b_qv, b_out, g1, b1, b_up, b_down, g2, b2, b_pool = small_out
    at = grid.me()
    own = tuple(at[d] for d in DIMS)
    load = pltpu.make_async_copy(keep_a, keep, keep_sem)
    load.start()
    to_own = []
    for i, (src, dst) in enumerate(((wq, gq), (wo, go), (wu, gu), (wd, gd), (wp, gp))):
        to_own.append(pltpu.make_async_copy(src, dst.at[own], own_sem.at[i]))
        to_own[-1].start()
    mine = gs.at[own]
    mine[...] = jnp.zeros(mine.shape, bf16)
    for i, (ref, n) in enumerate(zip(small_in, sizes)):
        mine[i : i + 1, 0:n] = ref[...]
    where = dict(q=gq, o=go, u=gu, d=gd, p=gp, s=gs)
    gather = Gather(grid, [(where[name], sub, order) for name, sub, order in plan], send, recv)
    number = {}
    for i, (name, _, _) in enumerate(plan):
        number.setdefault(name, []).append(i)
    end = {name: [gather.whole[i] for i in numbers] for name, numbers in number.items()}
    whole.barrier()
    for copy in to_own:
        copy.wait()
    gather.begin()
    tokens_t[...] = tokens_ref[...].astype(f32).T.astype(bf16)
    gather.until(end["s"][0])
    rows = gs[...].reshape((grid.count,) + gs.shape[-2:])
    for i, (ref, n) in enumerate(zip(small_out, sizes)):
        ref[...] = spread_vector(rows[:, i, :], n)
    for i in number["q"]:
        gather.until(gather.whole[i])
        lo, n = plan[i][1][1].start, plan[i][1][1].size
        out = dotg(tokens_ref[...], gq[:, :, :, :, :, lo : lo + n].reshape(-1, n), 1, 0)
        if lo < width:
            out = out + b_qv[:, lo : lo + n]
        elif lo >= 2 * width:
            out = out + b_qv[:, lo - width : lo - width + n]
        qkv_ref[:, lo : lo + n] = out.astype(bf16)

    pairs, block = width // LANES, min(512, length)
    blocks, live = length // block, len_ref[0]
    slots = pairs * blocks
    first, last = gather.now, end["u"][len(end["u"]) // 2]

    def attention(t):
        at_row = pl.ds(pl.multiple_of((t % blocks) * block, block), block)
        attend(qkv_ref, context, lse, live, t // blocks, at_row, block)

    gather.loop(slots, [first + t * (last - first) // slots for t in range(slots)], attention)

    load.wait()
    block = min(256, length)
    blocks = length // block

    def row_block(t):
        return pl.ds(pl.multiple_of(t * block, block), block)

    gather.until(end["o"][-1])

    def project(t):
        here = row_block(t)
        attended = dotg(context[here, :], go[...].reshape(width, width), 1, 0) + b_out[...]
        total = tokens_ref[here, :].astype(f32) + attended * (keep[here, :].astype(f32) * keep_scale)
        norm, scale = normalize(total)
        out = norm * g1[...] + b1[...]
        hidden[here, :] = out
        hidden_low[here, :] = out.astype(bf16)
        hidden_t[:, here] = out.T.astype(bf16)
        context_t[:, here] = context[here, :].astype(f32).T.astype(bf16)
        norm1[here, :] = norm.astype(bf16)
        scale1[here, :] = jnp.broadcast_to(scale, (block, LANES))

    gather.loop(blocks, [gather.now] * blocks, project)
    load = pltpu.make_async_copy(keep_f, keep, keep_sem)
    load.start()

    parts = len(end["u"])
    step = gu.shape[-1] // parts

    def stored(buf, hbm, sem, t, here, cols, transposed):
        dst = hbm.at[cols, here] if transposed else hbm.at[here, cols]
        return pltpu.make_async_copy(buf.at[t % 2], dst, sem.at[t % 2])

    def up(t):
        here = row_block(t % blocks)
        cols = pl.ds(pl.multiple_of(t // blocks * step, step), step)
        pre = dotg(hidden_low[here, :], gu[:, :, :, :, :, cols].reshape(width, step), 1, 0) + b_up[:, cols]
        cdf = 0.5 * (1.0 + lax.erf(pre * (1.0 / math.sqrt(2.0))))
        pdf = jnp.exp(-0.5 * pre * pre) * (1.0 / math.sqrt(2.0 * math.pi))
        out = pre * cdf
        act[here, cols] = out.astype(bf16)

        @pl.when(t >= 2)
        def _():
            stored(act_buf, act_t, act_sem, t, here, cols, True).wait()
            stored(slope_buf, slope, slope_sem, t, here, cols, False).wait()

        act_buf[t % 2] = out.T.astype(bf16)
        slope_buf[t % 2] = (cdf + pre * pdf).astype(bf16)
        stored(act_buf, act_t, act_sem, t, here, cols, True).start()
        stored(slope_buf, slope, slope_sem, t, here, cols, False).start()

    slots = parts * blocks
    marks = []
    for t in range(slots):
        marks.append(end["u"][t // blocks])
    last = end["d"][0]
    for t in range(slots):
        marks[t] = max(marks[t], gather.now + t * (last - gather.now) // slots if last > gather.now else 0)
    gather.loop(slots, marks, up)
    for t in (slots - 2, slots - 1):
        here, cols = row_block(0), pl.ds(0, step)
        stored(act_buf, act_t, act_sem, t, here, cols, True).wait()
        stored(slope_buf, slope, slope_sem, t, here, cols, False).wait()

    load.wait()
    parts = len(end["d"]) // len(cuts(gd.shape[-2], 2, 8))
    step = width // parts

    def down(here, cols):
        out = dotg(act[here, :], gd[:, :, :, :, :, cols].reshape(-1, step), 1, 0) + b_down[:, cols]
        hidden[here, cols] += out * (keep[here, cols].astype(f32) * keep_scale)

    slots = (parts - 1) * blocks
    ends = end["d"][len(end["d"]) // parts - 1 :: len(end["d"]) // parts]
    gather.loop(
        slots,
        [ends[t // blocks] for t in range(slots)],
        lambda t: down(row_block(t % blocks), pl.ds(pl.multiple_of(t // blocks * step, step), step)),
    )
    gather.until(ends[-1])
    at_all = whole.me()
    exchange = Gather(whole, [(views, (), GATHER_ORDERS[0])], view_send, view_recv)

    def norm(t):
        here = row_block(t)
        down(here, pl.ds((parts - 1) * step, step))
        value, scale = normalize(hidden[here, :])
        out = value * g2[...] + b2[...]
        norm2[here, :] = value.astype(bf16)
        scale2[here, :] = jnp.broadcast_to(scale, (block, LANES))
        layer_out[here, :] = out.astype(bf16)

        @pl.when(t == 0)
        def _():
            head = out[0:8].astype(bf16)
            pooled = jnp.tanh(dotg(head, gp[...].reshape(width, width), 1, 0) + b_pool[...])
            pack[0:1, :] = pooled[0:1]
            pack[1:2, :] = head[0:1].astype(f32)
            views[tuple(at_all[d] for d in DIMS)] = pack[0:2, :]
            exchange.begin()

    exchange.loop(blocks, [max(0, t - 1) for t in range(blocks)], norm)
    outs = []
    for i, (src, dst) in enumerate(((gq, hq), (go, ho), (gu, hu), (gd, hd))):
        outs.append(pltpu.make_async_copy(src, dst, out_sem.at[i]))
        outs[-1].start()
    exchange.until(len(exchange.events))
    here = lax.axis_index("dp") * (whole.size["y"] * whole.size["x"]) + lax.axis_index("fsdp")
    pool_and_loss(views, partners_ref, gp[...].reshape(width, width), here, shard_rows, cls_grad, pool_w, pool_b, loss)
    exchange.finish()
    gather.finish()
    for copy in outs:
        copy.wait()


def run_forward(grid, whole, length_of, tokens, partners, keep_a, keep_f, big, small, shard_rows):
    length, width = tokens.shape
    names = ("q", "o", "u", "d", "p")
    shapes = {k: w.shape for k, w in zip(names, big)}
    inner = shapes["u"][1]
    sizes = [v.shape[0] for v in small]
    plan = gather_plan(shapes)
    pad = -(-max(sizes) // LANES) * LANES
    step = inner // sum(p[0] == "u" for p in plan)
    block = min(256, length)
    vmem, anywhere = pl.BlockSpec(memory_space=pltpu.VMEM), pl.BlockSpec(memory_space=pl.ANY)
    shape = jax.ShapeDtypeStruct
    outs = pl.pallas_call(
        functools.partial(forward_kernel, grid, whole, plan, sizes, shard_rows),
        out_shape=[shape(grid.shape + shapes[k], bf16) for k in names[:4]]
        + [
            shape((length, 3 * width), bf16),
            shape((length, width), bf16),
            shape((length, width), f32),
            shape((width, length), bf16),
            shape((width, length), bf16),
            shape((width, length), bf16),
            shape((length, width), bf16),
            shape((length, LANES), f32),
            shape((length, width), bf16),
            shape((length, LANES), f32),
            shape((length, width), bf16),
            shape((inner, length), bf16),
            shape((length, inner), bf16),
            shape((8, width), f32),
            shape((shard_rows, width), f32),
            shape((8, LANES), f32),
            shape((8, LANES), f32),
        ]
        + [shape((1, grid.count * n), f32) for n in sizes],
        in_specs=[pl.BlockSpec(memory_space=pltpu.SMEM), vmem, vmem, anywhere, anywhere] + [vmem] * (5 + len(small)),
        out_specs=[anywhere] * 4 + [vmem] * 11 + [anywhere] * 2 + [vmem] * (4 + len(small)),
        scratch_shapes=[pltpu.VMEM(grid.shape + shapes[k], bf16) for k in names]
        + [
            pltpu.VMEM(grid.shape + (16, pad), bf16),
            pltpu.VMEM(whole.shape + (2, width), f32),
            pltpu.VMEM((length, width), jnp.int32),
            pltpu.VMEM((length, width), f32),
            pltpu.VMEM((length, width), bf16),
            pltpu.VMEM((length, inner), bf16),
            pltpu.VMEM((2, step, block), bf16),
            pltpu.VMEM((2, block, step), bf16),
            pltpu.VMEM((8, width), f32),
            pltpu.SemaphoreType.DMA((len(plan), grid.slots)),
            pltpu.SemaphoreType.DMA((len(plan), grid.slots)),
            pltpu.SemaphoreType.DMA((1, whole.slots)),
            pltpu.SemaphoreType.DMA((1, whole.slots)),
            pltpu.SemaphoreType.DMA((5,)),
            pltpu.SemaphoreType.DMA,
            pltpu.SemaphoreType.DMA((2,)),
            pltpu.SemaphoreType.DMA((2,)),
            pltpu.SemaphoreType.DMA((4,)),
        ],
        compiler_params=pltpu.CompilerParams(
            collective_id=0, has_side_effects=True, vmem_limit_bytes=VMEM_LIMIT
        ),
        name="forward",
    )(length_of, tokens, partners.reshape(-1, 1), keep_a, keep_f, *big, *[v.reshape(1, -1) for v in small])
    return outs


def attend_back(qkv_ref, context, dcontext, lse, live, pair, block, prep, acc, tick):
    length, width = qkv_ref.shape[0], context.shape[1]
    scale = 1.0 / math.sqrt(HEAD_DIM)
    one = pl.ds(pl.multiple_of(pair * LANES, LANES), LANES)

    def col(part):
        return pl.ds(pl.multiple_of(part * width + pair * LANES, LANES), LANES)

    q, k, v = (qkv_ref[:, col(j)].astype(f32) for j in range(3))
    d = dcontext[:, one].astype(f32)
    lane, row = iota((length, LANES), 1), iota((length, LANES), 0)
    bias = jnp.where(row < live, 0.0, neg_fill)
    both = d * context[:, one].astype(f32)
    total = lse[:, one]
    other = pltpu.roll(total, HEAD_DIM, 1)
    for h in range(2):
        mine, a = lane // HEAD_DIM == h, HEAD_DIM * (1 - h)
        inner = jnp.sum(jnp.where(mine, both, 0.0), axis=1, keepdims=True)
        l0, l1, l2 = three_parts(-other)
        d0, d1, d2 = three_parts(-inner)

        def lanes(base, *extra):
            out = 0.0
            for j, e in reversed(list(enumerate(extra))):
                out = jnp.where(lane == a + j, e, out)
            return jnp.where(mine, base, out).astype(bf16)

        prep[h, 0] = lanes(q * scale, 1.0, l0, l1, l2)
        prep[h, 1] = lanes(k, bias, 1.0, 1.0, 1.0)
        prep[h, 2] = lanes(d, d0, d1, d2)
        prep[h, 3] = lanes(v, 1.0, 1.0, 1.0)
        prep[h, 4] = lanes(q * scale)
        prep[h, 5] = lanes(d)
        prep[h, 6] = lanes(k * scale)
    q_t = (q * scale).T.astype(bf16)
    d_t = d.T.astype(bf16)
    acc[...] = jnp.zeros_like(acc)
    for i in range(length // block):
        rows = slice(i * block, (i + 1) * block)
        dq = jnp.zeros((block, LANES), f32)
        for h in range(2):
            head = slice(h * HEAD_DIM, (h + 1) * HEAD_DIM)
            p = jnp.exp(dotg(prep[h, 0, rows, :], prep[h, 1], 1, 1))
            dp = dotg(prep[h, 2, rows, :], prep[h, 3], 1, 1)
            ds = (p * dp).astype(bf16)
            acc[0, head, :] += dotg(d_t[head, rows], p.astype(bf16), 1, 0)
            acc[1, head, :] += dotg(q_t[head, rows], ds, 1, 0)
            dq = dq + dotg(ds, prep[h, 6], 1, 0)
        qkv_ref[rows, col(0)] = dq.astype(bf16)
        tick(i)
    qkv_ref[:, col(1)] = acc[1].T.astype(bf16)
    qkv_ref[:, col(2)] = acc[0].T.astype(bf16)


def scatter_plan(grid, shapes):
    plan, every = [], slice(None)
    for name, parts in (("d", 6), ("u", 6), ("o", 2), ("q", 9)):
        rows, columns = shapes[name]
        if name == "d":
            plan += [(name, (pl.ds(a, n), every), n, columns) for a, n in cuts(rows, parts, 8)]
        else:
            plan += [(name, (every, pl.ds(a, n)), rows, n) for a, n in cuts(columns, parts, LANES)]
    plan.append(("s", (), 16, shapes["s"]))
    return [(p[0], p[1], SCATTER_ORDERS[i % 2]) + p[2:] for i, p in enumerate(plan)]


def backward_kernel(grid, plan, sizes, len_ref, qkv_hbm, context, dcontext, lse, tokens_t, first_grad, wq, dd, du, do, *refs):
    count = len(sizes)
    small_in, refs = refs[: count - 1], refs[count - 1 :]
    (rq, ro, ru, rd, rs, tokens_grad), refs = refs[:6], refs[6:]
    (qkv_ref, dq, dsmall, prep, acc, send, recv, sem), bufs = refs[:8], list(refs[8:])
    load = pltpu.make_async_copy(qkv_hbm, qkv_ref, sem)
    load.start()
    sources, results = dict(d=dd, u=du, o=do, q=dq, s=dsmall), dict(d=rd, u=ru, o=ro, q=rq, s=rs)
    pieces = []
    for name, sub, order, _, _ in plan:
        n = len(grid.order(order))
        pieces.append((sources[name], sub, order, bufs[:n], results[name].at[sub] if sub else results[name]))
        bufs = bufs[n:]
    scatter = Scatter(grid, pieces, send, recv)
    names = [p[0] for p in plan]
    ready = names.index("q")
    grid.barrier()
    for i in range(ready):
        scatter.begin(i)
    load.wait()
    length, width = context.shape
    pairs, block = width // LANES, min(256, length)
    blocks = length // block
    slots, live = pairs * blocks, len_ref[0]

    def one_pair(pair, _):
        def tick(i):
            for p in range(pairs):
                t = p * blocks + i

                @pl.when(pair == p)
                def _():
                    scatter.run(t * ready // slots, (t + 1) * ready // slots)

        attend_back(qkv_ref, context, dcontext, lse, live, pair, block, prep, acc, tick)
        return 0

    lax.fori_loop(0, pairs, one_pair, 0)
    step = ready
    for i in range(ready, len(plan) - 1):
        sub = plan[i][1]
        part = dotg(tokens_t[...], qkv_ref[:, sub[1].start : sub[1].start + sub[1].size], 1, 0)
        dq[:, :, :, :, :, sub[1]] = part.astype(bf16).reshape(grid.shape + (-1, sub[1].size))
        scatter.begin(i)
        if i - 2 >= ready:
            scatter.run(step, step + 1)
            step += 1
    sums = dotg(jnp.ones((8, length), bf16), qkv_ref[...], 1, 0)[0:1]
    vectors = [jnp.concatenate([sums[:, :width], sums[:, 2 * width :]], axis=1)] + [r[...] for r in small_in]
    pad = dsmall.shape[-1]
    dsmall[...] = jnp.zeros_like(dsmall)
    for j, (v, n) in enumerate(zip(vectors, sizes)):
        dsmall[:, :, :, :, j, :] = fold_vector(v, grid.count, n, pad).reshape(grid.shape + (pad,))
    scatter.begin(len(plan) - 1)
    rest = scatter.steps - step
    parts = 4
    rows = length // parts
    for i in range(parts):
        scatter.run(step + i * rest // parts, step + (i + 1) * rest // parts)
        here = slice(i * rows, (i + 1) * rows)
        grad = first_grad[here, :] + dotg(qkv_ref[here, :], wq[...], 1, 1)
        tokens_grad[here, :] = grad.astype(bf16)
    scatter.finish()


def run_backward(grid, length_of, qkv, context, dcontext, lse, tokens_t, first_grad, wq, big, small, sizes):
    width, length = tokens_t.shape
    dd, du, do = big
    rows = {k: w.shape[0] // grid.count for k, w in (("d", dd), ("u", du), ("o", do), ("q", wq))}
    columns = {k: w.shape[1] for k, w in (("d", dd), ("u", du), ("o", do), ("q", wq))}
    pad = -(-max(sizes) // LANES) * LANES
    shapes = {k: (rows[k], columns[k]) for k in rows}
    shapes["s"] = pad
    plan = scatter_plan(grid, shapes)
    bufs = []
    for name, _, order, r, c in plan:
        bufs += scatter_buffers(grid, order, r, c, f32 if name == "s" else bf16)
    vmem, anywhere = pl.BlockSpec(memory_space=pltpu.VMEM), pl.BlockSpec(memory_space=pl.ANY)
    return pl.pallas_call(
        functools.partial(backward_kernel, grid, plan, sizes),
        out_shape=[jax.ShapeDtypeStruct(shapes[k], f32) for k in ("q", "o", "u", "d")]
        + [jax.ShapeDtypeStruct((16, pad), f32), jax.ShapeDtypeStruct((length, width), bf16)],
        in_specs=[pl.BlockSpec(memory_space=pltpu.SMEM), anywhere] + [vmem] * (9 + len(small)),
        out_specs=[vmem] * 6,
        scratch_shapes=[
            pltpu.VMEM(qkv.shape, bf16),
            pltpu.VMEM(grid.shape + shapes["q"], bf16),
            pltpu.VMEM(grid.shape + (16, pad), f32),
            pltpu.VMEM((2, 7, length, LANES), bf16),
            pltpu.VMEM((2, LANES, length), f32),
            pltpu.SemaphoreType.DMA((len(plan), grid.slots)),
            pltpu.SemaphoreType.DMA((len(plan), grid.slots)),
            pltpu.SemaphoreType.DMA,
        ]
        + bufs,
        compiler_params=pltpu.CompilerParams(
            collective_id=2, has_side_effects=True, vmem_limit_bytes=VMEM_LIMIT
        ),
        name="attend_back_and_scatter",
    )(
        length_of,
        qkv,
        context,
        dcontext,
        lse,
        tokens_t,
        first_grad,
        wq,
        *[w.reshape(grid.shape + (-1, w.shape[1])) for w in (dd, du, do)],
        *[v.reshape(1, -1) for v in small],
    )


def dot(a, b):
    return jnp.dot(a, b, preferred_element_type=f32)


def on_device(whole, grid, tokens, lengths, keep_attn, keep_ffn, partners, out_cot, *weights):
    (w_qkv, b_qv, w_out, b_out, ln1_gain, ln1_bias, w_up, b_up, w_down, b_down, ln2_gain, ln2_bias, w_pool, b_pool) = weights
    _, length, width = tokens.shape
    big = [w_qkv, w_out, w_up, w_down, w_pool]
    small = [b_qv, b_out, ln1_gain, ln1_bias, b_up, b_down, ln2_gain, ln2_bias, b_pool]
    shard_rows = w_qkv.shape[0]
    if not grid.with_fsdp:
        big = [lax.all_gather(w, "fsdp", axis=0, tiled=True) for w in big]
        small = [lax.all_gather(v, "fsdp", axis=0, tiled=True) for v in small]
    sizes = [v.shape[0] for v in small]
    outs = run_forward(
        grid, whole, lengths, tokens.reshape(length, width), partners, keep_attn.reshape(length, width),
        keep_ffn.reshape(length, width), big, small, shard_rows,
    )
    wq, wo, wu, wd = (g.reshape(-1, g.shape[-1]) for g in outs[:4])
    qkv, context, lse, tokens_t, context_t, hidden_t, norm1, scale1, norm2, scale2, layer_out = outs[4:15]
    act_t, slope, cls_grad, pool_weight_grad, pool_bias_grad, loss = outs[15:21]
    v_g1, v_g2 = outs[21 + 2], outs[21 + 6]
    keep_a = keep_attn.reshape(length, width).astype(f32) * keep_scale
    keep_f = keep_ffn.reshape(length, width).astype(f32) * keep_scale
    first_row = jnp.arange(length, dtype=jnp.int32)[:, None] == 0
    out_grad = out_cot.reshape(length, width).astype(f32) + jnp.where(first_row, cls_grad[0:1], 0.0)

    def norm_back(grad, norm, scale, gain):
        norm = norm.astype(f32)
        scaled = grad * gain
        along = jnp.mean(scaled * norm, axis=1, keepdims=True)
        back = scale[:, 0:1] * (scaled - jnp.mean(scaled, axis=1, keepdims=True) - norm * along)
        return back, jnp.sum(grad * norm, axis=0), jnp.sum(grad, axis=0)

    second_grad, g2_grad, b2_grad = norm_back(out_grad, norm2, scale2, v_g2)
    down_grad = (second_grad * keep_f).astype(bf16)
    down_weight_grad = dot(act_t, down_grad).astype(bf16)
    up_grad = lax.dot_general(down_grad, wd, (((1,), (1,)), ((), ())), preferred_element_type=f32)
    up_grad = (up_grad * slope.astype(f32)).astype(bf16)
    up_weight_grad = dot(hidden_t, up_grad).astype(bf16)
    hidden_grad = second_grad + lax.dot_general(up_grad, wu, (((1,), (1,)), ((), ())), preferred_element_type=f32)
    first_grad, g1_grad, b1_grad = norm_back(hidden_grad, norm1, scale1, v_g1)
    attended_grad = (first_grad * keep_a).astype(bf16)
    out_weight_grad = dot(context_t, attended_grad).astype(bf16)
    context_grad = lax.dot_general(attended_grad, wo, (((1,), (1,)), ((), ())), preferred_element_type=f32).astype(bf16)

    def column_sum(x):
        return jnp.sum(x.astype(f32), axis=0)

    vector_grads = [column_sum(attended_grad), g1_grad, b1_grad, column_sum(up_grad), column_sum(down_grad), g2_grad, b2_grad]
    rq, ro, ru, rd, rs, tokens_grad = run_backward(
        grid, lengths, qkv, context, context_grad, lse, tokens_t, first_grad, wq,
        [down_weight_grad, up_weight_grad, out_weight_grad], vector_grads, sizes[:-1],
    )
    owned = [rq, ro, ru, rd] + [rs[j, :n] for j, n in enumerate(sizes[:-1])]
    if not grid.with_fsdp:
        owned = [lax.psum_scatter(g, "fsdp", scatter_dimension=0, tiled=True) for g in owned]
    rq, ro, ru, rd, s_qv, s_out, s_g1, s_b1, s_up, s_down, s_g2, s_b2 = owned
    return (
        layer_out.reshape(tokens.shape), tokens_grad.reshape(tokens.shape), rq, s_qv, ro, s_out, s_g1, s_b1, ru, s_up,
        rd, s_down, s_g2, s_b2, pool_weight_grad, pool_bias_grad[0, :shard_rows], loss[0, 0],
    )


def solution(mesh):
    rows, vector, matrix = P(AXES, None, None), P(AXES), P(AXES, None)
    weights = (matrix, vector, matrix, vector, vector, vector, matrix, vector, matrix, vector, vector, vector, matrix, vector)
    devices = mesh.shape["dp"] * mesh.shape["fsdp"]

    def step(*args):
        whole = Grid(mesh)
        grid = whole if (args[6].shape[0] // devices) % 8 == 0 else Grid(mesh, False)
        return jax.shard_map(
            functools.partial(on_device, whole, grid),
            mesh=mesh,
            in_specs=(rows, vector, rows, rows, P(), rows) + weights,
            out_specs=(rows, rows) + weights + (P(),),
            check_vma=False,
        )(*args)

    return step
```

```python
import functools
import math

import jax
import jax.numpy as jnp
from jax import lax
from jax.experimental import pallas as pl
from jax.experimental.pallas import tpu as pltpu
from jax.sharding import PartitionSpec as P

HEAD_DIM = 64
LANES = 128
f32, bf16 = jnp.float32, jnp.bfloat16
MESH = pl.DeviceIdType.MESH
AXES = ("dp", "fsdp")
eps_norm = 1e-05
keep_scale = 1.0 / 0.9
logit_divisor = 0.05
neg_fill = -1000000000.0
VMEM_LIMIT = 67043328
DIMS = ("z", "c", "y", "x")
GATHER_ORDERS = (
    ("z", "x", "y", "c"),
    ("x", "z", "y", "c"),
    ("z", "y", "x", "c"),
    ("z", "y", "x", "c"),
    ("y", "z", "x", "c"),
    ("z", "x", "y", "c"),
)
SCATTER_ORDERS = (("c", "y", "x", "z"), ("c", "x", "y", "z"))
LAG = 2


class Grid:
    def __init__(self, mesh, with_fsdp=True):
        dp, fsdp = mesh.shape["dp"], mesh.shape["fsdp"]
        cores = 2 if dp % 2 == 0 else 1
        side = math.isqrt(fsdp)
        if side * side != fsdp:
            side = fsdp
        self.with_fsdp = with_fsdp
        self.size = {
            "z": dp // cores,
            "c": cores,
            "y": fsdp // side if with_fsdp else 1,
            "x": side if with_fsdp else 1,
        }
        self.shape = tuple(self.size[d] for d in DIMS)
        self.count = math.prod(self.shape)
        self.slots = sum(n - 1 for n in self.shape)

    def me(self):
        dp, fsdp = lax.axis_index("dp"), lax.axis_index("fsdp")
        at = {"z": lax.div(dp, self.size["c"]), "c": lax.rem(dp, self.size["c"])}
        if self.with_fsdp:
            at["y"], at["x"] = lax.div(fsdp, self.size["x"]), lax.rem(fsdp, self.size["x"])
        else:
            at["y"], at["x"] = 0, 0
        return at

    def device(self, at):
        fsdp = at["y"] * self.size["x"] + at["x"] if self.with_fsdp else lax.axis_index("fsdp")
        return (at["z"] * self.size["c"] + at["c"], fsdp)

    def peer(self, at, dim, j):
        other = dict(at)
        other[dim] = lax.rem(at[dim] + j, self.size[dim])
        return other

    def slot(self, dim, j):
        base = 0
        for d in DIMS:
            if d == dim:
                return base + j - 1
            base += self.size[d] - 1

    def order(self, order):
        return tuple(d for d in order if self.size[d] > 1)

    def straight(self):
        return [{d: j} for d in DIMS for j in range(1, self.size[d])]

    def around(self, dims):
        offsets = [{}]
        for d in dims:
            offsets = [{**o, d: j} if j else o for o in offsets for j in range(self.size[d])]
        return [o for o in offsets if o]

    def moved(self, at, offset):
        return {d: lax.rem(at[d] + offset[d], self.size[d]) if d in offset else at[d] for d in DIMS}

    def barrier(self, offsets):
        at, sem = self.me(), pltpu.get_barrier_semaphore()
        for offset in offsets:
            pl.semaphore_signal(
                sem, inc=1, device_id=self.device(self.moved(at, offset)), device_id_type=MESH
            )
        pl.semaphore_wait(sem, len(offsets))


class Exchange:
    def __init__(self, grid, ref, send, recv):
        self.grid, self.ref, self.send, self.recv, self.at = grid, ref, send, recv, grid.me()
        self.groups = [("z", "c"), ("y", "x")]

    def copies(self, stage):
        done = self.groups[0] if stage else ()
        view = self.ref.at[tuple(slice(None) if d in done else self.at[d] for d in DIMS)]
        first = len(self.grid.around(self.groups[0])) if stage else 0
        for j, offset in enumerate(self.grid.around(self.groups[stage])):
            yield pltpu.make_async_remote_copy(
                src_ref=view,
                dst_ref=view,
                send_sem=self.send.at[first + j],
                recv_sem=self.recv.at[first + j],
                device_id=self.grid.device(self.grid.moved(self.at, offset)),
                device_id_type=MESH,
            )

    def start(self, stage):
        for copy in self.copies(stage):
            copy.start()

    def wait(self, stage):
        for copy in self.copies(stage):
            copy.wait_recv()

    def finish(self):
        for stage in range(2):
            for copy in self.copies(stage):
                copy.wait_send()


class Gather:
    def __init__(self, grid, pieces, send, recv, window=4, lag=3):
        self.grid, self.send, self.recv, self.at = grid, send, recv, grid.me()
        self.pieces = [(ref, sub, grid.order(order)) for ref, sub, order in pieces]
        self.stages, self.window, self.now = len(self.pieces[0][2]), window, 0
        self.events = [
            (step - stage * lag, stage)
            for step in range(len(pieces) + (self.stages - 1) * lag)
            for stage in range(self.stages)
            if 0 <= step - stage * lag < len(pieces)
        ]
        self.whole = [self.events.index((i, self.stages - 1)) + 1 for i in range(len(pieces))]

    def copies(self, i, stage):
        ref, sub, order = self.pieces[i]
        dim, done = order[stage], order[:stage]
        index = tuple(slice(None) if d in done else self.at[d] for d in DIMS)
        view = ref.at[index + sub]
        for j in range(1, self.grid.size[dim]):
            slot = self.grid.slot(dim, j)
            yield pltpu.make_async_remote_copy(
                src_ref=view,
                dst_ref=view,
                send_sem=self.send.at[i, slot],
                recv_sem=self.recv.at[i, slot],
                device_id=self.grid.device(self.grid.peer(self.at, dim, j)),
                device_id_type=MESH,
            )

    def start(self, i, stage):
        for copy in self.copies(i, stage):
            copy.start()

    def begin(self):
        for i in range(min(self.window, len(self.pieces))):
            self.start(i, 0)

    def run(self, first, last):
        for i, stage in self.events[first:last]:
            for copy in self.copies(i, stage):
                copy.wait_recv()
            if stage == 0 and i + self.window < len(self.pieces):
                self.start(i + self.window, 0)
            if stage < self.stages - 1:
                self.start(i, stage + 1)

    def until(self, last):
        self.run(self.now, max(self.now, last))
        self.now = max(self.now, last)

    def finish(self):
        self.until(len(self.events))
        for i in range(len(self.pieces)):
            for stage in range(self.stages):
                for copy in self.copies(i, stage):
                    copy.wait_send()

    def loop(self, count, marks, body):
        marks = [max(self.now, m) for m in marks]
        starts = [self.now] + marks[:-1]

        def step(t, _):
            for k in range(count):
                if marks[k] > starts[k]:

                    @pl.when(t == k)
                    def _():
                        self.run(starts[k], marks[k])

            body(t)
            return 0

        lax.fori_loop(0, count, step, 0)
        self.now = marks[-1]


class Scatter:
    def __init__(self, grid, pieces, send, recv):
        self.grid, self.send, self.recv, self.at = grid, send, recv, grid.me()
        self.pieces = [(src, sub, grid.order(order), bufs, out) for src, sub, order, bufs, out in pieces]
        self.stages = len(self.pieces[0][2])
        self.steps = len(pieces) + (self.stages - 1) * LAG

    def pick(self, i, stage, where):
        src, sub, order, bufs, _ = self.pieces[i]
        left = tuple(d for d in DIMS if d not in order[:stage])
        index = tuple(where if d == order[stage] else slice(None) for d in left)
        if stage == 0:
            return src.at[index + sub]
        return bufs[stage - 1].at[(0,) + index]

    def copies(self, i, stage):
        _, _, order, bufs, _ = self.pieces[i]
        dim = order[stage]
        for j in range(1, self.grid.size[dim]):
            other = self.grid.peer(self.at, dim, j)
            slot = self.grid.slot(dim, j)
            yield pltpu.make_async_remote_copy(
                src_ref=self.pick(i, stage, other[dim]),
                dst_ref=bufs[stage].at[j - 1],
                send_sem=self.send.at[i, slot],
                recv_sem=self.recv.at[i, slot],
                device_id=self.grid.device(other),
                device_id_type=MESH,
            )

    def begin(self, i):
        for copy in self.copies(i, 0):
            copy.start()

    def run(self, first, last):
        for step in range(first, last):
            for stage in range(self.stages):
                i = step - stage * LAG
                if 0 <= i < len(self.pieces):
                    self.add(i, stage)
                    if stage < self.stages - 1:
                        for copy in self.copies(i, stage + 1):
                            copy.start()

    def add(self, i, stage):
        _, _, order, bufs, out = self.pieces[i]
        for copy in self.copies(i, stage):
            copy.wait_recv()
        buf = bufs[stage]
        total = self.pick(i, stage, self.at[order[stage]])[...].astype(f32)
        for j in range(self.grid.size[order[stage]] - 1):
            total = total + buf[j].astype(f32)
        if stage == self.stages - 1:
            out[...] = total.reshape(out.shape)
        else:
            buf[0] = total.astype(buf.dtype)

    def finish(self):
        for i in range(len(self.pieces)):
            for stage in range(self.stages):
                for copy in self.copies(i, stage):
                    copy.wait_send()


def scatter_buffers(grid, order, rows, columns, dtype):
    shapes, left = [], list(DIMS)
    for d in grid.order(order):
        left.remove(d)
        shapes.append((grid.size[d] - 1,) + tuple(grid.size[e] for e in left) + (rows, columns))
    return [pltpu.VMEM(s, dtype) for s in shapes]


def cuts(total, parts, unit):
    while parts > 1 and total % (parts * unit):
        parts -= 1
    return [(j * (total // parts), total // parts) for j in range(parts)]


def dotg(a, b, ca, cb, precision=None):
    return lax.dot_general(
        a, b, (((ca,), (cb,)), ((), ())), preferred_element_type=f32, precision=precision
    )


def iota(shape, dim):
    return lax.broadcasted_iota(jnp.int32, shape, dim)


def three_parts(x):
    high = x.astype(bf16).astype(f32)
    mid = (x - high).astype(bf16).astype(f32)
    return high, mid, x - high - mid


def spread_vector(rows, n):
    shards, width = rows.shape
    total = shards * n
    place = (iota((width, total), 1) % n == iota((width, total), 0)).astype(f32).astype(bf16)
    wide = dotg(rows, place, 1, 0)
    keep = iota((shards, total), 1) // n == iota((shards, total), 0)
    return jnp.sum(jnp.where(keep, wide, 0.0), axis=0, keepdims=True)


def fold_vector(vector, shards, n, width):
    total = shards * n
    keep = iota((shards, total), 1) // n == iota((shards, total), 0)
    place = (iota((total, width), 0) % n == iota((total, width), 1)).astype(f32).astype(bf16)
    parts = [jnp.where(keep, part, 0.0).astype(bf16) for part in three_parts(vector)]
    return sum(dotg(part, place, 1, 0) for part in parts)


def attend_prepare(qkv_ref, prep, live, pair):
    length, width = qkv_ref.shape[0], qkv_ref.shape[1] // 3
    k = qkv_ref[:, pl.ds(pl.multiple_of(width + pair * LANES, LANES), LANES)].astype(f32)
    v = qkv_ref[:, pl.ds(pl.multiple_of(2 * width + pair * LANES, LANES), LANES)].astype(f32)
    lane, row = iota((length, LANES), 1), iota((length, LANES), 0)
    bias = jnp.where(row < live, 0.0, neg_fill)
    k = k * (1.0 / math.sqrt(HEAD_DIM))
    for h in range(2):
        mine, spare = lane // HEAD_DIM == h, HEAD_DIM * (1 - h)
        prep[h, 0] = jnp.where(mine, k, jnp.where(lane == spare, bias, 0.0)).astype(bf16)
        prep[h, 1] = jnp.where(mine, v, 1.0).astype(bf16)


def attend(qkv_ref, context_ref, lse_ref, prep, pair, rows, block):
    out = pl.ds(pl.multiple_of(pair * LANES, LANES), LANES)
    q = qkv_ref[rows, out].astype(f32)
    lane = iota((block, LANES), 1)
    low = lane < HEAD_DIM
    sums, tops = [], []
    for h in range(2):
        spare = HEAD_DIM * (1 - h)
        query = jnp.where(lane // HEAD_DIM == h, q, jnp.where(lane == spare, 1.0, 0.0)).astype(bf16)
        scores = dotg(query, prep[h, 0], 1, 1)
        top = jnp.max(scores, axis=1, keepdims=True)
        weights = jnp.exp(scores - top).astype(bf16)
        sums.append(dotg(weights, prep[h, 1], 1, 0))
        tops.append(top)
    num = jnp.where(low, sums[0], sums[1])
    den = pltpu.roll(jnp.where(low, sums[1], sums[0]), HEAD_DIM, 1)
    context_ref[rows, out] = (num / den).astype(bf16)
    total = jnp.where(low, tops[0], tops[1]) + jnp.log(den)
    other = pltpu.roll(total, HEAD_DIM, 1)
    kept = jnp.where(lane == 2 * pair + 1, other, lse_ref[rows, :])
    lse_ref[rows, :] = jnp.where(lane == 2 * pair, total, kept)


def gelu_parts(x):
    cdf = 0.5 * (1.0 + lax.erf(x * (1.0 / math.sqrt(2.0))))
    return cdf, jnp.exp(-0.5 * x * x) * (1.0 / math.sqrt(2.0 * math.pi))


def normalize(values):
    center = values - jnp.mean(values, axis=-1, keepdims=True)
    scale = lax.rsqrt(jnp.mean(center * center, axis=-1, keepdims=True) + eps_norm)
    return center * scale, scale


def gather_plan(shapes):
    plan, every = [("s", ())], slice(None)
    width = shapes["o"][1]
    for a, n in cuts(width, 3, LANES):
        plan += [("q", (every, pl.ds(part * width + a, n))) for part in range(3)]
    for name, parts in (("o", 2), ("u", 6), ("p", 2), ("d", 3)):
        rows, columns = shapes[name]
        for a, n in cuts(columns, parts, LANES):
            for b, m in cuts(rows, 2 if name == "d" else 1, 8):
                plan.append((name, (pl.ds(b, m) if name == "d" else every, pl.ds(a, n))))
    return [(name, sub, GATHER_ORDERS[i % len(GATHER_ORDERS)]) for i, (name, sub) in enumerate(plan)]


def forward_kernel(grid, plan, sizes, *refs):
    (len_ref, tokens_ref, keep_a, keep_f, wq, wo, wu, wd, wp), refs = refs[:9], refs[9:]
    count = len(sizes)
    small_in, refs = refs[:count], refs[count:]
    kept_hbm, (act_t, slope), refs = refs[:16], refs[16:18], refs[18:]
    firsts, small_out, refs = refs[0], refs[1 : 1 + count], refs[1 + count :]
    kept, refs = refs[:16], refs[16:]
    (gq, go, gu, gd, gp, qkv_ref, context, lse, tokens_t, context_t, hidden_t, norm1, scale1, norm2, scale2, layer_out) = kept
    (gs, keep, hidden, hidden_low, act, act_buf, slope_buf, prep, bias), refs = refs[:9], refs[9:]
    send, recv, own_sem, keep_sem, act_sem, slope_sem, out_sem = refs
    length, width = context.shape
    b_qv, b_out, g1, b1, b_up, b_down, g2, b2, b_pool = small_out
    outs = [pltpu.make_async_copy(src, dst, out_sem.at[i]) for i, (src, dst) in enumerate(zip(kept, kept_hbm))]

    def put(*which):
        for i, ref in enumerate(kept):
            if any(ref is w for w in which):
                outs[i].start()

    at = grid.me()
    own = tuple(at[d] for d in DIMS)
    load = pltpu.make_async_copy(keep_a, keep, keep_sem)
    load.start()
    to_own = []
    for i, (src, dst) in enumerate(((wq, gq), (wo, go), (wu, gu), (wd, gd), (wp, gp))):
        to_own.append(pltpu.make_async_copy(src, dst.at[own], own_sem.at[i]))
        to_own[-1].start()
    mine = gs.at[own]
    mine[...] = jnp.zeros(mine.shape, bf16)
    for i, (ref, n) in enumerate(zip(small_in, sizes)):
        mine[i : i + 1, 0:n] = ref[...]
    where = dict(q=gq, o=go, u=gu, d=gd, p=gp, s=gs)
    gather = Gather(grid, [(where[name], sub, order) for name, sub, order in plan], send, recv)
    number = {}
    for i, (name, _, _) in enumerate(plan):
        number.setdefault(name, []).append(i)
    end = {name: [gather.whole[i] for i in numbers] for name, numbers in number.items()}
    grid.barrier(grid.straight())
    for copy in to_own:
        copy.wait()
    gather.begin()
    tokens_t[...] = tokens_ref[...].T
    lse[...] = jnp.zeros_like(lse)
    put(tokens_t)
    gather.until(end["s"][0])
    rows = gs[...].reshape((grid.count,) + gs.shape[-2:])
    for i, (ref, n) in enumerate(zip(small_out, sizes)):
        ref[...] = spread_vector(rows[:, i, :], n)
    bias[:, :width] = b_qv[:, :width]
    bias[:, width : 2 * width] = jnp.zeros((1, width), f32)
    bias[:, 2 * width :] = b_qv[:, width:]

    groups = len(number["q"]) // 3
    part = width // groups
    pairs, block = part // LANES, min(512, length)
    blocks, live = length // block, len_ref[0]
    each = pairs * blocks

    def attention(t):
        @pl.when(t % each == 0)
        def _():
            for j in range(3):
                cols = pl.ds(pl.multiple_of(j * width + t // each * part, part), part)
                out = dotg(tokens_ref[...], gq[:, :, :, :, :, cols].reshape(width, part), 1, 0)
                qkv_ref[:, cols] = (out + bias[:, cols]).astype(bf16)

        @pl.when(t % blocks == 0)
        def _():
            attend_prepare(qkv_ref, prep, live, t // blocks)

        rows = pl.ds(pl.multiple_of((t % blocks) * block, block), block)
        attend(qkv_ref, context, lse, prep, t // blocks, rows, block)

    slots = groups * each
    first, last = end["q"][2], end["u"][len(end["u"]) // 2]
    gather.loop(
        slots,
        [max(end["q"][3 * (t // each) + 2], first + t * (last - first) // slots) for t in range(slots)],
        attention,
    )
    put(gq, qkv_ref, context, lse)

    load.wait()
    block = min(512, length)
    blocks = length // block

    def row_block(t):
        return pl.ds(pl.multiple_of(t * block, block), block)

    gather.until(end["o"][-1])

    def project(t):
        here = row_block(t)
        attended = dotg(context[here, :], go[...].reshape(width, width), 1, 0) + b_out[...]
        total = tokens_ref[here, :].astype(f32) + attended * (keep[here, :].astype(f32) * keep_scale)
        norm, scale = normalize(total)
        out = norm * g1[...] + b1[...]
        hidden[here, :] = out
        hidden_low[here, :] = out.astype(bf16)
        hidden_t[:, here] = out.astype(bf16).T
        context_t[:, here] = context[here, :].T
        norm1[here, :] = norm.astype(bf16)
        scale1[here, :] = jnp.broadcast_to(scale, (block, LANES))

    gather.loop(blocks, [gather.now] * blocks, project)
    load = pltpu.make_async_copy(keep_f, keep, keep_sem)
    load.start()
    put(go, hidden_t, context_t, norm1, scale1)

    parts = len(end["u"])
    step = gu.shape[-1] // parts
    strip = min(128, length)

    def saved(t, cols):
        yield pltpu.make_async_copy(act_buf.at[t % 2], act_t.at[cols, :], act_sem.at[t % 2])
        yield pltpu.make_async_copy(slope_buf.at[t % 2], slope.at[:, cols], slope_sem.at[t % 2])

    def up(t):
        cols = pl.ds(pl.multiple_of(t * step, step), step)
        weight = gu[:, :, :, :, :, cols].reshape(width, step)

        @pl.when(t >= 2)
        def _():
            for copy in saved(t, cols):
                copy.wait()

        for i in range(length // strip):
            here = slice(i * strip, (i + 1) * strip)
            pre = dotg(hidden_low[here, :], weight, 1, 0) + b_up[:, cols]
            cdf, pdf = gelu_parts(pre)
            out = (pre * cdf).astype(bf16)
            act[here, cols] = out
            act_buf[t % 2, :, here] = out.T
            slope_buf[t % 2, here, :] = (cdf + pre * pdf).astype(bf16)
        for copy in saved(t, cols):
            copy.start()

    gather.loop(parts, end["u"], up)
    for t in range(max(0, parts - 2), parts):
        for copy in saved(t, pl.ds(0, step)):
            copy.wait()

    load.wait()
    put(gu)
    halves = len(cuts(gd.shape[-2], 2, 8))
    ends = end["d"][halves - 1 :: halves]
    parts = len(ends)
    step = width // parts

    def down(t):
        cols = pl.ds(pl.multiple_of(t * step, step), step)
        out = dotg(act[...], gd[:, :, :, :, :, cols].reshape(-1, step), 1, 0) + b_down[:, cols]
        hidden[:, cols] += out * (keep[:, cols].astype(f32) * keep_scale)

    gather.loop(parts, ends, down)
    put(gd, gp)
    block = min(256, length)
    blocks = length // block

    def norm(t):
        here = row_block(t)
        value, scale = normalize(hidden[here, :])
        out = value * g2[...] + b2[...]
        norm2[here, :] = value.astype(bf16)
        scale2[here, :] = jnp.broadcast_to(scale, (block, LANES))
        layer_out[here, :] = out.astype(bf16)

        @pl.when(t == 0)
        def _():
            first = out[0:8].astype(bf16)
            pooled = jnp.tanh(dotg(first, gp[...].reshape(width, width), 1, 0) + b_pool[...])
            firsts[0:1, :] = pooled[0:1]
            firsts[1:2, :] = first[0:1].astype(f32)

    gather.loop(blocks, [gather.now] * blocks, norm)
    put(norm2, scale2, layer_out)
    gather.finish()
    for copy in outs:
        copy.wait()


def run_forward(grid, length_of, tokens, keep_a, keep_f, big, small):
    length, width = tokens.shape
    names = ("q", "o", "u", "d", "p")
    shapes = {k: w.shape for k, w in zip(names, big)}
    inner = shapes["u"][1]
    sizes = [v.shape[0] for v in small]
    plan = gather_plan(shapes)
    pad = -(-max(sizes) // LANES) * LANES
    step = inner // sum(p[0] == "u" for p in plan)
    vmem, anywhere = pl.BlockSpec(memory_space=pltpu.VMEM), pl.BlockSpec(memory_space=pl.ANY)
    shape = jax.ShapeDtypeStruct
    kept = [(grid.shape + shapes[k], bf16) for k in names] + [
        ((length, 3 * width), bf16),
        ((length, width), bf16),
        ((length, LANES), f32),
        ((width, length), bf16),
        ((width, length), bf16),
        ((width, length), bf16),
        ((length, width), bf16),
        ((length, LANES), f32),
        ((length, width), bf16),
        ((length, LANES), f32),
        ((length, width), bf16),
    ]
    return pl.pallas_call(
        functools.partial(forward_kernel, grid, plan, sizes),
        out_shape=[shape(*k) for k in kept]
        + [shape((inner, length), bf16), shape((length, inner), bf16), shape((2, width), f32)]
        + [shape((1, grid.count * n), f32) for n in sizes],
        in_specs=[pl.BlockSpec(memory_space=pltpu.SMEM), vmem, anywhere, anywhere] + [vmem] * (5 + len(small)),
        out_specs=[anywhere] * 18 + [vmem] * (1 + len(small)),
        scratch_shapes=[pltpu.VMEM(*k) for k in kept]
        + [
            pltpu.VMEM(grid.shape + (16, pad), bf16),
            pltpu.VMEM((length, width), jnp.int32),
            pltpu.VMEM((length, width), f32),
            pltpu.VMEM((length, width), bf16),
            pltpu.VMEM((length, inner), bf16),
            pltpu.VMEM((2, step, length), bf16),
            pltpu.VMEM((2, length, step), bf16),
            pltpu.VMEM((2, 2, length, LANES), bf16),
            pltpu.VMEM((1, 3 * width), f32),
            pltpu.SemaphoreType.DMA((len(plan), grid.slots)),
            pltpu.SemaphoreType.DMA((len(plan), grid.slots)),
            pltpu.SemaphoreType.DMA((5,)),
            pltpu.SemaphoreType.DMA,
            pltpu.SemaphoreType.DMA((2,)),
            pltpu.SemaphoreType.DMA((2,)),
            pltpu.SemaphoreType.DMA((16,)),
        ],
        compiler_params=pltpu.CompilerParams(
            collective_id=0, has_side_effects=True, vmem_limit_bytes=VMEM_LIMIT
        ),
        name="forward",
    )(length_of, tokens, keep_a, keep_f, *big, *[v.reshape(1, -1) for v in small])


def pool_and_loss(views, partners_ref, wp, here, shard_rows, unit_ref, work, cls_grad, pool_w, pool_b, loss):
    high = lax.Precision.HIGHEST
    count, width = math.prod(views.shape[:4]), views.shape[-1]
    each = count // views.shape[0]

    def pooled_rows(z):
        rows = views[z].reshape((each,) + views.shape[-2:])
        pooled = rows[:, 0, :]
        scale = lax.rsqrt(jnp.sum(pooled * pooled, axis=1, keepdims=True) + 1e-06)
        return slice(z * each, (z + 1) * each), pooled, scale, rows[:, 1, :]

    for z in range(views.shape[0]):
        at, pooled, scale, cls = pooled_rows(z)
        unit_ref[at, :] = pooled * scale
        work[count + z * each : count + (z + 1) * each, :] = cls.astype(bf16)
    unit = unit_ref[0:count, :]
    sims = dotg(unit, unit, 1, 1, high) / logit_divisor
    column, row = iota((count, count), 1), iota((count, count), 0)
    others = jnp.where(row == column, neg_fill, sims)
    top = jnp.max(others, axis=1, keepdims=True)
    weights = jnp.exp(others - top)
    total = jnp.sum(weights, axis=1, keepdims=True)
    partner = column == partners_ref[...]
    target = jnp.sum(jnp.where(partner, sims, 0.0), axis=1, keepdims=True)
    lost = jnp.sum(top + jnp.log(total) - target, axis=0, keepdims=True) / count
    loss[...] = jnp.broadcast_to(lost, loss.shape)
    pull = weights / total - jnp.where(partner, 1.0, 0.0)
    pull = pull + dotg(pull, (row == column).astype(f32), 0, 0, high)
    for z in range(views.shape[0]):
        at, pooled, scale, _ = pooled_rows(z)
        unit_grad = dotg(pull[at], unit, 1, 0, high) / logit_divisor
        along = jnp.sum(pooled * unit_grad, axis=1, keepdims=True)
        pooled_grad = scale * unit_grad - pooled * (scale * scale * scale * along)
        work[at, :] = (pooled_grad * (1.0 - pooled * pooled)).astype(bf16)
    pre, cls = work[0:count, :], work[count : 2 * count, :]
    mine = jnp.sum(jnp.where(iota((count, width), 0) == here, pre.astype(f32), 0.0), axis=0, keepdims=True)
    cls_grad[...] = dotg(jnp.broadcast_to(mine, (8, width)).astype(bf16), wp, 1, 1)
    place = (iota((width, LANES), 0) == here * shard_rows + iota((width, LANES), 1)).astype(f32).astype(bf16)
    cls_rows = dotg(cls, place, 1, 0).astype(bf16)
    pool_w[...] = dotg(cls_rows, pre, 0, 0)[:shard_rows]
    sums = jnp.broadcast_to(jnp.sum(pre.astype(f32), axis=0, keepdims=True), (8, width))
    pool_b[...] = sum(dotg(part.astype(bf16), place, 1, 0) for part in three_parts(sums))


def attend_back(qkv_ref, context, dcontext, lse, live, pair, prep):
    length, width = qkv_ref.shape[0], context.shape[1]
    scale = 1.0 / math.sqrt(HEAD_DIM)
    one = pl.ds(pl.multiple_of(pair * LANES, LANES), LANES)

    def col(part):
        return pl.ds(pl.multiple_of(part * width + pair * LANES, LANES), LANES)

    q, k, v = (qkv_ref[:, col(j)].astype(f32) for j in range(3))
    d = dcontext[:, one].astype(f32)
    lane, row = iota((length, LANES), 1), iota((length, LANES), 0)
    bias = jnp.where(row < live, 0.0, neg_fill)
    both = d * context[:, one].astype(f32)
    for h in range(2):
        mine, a = lane // HEAD_DIM == h, HEAD_DIM * (1 - h)
        inner = jnp.sum(jnp.where(mine, both, 0.0), axis=1, keepdims=True)
        total = jnp.sum(jnp.where(lane == 2 * pair + h, lse[...], 0.0), axis=1, keepdims=True)
        l0, l1, l2 = three_parts(-total)
        d0, d1, d2 = three_parts(-inner)

        def lanes(base, *extra):
            out = 0.0
            for j, e in reversed(list(enumerate(extra))):
                out = jnp.where(lane == a + j, e, out)
            return jnp.where(mine, base, out).astype(bf16)

        prep[h, 0] = lanes(q * scale, 1.0, l0, l1, l2)
        prep[h, 1] = lanes(k, bias, 1.0, 1.0, 1.0)
        prep[h, 2] = lanes(d, d0, d1, d2)
        prep[h, 3] = lanes(v, 1.0, 1.0, 1.0)
        prep[h, 4] = lanes(k * scale)
    return (q * scale).astype(bf16).T, d.astype(bf16).T


def scatter_plan(grid, shapes):
    plan, every = [], slice(None)
    width = shapes["o"][1]
    rows, columns = shapes["d"]
    plan += [("d", (pl.ds(a, n), every), n, columns) for a, n in cuts(rows, 6, 8)]
    for name, parts in (("u", 6), ("o", 2)):
        rows, columns = shapes[name]
        plan += [(name, (every, pl.ds(a, n)), rows, n) for a, n in cuts(columns, parts, LANES)]
    for a, n in cuts(width, 3, LANES):
        plan += [("q", (every, pl.ds(part * width + a, n)), shapes["q"][0], n) for part in range(3)]
    plan.append(("s", (), 16, shapes["s"]))
    return [(p[0], p[1], SCATTER_ORDERS[i % 2]) + p[2:] for i, p in enumerate(plan)]


def backward_kernel(grid, whole, plan, sizes, shard_rows, *refs):
    (len_ref, partners_ref, firsts, g1, g2), refs = refs[:5], refs[5:]
    (h_cot, h_keep_a, h_keep_f, h_norm1, h_scale1, h_norm2, h_scale2, h_act, h_slope, h_hidden, h_context_t), refs = refs[:11], refs[11:]
    (h_qkv, h_context, h_lse, h_tokens, h_wq, h_wo, h_wu, h_wd, h_wp), refs = refs[:9], refs[9:]
    (rq, ro, ru, rd, rs, pool_w, pool_b, loss, h_tokens_grad), refs = refs[:9], refs[9:]
    (dd, du, do, dsmall, grad, gctx, low, norm, keep, scale, vec, cls_grad, views, wp), refs = refs[:14], refs[14:]
    (send, recv, view_send, view_recv, sems, pair_sems), bufs = refs[:6], list(refs[6:])
    length, width = grad.shape
    inner = vec.shape[1]
    sources, results = dict(d=dd, u=du, o=do, s=dsmall), dict(d=rd, u=ru, o=ro, q=rq, s=rs)
    number = {}
    for i, p in enumerate(plan):
        number.setdefault(p[0], []).append(i)
    cot = low

    def copy(k, src, dst):
        return pltpu.make_async_copy(src, dst, sems.at[k])

    first_loads = [copy(0, h_cot, cot), copy(1, h_norm2, norm), copy(2, h_scale2, scale), copy(3, h_keep_f, keep), copy(4, h_wp, wp)]
    for c in first_loads:
        c.start()
    at_all = whole.me()
    views[tuple(at_all[d] for d in DIMS)] = firsts[...]
    exchange = Exchange(whole, views, view_send, view_recv)
    whole.barrier(whole.straight() + [o for o in whole.around(("z", "c")) + whole.around(("y", "x")) if len(o) > 1])
    exchange.start(0)
    vec[...] = jnp.zeros_like(vec)
    for c in first_loads:
        c.wait()
    strip = min(128, length)
    strips = length // strip

    def strip_of(t):
        return pl.ds(pl.multiple_of(t * strip, strip), strip)

    def add_row(j, x):
        vec[j : j + 1, : x.shape[1]] += jnp.sum(x, axis=0, keepdims=True)

    def norm_back(here, up, gain, slot):
        value = norm[here, :].astype(f32)
        scaled = up * gain[...]
        along = jnp.mean(scaled * value, axis=1, keepdims=True)
        back = scale[here, 0:1] * (scaled - jnp.mean(scaled, axis=1, keepdims=True) - value * along)
        add_row(slot, up * value)
        add_row(slot + 1, up)
        grad[here, :] = back
        out = (back * (keep[here, :].astype(f32) * keep_scale)).astype(bf16)
        low[here, :] = out
        return out.astype(f32)

    def second_norm(t, extra):
        here = strip_of(t)
        up = cot[here, :].astype(f32)
        if extra is not None:
            up = up + jnp.where(iota((strip, width), 0) + t * strip == 0, extra, 0.0)
        add_row(5, norm_back(here, up, g2, 6))
        return 0

    held = -(-math.prod(whole.shape) // strip)
    lax.fori_loop(held, strips, lambda t, _: second_norm(t, None), 0)
    exchange.wait(0)
    exchange.start(1)
    exchange.wait(1)
    here = lax.axis_index("dp") * (whole.size["y"] * whole.size["x"]) + lax.axis_index("fsdp")
    pool_and_loss(views, partners_ref, wp[...], here, shard_rows, grad, gctx, cls_grad, pool_w, pool_b, loss)
    lax.fori_loop(0, held, lambda t, _: second_norm(t, cls_grad[0:1, :]), 0)
    wo = wp
    second_loads = [copy(1, h_norm1, norm), copy(2, h_scale1, scale), copy(3, h_keep_a, keep), copy(6, h_wo, wo)]
    for c in second_loads:
        c.start()

    pieces, left = [], bufs
    for name, sub, order, _, _ in plan:
        n = len(grid.order(order))
        pieces.append([sources.get(name), sub, order, left[:n], results[name].at[sub] if sub else results[name]])
        left = left[n:]
    scatter = Scatter(grid, pieces, send, recv)

    def feed_forward(act, slope, wd, wu, gup, turned):
        third = [copy(5, h_hidden, turned), copy(7, h_context_t, turned)]
        third[0].start()
        block = min(256, length)
        chunk, part = act.shape[1], slope.shape[2]
        chunks, parts = inner // chunk, inner // part
        slab = wu.shape[1]

        def act_load(t):
            return pltpu.make_async_copy(h_act.at[pl.ds(pl.multiple_of(t * chunk, chunk), chunk), :], act.at[t % 2], pair_sems.at[0, t % 2])

        def part_loads(t):
            cols = pl.ds(pl.multiple_of(t * part, part), part)
            yield pltpu.make_async_copy(h_slope.at[:, cols], slope.at[t % 2], pair_sems.at[1, t % 2])
            yield pltpu.make_async_copy(h_wd.at[cols, :], wd.at[t % 2], pair_sems.at[2, t % 2])

        def slab_load(t):
            return pltpu.make_async_copy(h_wu.at[pl.ds(pl.multiple_of(t * slab, slab), slab), :], wu.at[t % 2], pair_sems.at[3, t % 2])

        act_load(0).start()
        for c in part_loads(0):
            c.start()
        slab_load(0).start()
        across = grid.size["y"] * grid.size["x"]

        def down_weight(t, _):
            @pl.when(t + 1 < chunks)
            def _():
                act_load(t + 1).start()

            act_load(t).wait()
            out = dotg(act[t % 2], low[...], 1, 0).astype(bf16)
            dd[t // grid.size["c"], t % grid.size["c"]] = out.reshape(dd.shape[2:])
            return 0

        lax.fori_loop(0, chunks, down_weight, 0)
        for i in number["d"]:
            scatter.begin(i)
        third[0].wait()

        def up_part(t, _):
            cols = pl.ds(pl.multiple_of(t * part, part), part)

            @pl.when(t + 1 < parts)
            def _():
                for c in part_loads(t + 1):
                    c.start()

            for c in part_loads(t):
                c.wait()
            for i in range(length // block):
                rows = slice(i * block, (i + 1) * block)
                out = dotg(low[rows, :], wd[t % 2], 1, 1) * slope[t % 2, rows, :].astype(f32)
                gup[rows, cols] = out.astype(bf16)
            vec[4:5, cols] = jnp.sum(gup[:, cols].astype(f32), axis=0, keepdims=True)
            out = dotg(turned[...], gup[:, cols], 1, 0).astype(bf16)
            du[:, :, :, :, :, cols] = out.reshape(grid.shape + (-1, part))
            for k, i in enumerate(number["u"]):

                @pl.when(t == k)
                def _():
                    scatter.begin(i)
                    scatter.run(k, k + 1)

            return 0

        lax.fori_loop(0, parts, up_part, 0)
        third[1].start()

        def hidden_part(t, _):
            cols = pl.ds(pl.multiple_of(t * slab, slab), slab)

            @pl.when(t + 1 < width // slab)
            def _():
                slab_load(t + 1).start()

            slab_load(t).wait()
            grad[:, cols] += dotg(gup[...], wu[t % 2], 1, 1)
            for k in range(width // slab):

                @pl.when(t == k)
                def _():
                    scatter.run(parts + k, parts + k + 1)

            return 0

        lax.fori_loop(0, width // slab, hidden_part, 0)
        for c in second_loads:
            c.wait()

        def first_norm(t, _):
            add_row(1, norm_back(strip_of(t), grad[strip_of(t), :], g1, 2))
            return 0

        lax.fori_loop(0, strips, first_norm, 0)
        third[1].wait()
        for i in number["o"]:
            cols = plan[i][1][1]
            out = dotg(turned[...], low[:, cols], 1, 0).astype(bf16)
            do[:, :, :, :, :, cols] = out.reshape(grid.shape + (-1, cols.size))
            scatter.begin(i)
        for i in range(length // block):
            rows = slice(i * block, (i + 1) * block)
            gctx[rows, :] = dotg(low[rows, :], wo[...], 1, 1).astype(bf16)
        scatter.run(parts + width // slab, parts + width // slab + 1)
        return parts + width // slab + 1

    chunk, part, slab = inner // (grid.size["z"] * grid.size["c"]), inner // len(number["u"]), width // 3
    done = []

    def first_scope(*refs):
        done.append(feed_forward(*refs))

    pl.run_scoped(
        first_scope,
        pltpu.VMEM((2, chunk, length), bf16),
        pltpu.VMEM((2, length, part), bf16),
        pltpu.VMEM((2, part, width), bf16),
        pltpu.VMEM((2, slab, inner), bf16),
        pltpu.VMEM((length, inner), bf16),
        pltpu.VMEM((width, length), bf16),
    )
    step = done[0]

    def attention(qkv, lse, tokens_t, wq, dq, prep, turned, acc):
        context = norm
        block = min(256, length) if grid.with_fsdp else min(128, length)
        blocks = length // block

        def rows_of(t):
            return pl.ds(pl.multiple_of(t * block, block), block)

        for i in number["q"]:
            scatter.pieces[i] = (dq,) + scatter.pieces[i][1:]
        loads = [copy(8, h_qkv, qkv), copy(9, h_context, context), copy(10, h_lse, lse), copy(11, h_tokens, tokens_t), copy(12, h_wq.at[:, 0:width], wp), copy(6, h_wq.at[:, width : 2 * width], wq.at[0]), copy(7, h_wq.at[:, 2 * width :], wq.at[1])]
        for c in loads:
            c.start()
        for c in loads[:3]:
            c.wait()
        groups = len(number["q"]) // 3
        span = width // groups
        each = span // LANES * blocks
        slots = groups * each
        live = len_ref[0]
        head = [slice(h * HEAD_DIM, (h + 1) * HEAD_DIM) for h in range(2)]
        marks = []
        for g in range(groups):
            lo, hi = (step if g == 0 else number["q"][3 * g - 3]), number["q"][3 * g]
            marks += [(lo + j * (hi - lo) // each, lo + (j + 1) * (hi - lo) // each) for j in range(each)]

        def slot(t, _):
            pair, b = t // blocks, t % blocks
            rows = rows_of(b)
            one = pl.ds(pl.multiple_of(pair * LANES, LANES), LANES)

            @pl.when(b == 0)
            def _():
                turned[0], turned[1] = attend_back(qkv, context, gctx, lse, live, pair, prep)
                acc[...] = jnp.zeros_like(acc)

            dq_rows = jnp.zeros((block, LANES), f32)
            for h in range(2):
                p = jnp.exp(dotg(prep[h, 0, rows, :], prep[h, 1], 1, 1))
                dp = dotg(prep[h, 2, rows, :], prep[h, 3], 1, 1)
                ds = (p * dp).astype(bf16)
                acc[0, head[h], :] += dotg(turned[1, head[h], rows], p.astype(bf16), 1, 0)
                acc[1, head[h], :] += dotg(turned[0, head[h], rows], ds, 1, 0)
                dq_rows = dq_rows + dotg(ds, prep[h, 4], 1, 0)
            qkv[rows, one] = dq_rows.astype(bf16)

            @pl.when(b == blocks - 1)
            def _():
                qkv[:, pl.ds(pl.multiple_of(width + pair * LANES, LANES), LANES)] = acc[1].astype(bf16).T
                qkv[:, pl.ds(pl.multiple_of(2 * width + pair * LANES, LANES), LANES)] = acc[0].astype(bf16).T

            for k in range(slots):
                if marks[k][1] > marks[k][0]:

                    @pl.when(t == k)
                    def _():
                        scatter.run(*marks[k])

            @pl.when(t == each - 1)
            def _():
                loads[3].wait()

            @pl.when(t % each == each - 1)
            def _():
                for j in range(3):
                    cols = pl.ds(pl.multiple_of(j * width + t // each * span, LANES), span)
                    out = dotg(tokens_t[...], qkv[:, cols], 1, 0).astype(bf16)
                    dq[:, :, :, :, :, cols] = out.reshape(grid.shape + (-1, span))
                for g in range(groups):

                    @pl.when(t == each * (g + 1) - 1)
                    def _():
                        for i in number["q"][3 * g : 3 * g + 3]:
                            scatter.begin(i)

            return 0

        lax.fori_loop(0, slots, slot, 0)
        sums = dotg(jnp.ones((8, length), bf16), qkv[...], 1, 0)[0:1]
        vec[0:1, :width] = sums[:, :width]
        vec[0:1, width : 2 * width] = sums[:, 2 * width :]
        pad = dsmall.shape[-1]
        dsmall[...] = jnp.zeros_like(dsmall)
        for j, n in enumerate(sizes):
            folded = fold_vector(vec[j : j + 1, : grid.count * n], grid.count, n, pad)
            dsmall[:, :, :, :, j, :] = folded.reshape(grid.shape + (pad,))
        scatter.begin(number["s"][0])
        at_step = number["q"][-3]
        for c in loads[4:]:
            c.wait()
        rest, parts = scatter.steps - at_step, 4
        rows = length // parts
        for i in range(parts):
            scatter.run(at_step + i * rest // parts, at_step + (i + 1) * rest // parts)
            here = slice(i * rows, (i + 1) * rows)
            total = grad[here, :] + dotg(qkv[here, :width], wp[...], 1, 1)
            for j in range(2):
                total = total + dotg(qkv[here, (j + 1) * width : (j + 2) * width], wq[j], 1, 1)
            low[here, :] = total.astype(bf16)
        out = copy(13, low, h_tokens_grad)
        out.start()
        scatter.finish()
        exchange.finish()
        out.wait()

    pl.run_scoped(
        attention,
        pltpu.VMEM((length, 3 * width), bf16),
        pltpu.VMEM((length, LANES), f32),
        pltpu.VMEM((width, length), bf16),
        pltpu.VMEM((2, width, width), bf16),
        pltpu.VMEM(grid.shape + (width // grid.count, 3 * width), bf16),
        pltpu.VMEM((2, 5, length, LANES), bf16),
        pltpu.VMEM((2, LANES, length), bf16),
        pltpu.VMEM((2, LANES, length), f32),
    )


def run_backward(grid, whole, length_of, partners, firsts, gains, hbm, length, width, inner, sizes, shard_rows):
    rows = width // grid.count
    pad = -(-max(sizes) // LANES) * LANES
    shapes = {"q": (rows, 3 * width), "o": (rows, width), "u": (rows, inner), "d": (inner // grid.count, width), "s": pad}
    plan = scatter_plan(grid, shapes)
    bufs = []
    for name, _, order, r, c in plan:
        bufs += scatter_buffers(grid, order, r, c, f32 if name == "s" else bf16)
    views_count = len(whole.around(("z", "c"))) + len(whole.around(("y", "x")))
    vmem, anywhere = pl.BlockSpec(memory_space=pltpu.VMEM), pl.BlockSpec(memory_space=pl.ANY)
    shape = jax.ShapeDtypeStruct
    return pl.pallas_call(
        functools.partial(backward_kernel, grid, whole, plan, sizes, shard_rows),
        out_shape=[shape(shapes[k], f32) for k in ("q", "o", "u", "d")]
        + [
            shape((16, pad), f32),
            shape((shard_rows, width), f32),
            shape((8, LANES), f32),
            shape((8, LANES), f32),
            shape((length, width), bf16),
        ],
        in_specs=[pl.BlockSpec(memory_space=pltpu.SMEM)] + [vmem] * 4 + [anywhere] * len(hbm),
        out_specs=[vmem] * 8 + [anywhere],
        scratch_shapes=[pltpu.VMEM(grid.shape + shapes[k], bf16) for k in ("d", "u", "o")]
        + [
            pltpu.VMEM(grid.shape + (16, pad), f32),
            pltpu.VMEM((length, width), f32),
            pltpu.VMEM((length, width), bf16),
            pltpu.VMEM((length, width), bf16),
            pltpu.VMEM((length, width), bf16),
            pltpu.VMEM((length, width), jnp.int32),
            pltpu.VMEM((length, LANES), f32),
            pltpu.VMEM((16, inner), f32),
            pltpu.VMEM((8, width), f32),
            pltpu.VMEM(whole.shape + (2, width), f32),
            pltpu.VMEM((width, width), bf16),
            pltpu.SemaphoreType.DMA((len(plan), grid.slots)),
            pltpu.SemaphoreType.DMA((len(plan), grid.slots)),
            pltpu.SemaphoreType.DMA((views_count,)),
            pltpu.SemaphoreType.DMA((views_count,)),
            pltpu.SemaphoreType.DMA((14,)),
            pltpu.SemaphoreType.DMA((4, 2)),
        ]
        + bufs,
        compiler_params=pltpu.CompilerParams(
            collective_id=1, has_side_effects=True, vmem_limit_bytes=VMEM_LIMIT
        ),
        name="backward",
    )(length_of, partners.reshape(-1, 1), firsts, *gains, *hbm)


def on_device(whole, grid, tokens, lengths, keep_attn, keep_ffn, partners, out_cot, *weights):
    (w_qkv, b_qv, w_out, b_out, ln1_gain, ln1_bias, w_up, b_up, w_down, b_down, ln2_gain, ln2_bias, w_pool, b_pool) = weights
    _, length, width = tokens.shape
    inner = w_up.shape[1]
    big = [w_qkv, w_out, w_up, w_down, w_pool]
    small = [b_qv, b_out, ln1_gain, ln1_bias, b_up, b_down, ln2_gain, ln2_bias, b_pool]
    shard_rows = w_qkv.shape[0]
    if not grid.with_fsdp:
        big = [lax.all_gather(w, "fsdp", axis=0, tiled=True) for w in big]
        small = [lax.all_gather(v, "fsdp", axis=0, tiled=True) for v in small]
    sizes = [v.shape[0] for v in small][:-1]
    flat = (length, width)
    keep_a, keep_f = keep_attn.reshape(flat), keep_ffn.reshape(flat)
    outs = run_forward(grid, lengths, tokens.reshape(flat), keep_a, keep_f, big, small)
    wq, wo, wu, wd, wp = (g.reshape(-1, g.shape[-1]) for g in outs[:5])
    qkv, context, lse, tokens_t, context_t, hidden_t, norm1, scale1, norm2, scale2, layer_out = outs[5:16]
    act_t, slope, firsts = outs[16:19]
    vectors = outs[19:]
    hbm = [
        out_cot.reshape(flat), keep_a, keep_f, norm1, scale1, norm2, scale2, act_t, slope, hidden_t, context_t,
        qkv, context, lse, tokens_t, wq, wo, wu, wd, wp,
    ]
    rq, ro, ru, rd, rs, pool_w, pool_b, loss, tokens_grad = run_backward(
        grid, whole, lengths, partners, firsts, [vectors[2], vectors[6]], hbm, length, width, inner, sizes, shard_rows
    )
    owned = [rq, ro, ru, rd] + [rs[j, :n] for j, n in enumerate(sizes)]
    if not grid.with_fsdp:
        owned = [lax.psum_scatter(g, "fsdp", scatter_dimension=0, tiled=True) for g in owned]
    rq, ro, ru, rd, s_qv, s_out, s_g1, s_b1, s_up, s_down, s_g2, s_b2 = owned
    return (
        layer_out.reshape(tokens.shape), tokens_grad.reshape(tokens.shape), rq, s_qv, ro, s_out, s_g1, s_b1, ru, s_up,
        rd, s_down, s_g2, s_b2, pool_w, pool_b[0, :shard_rows], loss[0, 0],
    )


def solution(mesh):
    rows, vector, matrix = P(AXES, None, None), P(AXES), P(AXES, None)
    weights = (matrix, vector, matrix, vector, vector, vector, matrix, vector, matrix, vector, vector, vector, matrix, vector)
    devices = mesh.shape["dp"] * mesh.shape["fsdp"]

    def step(*args):
        whole = Grid(mesh)
        grid = whole if (args[6].shape[0] // devices) % 8 == 0 else Grid(mesh, False)
        return jax.shard_map(
            functools.partial(on_device, whole, grid),
            mesh=mesh,
            in_specs=(rows, vector, rows, rows, P(), rows) + weights,
            out_specs=(rows, rows) + weights + (P(),),
            check_vma=False,
        )(*args)

    return step
```

```python
import functools
import math

import jax
import jax.numpy as jnp
from jax import lax
from jax.experimental import pallas as pl
from jax.experimental.pallas import tpu as pltpu
from jax.sharding import PartitionSpec as P

HEAD_DIM = 64
LANES = 128
f32, bf16 = jnp.float32, jnp.bfloat16
MESH = pl.DeviceIdType.MESH
AXES = ("dp", "fsdp")
eps_norm = 1e-05
keep_scale = 1.0 / 0.9
logit_divisor = 0.05
neg_fill = -1000000000.0
VMEM_LIMIT = 67043328
DIMS = ("z", "c", "y", "x")
SPACING = 4
GATHER_ORDERS = (
    ("z", "x", "y", "c"),
    ("x", "z", "y", "c"),
    ("z", "y", "x", "c"),
    ("z", "y", "x", "c"),
    ("y", "z", "x", "c"),
    ("z", "x", "y", "c"),
)
SCATTER_ORDERS = (("c", "y", "x", "z"), ("c", "x", "y", "z"))


class Grid:
    def __init__(self, mesh, with_fsdp=True):
        dp, fsdp = mesh.shape["dp"], mesh.shape["fsdp"]
        cores = 2 if dp % 2 == 0 else 1
        side = math.isqrt(fsdp)
        if side * side != fsdp:
            side = fsdp
        self.with_fsdp = with_fsdp
        self.size = {
            "z": dp // cores,
            "c": cores,
            "y": fsdp // side if with_fsdp else 1,
            "x": side if with_fsdp else 1,
        }
        self.shape = tuple(self.size[d] for d in DIMS)
        self.count = math.prod(self.shape)
        self.slots = sum(n - 1 for n in self.shape)

    def me(self):
        dp, fsdp = lax.axis_index("dp"), lax.axis_index("fsdp")
        at = {"z": lax.div(dp, self.size["c"]), "c": lax.rem(dp, self.size["c"])}
        if self.with_fsdp:
            at["y"], at["x"] = lax.div(fsdp, self.size["x"]), lax.rem(fsdp, self.size["x"])
        else:
            at["y"], at["x"] = 0, 0
        return at

    def device(self, at):
        fsdp = at["y"] * self.size["x"] + at["x"] if self.with_fsdp else lax.axis_index("fsdp")
        return (at["z"] * self.size["c"] + at["c"], fsdp)

    def peer(self, at, dim, j):
        other = dict(at)
        other[dim] = lax.rem(at[dim] + j, self.size[dim])
        return other

    def slot(self, dim, j):
        base = 0
        for d in DIMS:
            if d == dim:
                return base + j - 1
            base += self.size[d] - 1

    def order(self, order):
        return tuple(d for d in order if self.size[d] > 1)

    def straight(self):
        return [{d: j} for d in DIMS for j in range(1, self.size[d])]

    def around(self, dims):
        offsets = [{}]
        for d in dims:
            offsets = [{**o, d: j} if j else o for o in offsets for j in range(self.size[d])]
        return [o for o in offsets if o]

    def moved(self, at, offset):
        return {d: lax.rem(at[d] + offset[d], self.size[d]) if d in offset else at[d] for d in DIMS}

    def barrier(self, offsets):
        at, sem = self.me(), pltpu.get_barrier_semaphore()
        for offset in offsets:
            pl.semaphore_signal(
                sem, inc=1, device_id=self.device(self.moved(at, offset)), device_id_type=MESH
            )
        pl.semaphore_wait(sem, len(offsets))


class Exchange:
    def __init__(self, grid, ref, send, recv):
        self.grid, self.ref, self.send, self.recv, self.at = grid, ref, send, recv, grid.me()
        self.groups = [("z", "c"), ("y", "x")]

    def copies(self, stage):
        done = self.groups[0] if stage else ()
        view = self.ref.at[tuple(slice(None) if d in done else self.at[d] for d in DIMS)]
        first = len(self.grid.around(self.groups[0])) if stage else 0
        for j, offset in enumerate(self.grid.around(self.groups[stage])):
            yield pltpu.make_async_remote_copy(
                src_ref=view,
                dst_ref=view,
                send_sem=self.send.at[first + j],
                recv_sem=self.recv.at[first + j],
                device_id=self.grid.device(self.grid.moved(self.at, offset)),
                device_id_type=MESH,
            )

    def start(self, stage):
        for copy in self.copies(stage):
            copy.start()

    def wait(self, stage):
        for copy in self.copies(stage):
            copy.wait_recv()

    def finish(self):
        for stage in range(2):
            for copy in self.copies(stage):
                copy.wait_send()


class Gather:
    def __init__(self, grid, pieces, send, recv, window=3, lag=3):
        self.grid, self.send, self.recv, self.at = grid, send, recv, grid.me()
        self.pieces = [(ref, sub, grid.order(order)) for ref, sub, order in pieces]
        self.stages, self.window, self.now = len(self.pieces[0][2]), window, 0
        self.events = [
            (step - stage * lag, stage)
            for step in range(len(pieces) + (self.stages - 1) * lag)
            for stage in range(self.stages)
            if 0 <= step - stage * lag < len(pieces)
        ]
        self.whole = [self.events.index((i, self.stages - 1)) + 1 for i in range(len(pieces))]

    def copies(self, i, stage):
        ref, sub, order = self.pieces[i]
        dim, done = order[stage], order[:stage]
        index = tuple(slice(None) if d in done else self.at[d] for d in DIMS)
        view = ref.at[index + sub]
        for j in range(1, self.grid.size[dim]):
            slot = self.grid.slot(dim, j)
            yield pltpu.make_async_remote_copy(
                src_ref=view,
                dst_ref=view,
                send_sem=self.send.at[i, slot],
                recv_sem=self.recv.at[i, slot],
                device_id=self.grid.device(self.grid.peer(self.at, dim, j)),
                device_id_type=MESH,
            )

    def start(self, i, stage):
        for copy in self.copies(i, stage):
            copy.start()

    def begin(self):
        for i in range(min(self.window, len(self.pieces))):
            self.start(i, 0)

    def run(self, first, last):
        for i, stage in self.events[first:last]:
            for copy in self.copies(i, stage):
                copy.wait_recv()
            if stage == 0 and i + self.window < len(self.pieces):
                self.start(i + self.window, 0)
            if stage < self.stages - 1:
                self.start(i, stage + 1)

    def until(self, last):
        self.run(self.now, max(self.now, last))
        self.now = max(self.now, last)

    def finish(self):
        self.until(len(self.events))
        for i in range(len(self.pieces)):
            for stage in range(self.stages):
                for copy in self.copies(i, stage):
                    copy.wait_send()

    def loop(self, count, marks, body):
        marks = [max(self.now, m) for m in marks]
        starts = [self.now] + marks[:-1]

        def step(t, _):
            for k in range(count):
                if marks[k] > starts[k]:

                    @pl.when(t == k)
                    def _():
                        self.run(starts[k], marks[k])

            body(t)
            return 0

        lax.fori_loop(0, count, step, 0)
        self.now = marks[-1]


class Scatter:
    def __init__(self, grid, pieces, send, recv):
        self.grid, self.send, self.recv, self.at = grid, send, recv, grid.me()
        self.pieces = [(src, sub, grid.order(order), bufs, out) for src, sub, order, bufs, out in pieces]
        self.stages = len(self.pieces[0][2])

    def pick(self, i, stage, where):
        src, sub, order, bufs, _ = self.pieces[i]
        left = tuple(d for d in DIMS if d not in order[:stage])
        index = tuple(where if d == order[stage] else slice(None) for d in left)
        if stage == 0:
            return src.at[index + sub]
        return bufs[stage - 1].at[(0,) + index]

    def copies(self, i, stage):
        _, _, order, bufs, _ = self.pieces[i]
        dim = order[stage]
        for j in range(1, self.grid.size[dim]):
            other = self.grid.peer(self.at, dim, j)
            slot = self.grid.slot(dim, j)
            yield pltpu.make_async_remote_copy(
                src_ref=self.pick(i, stage, other[dim]),
                dst_ref=bufs[stage].at[j - 1],
                send_sem=self.send.at[i, slot],
                recv_sem=self.recv.at[i, slot],
                device_id=self.grid.device(other),
                device_id_type=MESH,
            )

    def begin(self, i):
        for copy in self.copies(i, 0):
            copy.start()

    def run(self, events):
        for i, stage in events:
            self.add(i, stage)
            if stage < self.stages - 1:
                for copy in self.copies(i, stage + 1):
                    copy.start()

    def add(self, i, stage):
        _, _, order, bufs, out = self.pieces[i]
        for copy in self.copies(i, stage):
            copy.wait_recv()
        buf = bufs[stage]
        total = self.pick(i, stage, self.at[order[stage]])[...].astype(f32)
        for j in range(self.grid.size[order[stage]] - 1):
            total = total + buf[j].astype(f32)
        if stage == self.stages - 1:
            out[...] = total.reshape(out.shape)
        else:
            buf[0] = total.astype(buf.dtype)

    def finish(self):
        for i in range(len(self.pieces)):
            for stage in range(self.stages):
                for copy in self.copies(i, stage):
                    copy.wait_send()


def scatter_buffers(grid, order, rows, columns, dtype):
    shapes, left = [], list(DIMS)
    for d in grid.order(order):
        left.remove(d)
        shapes.append((grid.size[d] - 1,) + tuple(grid.size[e] for e in left) + (rows, columns))
    return [pltpu.VMEM(s, dtype) for s in shapes]


def cuts(total, parts, unit):
    while parts > 1 and total % (parts * unit):
        parts -= 1
    return [(j * (total // parts), total // parts) for j in range(parts)]


def dotg(a, b, ca, cb, precision=None):
    return lax.dot_general(
        a, b, (((ca,), (cb,)), ((), ())), preferred_element_type=f32, precision=precision
    )


def iota(shape, dim):
    return lax.broadcasted_iota(jnp.int32, shape, dim)


def three_parts(x):
    high = x.astype(bf16).astype(f32)
    mid = (x - high).astype(bf16).astype(f32)
    return high, mid, x - high - mid


def spread_vector(rows, n):
    shards, width = rows.shape
    total = shards * n
    place = (iota((width, total), 1) % n == iota((width, total), 0)).astype(f32).astype(bf16)
    wide = dotg(rows, place, 1, 0)
    keep = iota((shards, total), 1) // n == iota((shards, total), 0)
    return jnp.sum(jnp.where(keep, wide, 0.0), axis=0, keepdims=True)


def fold_vector(vector, shards, n, width):
    total = shards * n
    keep = iota((shards, total), 1) // n == iota((shards, total), 0)
    place = (iota((total, width), 0) % n == iota((total, width), 1)).astype(f32).astype(bf16)
    parts = [jnp.where(keep, part, 0.0).astype(bf16) for part in three_parts(vector)]
    return sum(dotg(part, place, 1, 0) for part in parts)


def attend_prepare(qkv_ref, prep, live, pair):
    length, width = qkv_ref.shape[0], qkv_ref.shape[1] // 3
    k = qkv_ref[:, pl.ds(pl.multiple_of(width + pair * LANES, LANES), LANES)].astype(f32)
    v = qkv_ref[:, pl.ds(pl.multiple_of(2 * width + pair * LANES, LANES), LANES)].astype(f32)
    lane, row = iota((length, LANES), 1), iota((length, LANES), 0)
    bias = jnp.where(row < live, 0.0, neg_fill)
    k = k * (1.0 / math.sqrt(HEAD_DIM))
    for h in range(2):
        mine, spare = lane // HEAD_DIM == h, HEAD_DIM * (1 - h)
        prep[h, 0] = jnp.where(mine, k, jnp.where(lane == spare, bias, 0.0)).astype(bf16)
        prep[h, 1] = jnp.where(mine, v, 1.0).astype(bf16)


def attend(qkv_ref, context_ref, lse_ref, prep, pair, rows, block):
    out = pl.ds(pl.multiple_of(pair * LANES, LANES), LANES)
    q = qkv_ref[rows, out].astype(f32)
    lane = iota((block, LANES), 1)
    low = lane < HEAD_DIM
    sums, tops = [], []
    for h in range(2):
        spare = HEAD_DIM * (1 - h)
        query = jnp.where(lane // HEAD_DIM == h, q, jnp.where(lane == spare, 1.0, 0.0)).astype(bf16)
        scores = dotg(query, prep[h, 0], 1, 1)
        top = jnp.max(scores, axis=1, keepdims=True)
        weights = jnp.exp(scores - top).astype(bf16)
        sums.append(dotg(weights, prep[h, 1], 1, 0))
        tops.append(top)
    num = jnp.where(low, sums[0], sums[1])
    den = pltpu.roll(jnp.where(low, sums[1], sums[0]), HEAD_DIM, 1)
    context_ref[rows, out] = (num / den).astype(bf16)
    total = jnp.where(low, tops[0], tops[1]) + jnp.log(den)
    other = pltpu.roll(total, HEAD_DIM, 1)
    kept = jnp.where(lane == 2 * pair + 1, other, lse_ref[rows, :])
    lse_ref[rows, :] = jnp.where(lane == 2 * pair, total, kept)


def gelu_parts(x):
    cdf = 0.5 * (1.0 + lax.erf(x * (1.0 / math.sqrt(2.0))))
    return cdf, jnp.exp(-0.5 * x * x) * (1.0 / math.sqrt(2.0 * math.pi))


def normalize(values):
    center = values - jnp.mean(values, axis=-1, keepdims=True)
    scale = lax.rsqrt(jnp.mean(center * center, axis=-1, keepdims=True) + eps_norm)
    return center * scale, scale


def gather_plan(shapes):
    plan, every = [("s", ())], slice(None)
    width = shapes["o"][1]
    for a, n in cuts(width, 3, LANES):
        plan += [("q", (every, pl.ds(part * width + a, n))) for part in range(3)]
    for name, parts in (("o", 2), ("u", 6), ("p", 2), ("d", 3)):
        rows, columns = shapes[name]
        for a, n in cuts(columns, parts, LANES):
            for b, m in cuts(rows, 2 if name == "d" else 1, 8):
                plan.append((name, (pl.ds(b, m) if name == "d" else every, pl.ds(a, n))))
    return [(name, sub, GATHER_ORDERS[i % len(GATHER_ORDERS)]) for i, (name, sub) in enumerate(plan)]


def forward_kernel(grid, plan, sizes, *refs):
    (len_ref, tokens_ref, keep_a, keep_f, wq, wo, wu, wd, wp), refs = refs[:9], refs[9:]
    count = len(sizes)
    small_in, refs = refs[:count], refs[count:]
    kept_hbm, (act_t, slope), refs = refs[:16], refs[16:18], refs[18:]
    firsts, small_out, refs = refs[0], refs[1 : 1 + count], refs[1 + count :]
    kept, refs = refs[:16], refs[16:]
    (gq, go, gu, gd, gp, qkv_ref, context, lse, tokens_t, context_t, hidden_t, norm1, scale1, norm2, scale2, layer_out) = kept
    (gs, keep, hidden, hidden_low, act, act_buf, slope_buf, prep, bias), refs = refs[:9], refs[9:]
    send, recv, own_sem, keep_sem, act_sem, slope_sem, out_sem = refs
    length, width = context.shape
    b_qv, b_out, g1, b1, b_up, b_down, g2, b2, b_pool = small_out
    outs = [pltpu.make_async_copy(src, dst, out_sem.at[i]) for i, (src, dst) in enumerate(zip(kept, kept_hbm))]

    def put(*which):
        for i, ref in enumerate(kept):
            if any(ref is w for w in which):
                outs[i].start()

    at = grid.me()
    own = tuple(at[d] for d in DIMS)
    load = pltpu.make_async_copy(keep_a, keep, keep_sem)
    load.start()
    to_own = []
    for i, (src, dst) in enumerate(((wq, gq), (wo, go), (wu, gu), (wd, gd), (wp, gp))):
        to_own.append(pltpu.make_async_copy(src, dst.at[own], own_sem.at[i]))
        to_own[-1].start()
    mine = gs.at[own]
    mine[...] = jnp.zeros(mine.shape, bf16)
    for i, (ref, n) in enumerate(zip(small_in, sizes)):
        mine[i : i + 1, 0:n] = ref[...]
    where = dict(q=gq, o=go, u=gu, d=gd, p=gp, s=gs)
    gather = Gather(grid, [(where[name], sub, order) for name, sub, order in plan], send, recv)
    number = {}
    for i, (name, _, _) in enumerate(plan):
        number.setdefault(name, []).append(i)
    end = {name: [gather.whole[i] for i in numbers] for name, numbers in number.items()}
    grid.barrier(grid.straight())
    for copy in to_own:
        copy.wait()
    gather.begin()
    tokens_t[...] = tokens_ref[...].T
    lse[...] = jnp.zeros_like(lse)
    put(tokens_t)
    gather.until(end["s"][0])
    rows = gs[...].reshape((grid.count,) + gs.shape[-2:])
    for i, (ref, n) in enumerate(zip(small_out, sizes)):
        ref[...] = spread_vector(rows[:, i, :], n)
    bias[:, :width] = b_qv[:, :width]
    bias[:, width : 2 * width] = jnp.zeros((1, width), f32)
    bias[:, 2 * width :] = b_qv[:, width:]

    groups = len(number["q"]) // 3
    part = width // groups
    pairs, block = part // LANES, min(512, length)
    blocks, live = length // block, len_ref[0]
    each = pairs * blocks

    def attention(t):
        @pl.when(t % each == 0)
        def _():
            for j in range(3):
                cols = pl.ds(pl.multiple_of(j * width + t // each * part, part), part)
                out = dotg(tokens_ref[...], gq[:, :, :, :, :, cols].reshape(width, part), 1, 0)
                qkv_ref[:, cols] = (out + bias[:, cols]).astype(bf16)

        @pl.when(t % blocks == 0)
        def _():
            attend_prepare(qkv_ref, prep, live, t // blocks)

        rows = pl.ds(pl.multiple_of((t % blocks) * block, block), block)
        attend(qkv_ref, context, lse, prep, t // blocks, rows, block)

    slots = groups * each
    first, last = end["q"][2], end["u"][len(end["u"]) // 2]
    gather.loop(
        slots,
        [max(end["q"][3 * (t // each) + 2], first + t * (last - first) // slots) for t in range(slots)],
        attention,
    )
    put(gq, qkv_ref, context, lse)

    load.wait()
    block = min(512, length)
    blocks = length // block

    def row_block(t):
        return pl.ds(pl.multiple_of(t * block, block), block)

    gather.until(end["o"][-1])

    def project(t):
        here = row_block(t)
        attended = dotg(context[here, :], go[...].reshape(width, width), 1, 0) + b_out[...]
        total = tokens_ref[here, :].astype(f32) + attended * (keep[here, :].astype(f32) * keep_scale)
        norm, scale = normalize(total)
        out = norm * g1[...] + b1[...]
        hidden[here, :] = out
        hidden_low[here, :] = out.astype(bf16)
        hidden_t[:, here] = out.astype(bf16).T
        context_t[:, here] = context[here, :].T
        norm1[here, :] = norm.astype(bf16)
        scale1[here, :] = jnp.broadcast_to(scale, (block, LANES))

    gather.loop(blocks, [gather.now] * blocks, project)
    load = pltpu.make_async_copy(keep_f, keep, keep_sem)
    load.start()
    put(go, hidden_t, context_t, norm1, scale1)

    parts = len(end["u"])
    step = gu.shape[-1] // parts
    strip = min(128, length)

    def saved(t, cols):
        yield pltpu.make_async_copy(act_buf.at[t % 2], act_t.at[cols, :], act_sem.at[t % 2])
        yield pltpu.make_async_copy(slope_buf.at[t % 2], slope.at[:, cols], slope_sem.at[t % 2])

    def up(t):
        cols = pl.ds(pl.multiple_of(t * step, step), step)
        weight = gu[:, :, :, :, :, cols].reshape(width, step)

        @pl.when(t >= 2)
        def _():
            for copy in saved(t, cols):
                copy.wait()

        for i in range(length // strip):
            here = slice(i * strip, (i + 1) * strip)
            pre = dotg(hidden_low[here, :], weight, 1, 0) + b_up[:, cols]
            cdf, pdf = gelu_parts(pre)
            out = (pre * cdf).astype(bf16)
            act[here, cols] = out
            act_buf[t % 2, :, here] = out.T
            slope_buf[t % 2, here, :] = (cdf + pre * pdf).astype(bf16)
        for copy in saved(t, cols):
            copy.start()

    gather.loop(parts, end["u"], up)
    for t in range(max(0, parts - 2), parts):
        for copy in saved(t, pl.ds(0, step)):
            copy.wait()

    load.wait()
    put(gu)
    halves = len(cuts(gd.shape[-2], 2, 8))
    ends = end["d"][halves - 1 :: halves]
    parts = len(ends)
    step = width // parts

    def down(t):
        cols = pl.ds(pl.multiple_of(t * step, step), step)
        out = dotg(act[...], gd[:, :, :, :, :, cols].reshape(-1, step), 1, 0) + b_down[:, cols]
        hidden[:, cols] += out * (keep[:, cols].astype(f32) * keep_scale)

    gather.loop(parts, ends, down)
    put(gd, gp)
    block = min(256, length)
    blocks = length // block

    def norm(t):
        here = row_block(t)
        value, scale = normalize(hidden[here, :])
        out = value * g2[...] + b2[...]
        norm2[here, :] = value.astype(bf16)
        scale2[here, :] = jnp.broadcast_to(scale, (block, LANES))
        layer_out[here, :] = out.astype(bf16)

        @pl.when(t == 0)
        def _():
            first = out[0:8].astype(bf16)
            pooled = jnp.tanh(dotg(first, gp[...].reshape(width, width), 1, 0) + b_pool[...])
            firsts[0:1, :] = pooled[0:1]
            firsts[1:2, :] = first[0:1].astype(f32)

    gather.loop(blocks, [gather.now] * blocks, norm)
    put(norm2, scale2, layer_out)
    gather.finish()
    for copy in outs:
        copy.wait()


def run_forward(grid, length_of, tokens, keep_a, keep_f, big, small):
    length, width = tokens.shape
    names = ("q", "o", "u", "d", "p")
    shapes = {k: w.shape for k, w in zip(names, big)}
    inner = shapes["u"][1]
    sizes = [v.shape[0] for v in small]
    plan = gather_plan(shapes)
    pad = -(-max(sizes) // LANES) * LANES
    step = inner // sum(p[0] == "u" for p in plan)
    vmem, anywhere = pl.BlockSpec(memory_space=pltpu.VMEM), pl.BlockSpec(memory_space=pl.ANY)
    shape = jax.ShapeDtypeStruct
    kept = [(grid.shape + shapes[k], bf16) for k in names] + [
        ((length, 3 * width), bf16),
        ((length, width), bf16),
        ((length, LANES), f32),
        ((width, length), bf16),
        ((width, length), bf16),
        ((width, length), bf16),
        ((length, width), bf16),
        ((length, LANES), f32),
        ((length, width), bf16),
        ((length, LANES), f32),
        ((length, width), bf16),
    ]
    return pl.pallas_call(
        functools.partial(forward_kernel, grid, plan, sizes),
        out_shape=[shape(*k) for k in kept]
        + [shape((inner, length), bf16), shape((length, inner), bf16), shape((2, width), f32)]
        + [shape((1, grid.count * n), f32) for n in sizes],
        in_specs=[pl.BlockSpec(memory_space=pltpu.SMEM), vmem, anywhere, anywhere] + [vmem] * (5 + len(small)),
        out_specs=[anywhere] * 18 + [vmem] * (1 + len(small)),
        scratch_shapes=[pltpu.VMEM(*k) for k in kept]
        + [
            pltpu.VMEM(grid.shape + (16, pad), bf16),
            pltpu.VMEM((length, width), jnp.int32),
            pltpu.VMEM((length, width), f32),
            pltpu.VMEM((length, width), bf16),
            pltpu.VMEM((length, inner), bf16),
            pltpu.VMEM((2, step, length), bf16),
            pltpu.VMEM((2, length, step), bf16),
            pltpu.VMEM((2, 2, length, LANES), bf16),
            pltpu.VMEM((1, 3 * width), f32),
            pltpu.SemaphoreType.DMA((len(plan), grid.slots)),
            pltpu.SemaphoreType.DMA((len(plan), grid.slots)),
            pltpu.SemaphoreType.DMA((5,)),
            pltpu.SemaphoreType.DMA,
            pltpu.SemaphoreType.DMA((2,)),
            pltpu.SemaphoreType.DMA((2,)),
            pltpu.SemaphoreType.DMA((16,)),
        ],
        compiler_params=pltpu.CompilerParams(
            collective_id=0, has_side_effects=True, vmem_limit_bytes=VMEM_LIMIT
        ),
        name="forward",
    )(length_of, tokens, keep_a, keep_f, *big, *[v.reshape(1, -1) for v in small])


def pool_and_loss(views, partners_ref, wp, here, shard_rows, unit_ref, work, cls_grad, pool_w, pool_b, loss):
    high = lax.Precision.HIGHEST
    count, width = math.prod(views.shape[:4]), views.shape[-1]
    each = count // views.shape[0]

    def pooled_rows(z):
        rows = views[z].reshape((each,) + views.shape[-2:])
        pooled = rows[:, 0, :]
        scale = lax.rsqrt(jnp.sum(pooled * pooled, axis=1, keepdims=True) + 1e-06)
        return slice(z * each, (z + 1) * each), pooled, scale, rows[:, 1, :]

    for z in range(views.shape[0]):
        at, pooled, scale, cls = pooled_rows(z)
        unit_ref[at, :] = pooled * scale
        work[count + z * each : count + (z + 1) * each, :] = cls.astype(bf16)
    unit = unit_ref[0:count, :]
    sims = dotg(unit, unit, 1, 1, high) / logit_divisor
    column, row = iota((count, count), 1), iota((count, count), 0)
    others = jnp.where(row == column, neg_fill, sims)
    top = jnp.max(others, axis=1, keepdims=True)
    weights = jnp.exp(others - top)
    total = jnp.sum(weights, axis=1, keepdims=True)
    partner = row == partners_ref[...]
    target = jnp.sum(jnp.where(partner, sims, 0.0), axis=1, keepdims=True)
    lost = jnp.sum(top + jnp.log(total) - target, axis=0, keepdims=True) / count
    loss[...] = jnp.broadcast_to(lost, loss.shape)
    pull = weights / total - jnp.where(partner, 1.0, 0.0)
    pull = pull + dotg(pull, (row == column).astype(f32), 0, 0, high)
    for z in range(views.shape[0]):
        at, pooled, scale, _ = pooled_rows(z)
        unit_grad = dotg(pull[at], unit, 1, 0, high) / logit_divisor
        along = jnp.sum(pooled * unit_grad, axis=1, keepdims=True)
        pooled_grad = scale * unit_grad - pooled * (scale * scale * scale * along)
        work[at, :] = (pooled_grad * (1.0 - pooled * pooled)).astype(bf16)
    pre, cls = work[0:count, :], work[count : 2 * count, :]
    mine = jnp.sum(jnp.where(iota((count, width), 0) == here, pre.astype(f32), 0.0), axis=0, keepdims=True)
    cls_grad[...] = dotg(jnp.broadcast_to(mine, (8, width)).astype(bf16), wp, 1, 1)
    place = (iota((width, LANES), 0) == here * shard_rows + iota((width, LANES), 1)).astype(f32).astype(bf16)
    cls_rows = dotg(cls, place, 1, 0).astype(bf16)
    pool_w[...] = dotg(cls_rows, pre, 0, 0)[:shard_rows]
    sums = jnp.broadcast_to(jnp.sum(pre.astype(f32), axis=0, keepdims=True), (8, width))
    pool_b[...] = sum(dotg(part.astype(bf16), place, 1, 0) for part in three_parts(sums))


def attend_back(qkv_ref, context, dcontext, lse, live, pair, prep):
    length, width = qkv_ref.shape[0], context.shape[1]
    scale = 1.0 / math.sqrt(HEAD_DIM)
    one = pl.ds(pl.multiple_of(pair * LANES, LANES), LANES)

    def col(part):
        return pl.ds(pl.multiple_of(part * width + pair * LANES, LANES), LANES)

    q, k, v = (qkv_ref[:, col(j)].astype(f32) for j in range(3))
    d = dcontext[:, one].astype(f32)
    lane, row = iota((length, LANES), 1), iota((length, LANES), 0)
    bias = jnp.where(row < live, 0.0, neg_fill)
    mine, place = lane // HEAD_DIM, lane % HEAD_DIM
    source, target = iota((LANES, LANES), 0), iota((LANES, LANES), 1)
    swap = (source // HEAD_DIM != target // HEAD_DIM).astype(f32).astype(bf16)
    both = d * context[:, one].astype(f32)
    inner = sum(dotg(part.astype(bf16), swap, 1, 0) for part in three_parts(both))
    d0, d1, d2 = three_parts(-inner)
    extra_d = jnp.where(place == 0, d0, jnp.where(place == 1, d1, jnp.where(place == 2, d2, 0.0)))
    extra_q = jnp.where(place == 0, 1.0, 0.0)
    for j, part in enumerate(three_parts(-lse[...])):
        head = jnp.where(target < HEAD_DIM, 2 * pair + 1, 2 * pair)
        pick = ((source == head) & (target % HEAD_DIM == j + 1)).astype(f32).astype(bf16)
        extra_q = extra_q + dotg(part.astype(bf16), pick, 1, 0)
    extra_k = jnp.where(place == 0, bias, jnp.where(place < 4, 1.0, 0.0))
    extra_v = jnp.where(place < 3, 1.0, 0.0)
    q = q * scale
    for h in range(2):
        here = mine == h
        prep[h, 0] = jnp.where(here, q, extra_q).astype(bf16)
        prep[h, 1] = jnp.where(here, k, extra_k).astype(bf16)
        prep[h, 2] = jnp.where(here, d, extra_d).astype(bf16)
        prep[h, 3] = jnp.where(here, v, extra_v).astype(bf16)
        prep[h, 4] = jnp.where(here, k * scale, 0.0).astype(bf16)
    return q.astype(bf16).T, d.astype(bf16).T


def scatter_plan(grid, shapes):
    plan, every = [], slice(None)
    width = shapes["o"][1]
    rows, columns = shapes["d"]
    plan += [("d", (pl.ds(a, n), every), n, columns) for a, n in cuts(rows, 6, 8)]
    for name, parts in (("u", 6), ("o", 2)):
        rows, columns = shapes[name]
        plan += [(name, (every, pl.ds(a, n)), rows, n) for a, n in cuts(columns, parts, LANES)]
    for a, n in cuts(width, 3, LANES):
        plan += [("q", (every, pl.ds(part * width + a, n)), shapes["q"][0], n) for part in range(3)]
    plan.append(("s", (), 16, shapes["s"]))
    return [(p[0], p[1], SCATTER_ORDERS[i % 2]) + p[2:] for i, p in enumerate(plan)]


def backward_kernel(grid, whole, plan, sizes, shard_rows, *refs):
    (len_ref, partners_ref, firsts, g1, g2), refs = refs[:5], refs[5:]
    (h_cot, h_keep_a, h_keep_f, h_norm1, h_scale1, h_norm2, h_scale2, h_act, h_slope, h_hidden, h_context_t), refs = refs[:11], refs[11:]
    (h_qkv, h_context, h_lse, h_tokens, h_wq, h_wo, h_wu, h_wd, h_wp), refs = refs[:9], refs[9:]
    (rq, ro, ru, rd, rs, pool_w, pool_b, loss, h_tokens_grad), refs = refs[:9], refs[9:]
    (dd, du, do, dsmall, grad, gctx, low, norm, keep, scale, vec, cls_grad, views, wp), refs = refs[:14], refs[14:]
    (send, recv, view_send, view_recv, sems, pair_sems), bufs = refs[:6], list(refs[6:])
    length, width = grad.shape
    inner = vec.shape[1]
    sources, results = dict(d=dd, u=du, o=do, s=dsmall), dict(d=rd, u=ru, o=ro, q=rq, s=rs)
    number = {}
    for i, p in enumerate(plan):
        number.setdefault(p[0], []).append(i)
    cot = low

    def copy(k, src, dst):
        return pltpu.make_async_copy(src, dst, sems.at[k])

    first_loads = [copy(0, h_cot, cot), copy(1, h_norm2, norm), copy(2, h_scale2, scale), copy(3, h_keep_f, keep), copy(4, h_wp, wp)]
    for c in first_loads:
        c.start()
    at_all = whole.me()
    views[tuple(at_all[d] for d in DIMS)] = firsts[...]
    exchange = Exchange(whole, views, view_send, view_recv)
    whole.barrier(whole.straight() + [o for o in whole.around(("z", "c")) + whole.around(("y", "x")) if len(o) > 1])
    exchange.start(0)
    vec[...] = jnp.zeros_like(vec)
    for c in first_loads:
        c.wait()
    strip = min(128, length)
    strips = length // strip

    def strip_of(t):
        return pl.ds(pl.multiple_of(t * strip, strip), strip)

    def add_row(j, x):
        vec[j : j + 1, : x.shape[1]] += jnp.sum(x, axis=0, keepdims=True)

    def norm_back(here, up, gain, slot):
        value = norm[here, :].astype(f32)
        scaled = up * gain[...]
        along = jnp.mean(scaled * value, axis=1, keepdims=True)
        back = scale[here, 0:1] * (scaled - jnp.mean(scaled, axis=1, keepdims=True) - value * along)
        add_row(slot, up * value)
        add_row(slot + 1, up)
        grad[here, :] = back
        out = (back * (keep[here, :].astype(f32) * keep_scale)).astype(bf16)
        low[here, :] = out
        return out.astype(f32)

    def second_norm(t, extra):
        here = strip_of(t)
        up = cot[here, :].astype(f32)
        if extra is not None:
            up = up + jnp.where(iota((strip, width), 0) + t * strip == 0, extra, 0.0)
        add_row(5, norm_back(here, up, g2, 6))
        return 0

    held = -(-math.prod(whole.shape) // strip)
    lax.fori_loop(held, strips, lambda t, _: second_norm(t, None), 0)
    exchange.wait(0)
    exchange.start(1)
    exchange.wait(1)
    here = lax.axis_index("dp") * (whole.size["y"] * whole.size["x"]) + lax.axis_index("fsdp")
    pool_and_loss(views, partners_ref, wp[...], here, shard_rows, grad, gctx, cls_grad, pool_w, pool_b, loss)
    lax.fori_loop(0, held, lambda t, _: second_norm(t, cls_grad[0:1, :]), 0)
    wo = wp
    second_loads = [copy(1, h_norm1, norm), copy(2, h_scale1, scale), copy(3, h_keep_a, keep), copy(6, h_wo, wo)]
    for c in second_loads:
        c.start()

    pieces, left = [], bufs
    for name, sub, order, _, _ in plan:
        n = len(grid.order(order))
        pieces.append([sources.get(name), sub, order, left[:n], results[name].at[sub] if sub else results[name]])
        left = left[n:]
    groups = len(number["q"]) // 3
    early, last = len(plan) - 1 - len(number["q"]), len(plan) - 1
    scatter = Scatter(grid, pieces, send, recv)
    stages, lag = scatter.stages, 4
    steps = [
        [(j - stage * lag, stage) for stage in range(stages) if 0 <= j - stage * lag < early]
        for j in range(early + (stages - 1) * lag)
    ]

    def feed_forward(act, slope, wd, wu, gup, turned):
        third = [copy(5, h_hidden, turned), copy(7, h_context_t, turned)]
        third[0].start()
        block = min(256, length)
        chunk, part = act.shape[1], slope.shape[2]
        chunks, parts = inner // chunk, inner // part
        slab = wu.shape[1]

        def act_load(t):
            return pltpu.make_async_copy(h_act.at[pl.ds(pl.multiple_of(t * chunk, chunk), chunk), :], act.at[t % 2], pair_sems.at[0, t % 2])

        def part_loads(t):
            cols = pl.ds(pl.multiple_of(t * part, part), part)
            yield pltpu.make_async_copy(h_slope.at[:, cols], slope.at[t % 2], pair_sems.at[1, t % 2])
            yield pltpu.make_async_copy(h_wd.at[cols, :], wd.at[t % 2], pair_sems.at[2, t % 2])

        def slab_load(t):
            return pltpu.make_async_copy(h_wu.at[pl.ds(pl.multiple_of(t * slab, slab), slab), :], wu.at[t % 2], pair_sems.at[3, t % 2])

        act_load(0).start()
        for c in part_loads(0):
            c.start()
        slab_load(0).start()
        across = grid.size["y"] * grid.size["x"]

        def down_weight(t, _):
            @pl.when(t + 1 < chunks)
            def _():
                act_load(t + 1).start()

            act_load(t).wait()
            out = dotg(act[t % 2], low[...], 1, 0).astype(bf16)
            dd[t // grid.size["c"], t % grid.size["c"]] = out.reshape(dd.shape[2:])
            return 0

        lax.fori_loop(0, chunks, down_weight, 0)
        for i in number["d"]:
            scatter.begin(i)
        third[0].wait()

        def up_part(t, _):
            cols = pl.ds(pl.multiple_of(t * part, part), part)

            @pl.when(t + 1 < parts)
            def _():
                for c in part_loads(t + 1):
                    c.start()

            for c in part_loads(t):
                c.wait()
            for i in range(length // block):
                rows = slice(i * block, (i + 1) * block)
                out = dotg(low[rows, :], wd[t % 2], 1, 1) * slope[t % 2, rows, :].astype(f32)
                gup[rows, cols] = out.astype(bf16)
            vec[4:5, cols] = jnp.sum(gup[:, cols].astype(f32), axis=0, keepdims=True)
            out = dotg(turned[...], gup[:, cols], 1, 0).astype(bf16)
            du[:, :, :, :, :, cols] = out.reshape(grid.shape + (-1, part))
            for k, i in enumerate(number["u"]):

                @pl.when(t == k)
                def _():
                    scatter.begin(i)
                    scatter.run(steps[k])

            return 0

        lax.fori_loop(0, parts, up_part, 0)
        third[1].start()

        def hidden_part(t, _):
            cols = pl.ds(pl.multiple_of(t * slab, slab), slab)

            @pl.when(t + 1 < width // slab)
            def _():
                slab_load(t + 1).start()

            slab_load(t).wait()
            grad[:, cols] += dotg(gup[...], wu[t % 2], 1, 1)
            for k in range(width // slab):

                @pl.when(t == k)
                def _():
                    scatter.run(steps[parts + k])

            return 0

        lax.fori_loop(0, width // slab, hidden_part, 0)
        for c in second_loads:
            c.wait()

        def first_norm(t, _):
            add_row(1, norm_back(strip_of(t), grad[strip_of(t), :], g1, 2))
            return 0

        lax.fori_loop(0, strips, first_norm, 0)
        for c in (copy(9, h_context, norm), copy(10, h_lse, scale)):
            c.start()
        third[1].wait()
        for i in number["o"]:
            cols = plan[i][1][1]
            out = dotg(turned[...], low[:, cols], 1, 0).astype(bf16)
            do[:, :, :, :, :, cols] = out.reshape(grid.shape + (-1, cols.size))
            scatter.begin(i)
        for i in range(length // block):
            rows = slice(i * block, (i + 1) * block)
            gctx[rows, :] = dotg(low[rows, :], wo[...], 1, 1).astype(bf16)
        scatter.run(steps[parts + width // slab])
        return parts + width // slab + 1

    chunk, part, slab = inner // (grid.size["z"] * grid.size["c"]), inner // len(number["u"]), width // 3
    done = []

    def first_scope(*refs):
        done.append(feed_forward(*refs))

    pl.run_scoped(
        first_scope,
        pltpu.VMEM((2, chunk, length), bf16),
        pltpu.VMEM((2, length, part), bf16),
        pltpu.VMEM((2, part, width), bf16),
        pltpu.VMEM((2, slab, inner), bf16),
        pltpu.VMEM((length, inner), bf16),
        pltpu.VMEM((width, length), bf16),
    )
    step = done[0]

    def attention(qkv, tokens_t, wq, dq, prep, turned, acc):
        context, lse = norm, scale
        block = min(256, length) if grid.with_fsdp else min(128, length)
        blocks = length // block

        def rows_of(t):
            return pl.ds(pl.multiple_of(t * block, block), block)

        for i in number["q"]:
            scatter.pieces[i] = (dq,) + scatter.pieces[i][1:]
        span = width // groups

        def group_loads(g):
            for j in range(3):
                cols = pl.ds(j * width + g * span, span)
                yield pltpu.make_async_copy(h_qkv.at[:, cols], qkv.at[:, cols], pair_sems.at[j, g % 2])

        for g in range(min(2, groups)):
            for c in group_loads(g):
                c.start()
        loads = [copy(11, h_tokens, tokens_t), copy(12, h_wq.at[:, 0:width], wp)]
        loads += [copy(6, h_wq.at[:, width : 2 * width], wq.at[0]), copy(7, h_wq.at[:, 2 * width :], wq.at[1])]
        for c in loads:
            c.start()
        for c in (copy(9, h_context, norm), copy(10, h_lse, scale)):
            c.wait()
        each = span // LANES * blocks
        slots = groups * each
        live = len_ref[0]
        head = [slice(h * HEAD_DIM, (h + 1) * HEAD_DIM) for h in range(2)]
        due, late = [[] for _ in range(slots)], []
        for j, events in enumerate(steps[step:]):
            due[j * (slots - each // 2) // (len(steps) - step)] += events
        for g in range(groups - 1):
            for stage in range(stages):
                at, events = each * (g + 1) - 1 + SPACING * (stage + 1), [(i, stage) for i in number["q"][3 * g : 3 * g + 3]]
                if at < slots:
                    due[at] += events
                else:
                    late.append(events)
        tail = [late[j] if j < len(late) else [] for j in range(max(stages, len(late)))]
        for stage in range(stages):
            tail[len(tail) - stages + stage] += [(i, stage) for i in number["q"][-3:] + [last]]

        def slot(t, _):
            pair, b = t // blocks, t % blocks
            rows = rows_of(b)
            one = pl.ds(pl.multiple_of(pair * LANES, LANES), LANES)

            for g in range(groups):

                @pl.when(t == g * each)
                def _():
                    for c in group_loads(g):
                        c.wait()
                    if g + 2 < groups:
                        for c in group_loads(g + 2):
                            c.start()

            @pl.when(b == 0)
            def _():
                turned[0], turned[1] = attend_back(qkv, context, gctx, lse, live, pair, prep)
                acc[...] = jnp.zeros_like(acc)

            dq_rows = jnp.zeros((block, LANES), f32)
            for h in range(2):
                p = jnp.exp(dotg(prep[h, 0, rows, :], prep[h, 1], 1, 1))
                dp = dotg(prep[h, 2, rows, :], prep[h, 3], 1, 1)
                ds = (p * dp).astype(bf16)
                acc[0, head[h], :] += dotg(turned[1, head[h], rows], p.astype(bf16), 1, 0)
                acc[1, head[h], :] += dotg(turned[0, head[h], rows], ds, 1, 0)
                dq_rows = dq_rows + dotg(ds, prep[h, 4], 1, 0)
            qkv[rows, one] = dq_rows.astype(bf16)

            @pl.when(b == blocks - 1)
            def _():
                qkv[:, pl.ds(pl.multiple_of(width + pair * LANES, LANES), LANES)] = acc[1].astype(bf16).T
                qkv[:, pl.ds(pl.multiple_of(2 * width + pair * LANES, LANES), LANES)] = acc[0].astype(bf16).T

            for k in range(slots):
                if due[k]:

                    @pl.when(t == k)
                    def _():
                        scatter.run(due[k])

            @pl.when(t == each - 1)
            def _():
                loads[0].wait()

            @pl.when(t % each == each - 1)
            def _():
                for j in range(3):
                    cols = pl.ds(pl.multiple_of(j * width + t // each * span, LANES), span)
                    out = dotg(tokens_t[...], qkv[:, cols], 1, 0).astype(bf16)
                    dq[:, :, :, :, :, cols] = out.reshape(grid.shape + (-1, span))
                for g in range(groups):

                    @pl.when(t == each * (g + 1) - 1)
                    def _():
                        for i in number["q"][3 * g : 3 * g + 3]:
                            scatter.begin(i)

            return 0

        lax.fori_loop(0, slots, slot, 0)
        sums = dotg(jnp.ones((8, length), bf16), qkv[...], 1, 0)[0:1]
        vec[0:1, :width] = sums[:, :width]
        vec[0:1, width : 2 * width] = sums[:, 2 * width :]
        pad = dsmall.shape[-1]
        dsmall[...] = jnp.zeros_like(dsmall)
        for j, n in enumerate(sizes):
            folded = fold_vector(vec[j : j + 1, : grid.count * n], grid.count, n, pad)
            dsmall[:, :, :, :, j, :] = folded.reshape(grid.shape + (pad,))
        scatter.begin(number["s"][0])
        for c in loads[1:]:
            c.wait()
        rows = length // len(tail)
        for i, events in enumerate(tail):
            here = slice(i * rows, (i + 1) * rows)
            total = grad[here, :] + dotg(qkv[here, :width], wp[...], 1, 1)
            for j in range(2):
                total = total + dotg(qkv[here, (j + 1) * width : (j + 2) * width], wq[j], 1, 1)
            low[here, :] = total.astype(bf16)
            scatter.run(events)
        out = copy(13, low, h_tokens_grad)
        out.start()
        scatter.finish()
        exchange.finish()
        out.wait()

    pl.run_scoped(
        attention,
        pltpu.VMEM((length, 3 * width), bf16),
        pltpu.VMEM((width, length), bf16),
        pltpu.VMEM((2, width, width), bf16),
        pltpu.VMEM(grid.shape + (width // grid.count, 3 * width), bf16),
        pltpu.VMEM((2, 5, length, LANES), bf16),
        pltpu.VMEM((2, LANES, length), bf16),
        pltpu.VMEM((2, LANES, length), f32),
    )


def run_backward(grid, whole, length_of, partners, firsts, gains, hbm, length, width, inner, sizes, shard_rows):
    rows = width // grid.count
    pad = -(-max(sizes) // LANES) * LANES
    shapes = {"q": (rows, 3 * width), "o": (rows, width), "u": (rows, inner), "d": (inner // grid.count, width), "s": pad}
    plan = scatter_plan(grid, shapes)
    bufs = []
    for name, _, order, r, c in plan:
        bufs += scatter_buffers(grid, order, r, c, f32 if name == "s" else bf16)
    views_count = len(whole.around(("z", "c"))) + len(whole.around(("y", "x")))
    vmem, anywhere = pl.BlockSpec(memory_space=pltpu.VMEM), pl.BlockSpec(memory_space=pl.ANY)
    shape = jax.ShapeDtypeStruct
    return pl.pallas_call(
        functools.partial(backward_kernel, grid, whole, plan, sizes, shard_rows),
        out_shape=[shape(shapes[k], f32) for k in ("q", "o", "u", "d")]
        + [
            shape((16, pad), f32),
            shape((shard_rows, width), f32),
            shape((8, LANES), f32),
            shape((8, LANES), f32),
            shape((length, width), bf16),
        ],
        in_specs=[pl.BlockSpec(memory_space=pltpu.SMEM)] + [vmem] * 4 + [anywhere] * len(hbm),
        out_specs=[vmem] * 8 + [anywhere],
        scratch_shapes=[pltpu.VMEM(grid.shape + shapes[k], bf16) for k in ("d", "u", "o")]
        + [
            pltpu.VMEM(grid.shape + (16, pad), f32),
            pltpu.VMEM((length, width), f32),
            pltpu.VMEM((length, width), bf16),
            pltpu.VMEM((length, width), bf16),
            pltpu.VMEM((length, width), bf16),
            pltpu.VMEM((length, width), jnp.int32),
            pltpu.VMEM((length, LANES), f32),
            pltpu.VMEM((16, inner), f32),
            pltpu.VMEM((8, width), f32),
            pltpu.VMEM(whole.shape + (2, width), f32),
            pltpu.VMEM((width, width), bf16),
            pltpu.SemaphoreType.DMA((len(plan), grid.slots)),
            pltpu.SemaphoreType.DMA((len(plan), grid.slots)),
            pltpu.SemaphoreType.DMA((views_count,)),
            pltpu.SemaphoreType.DMA((views_count,)),
            pltpu.SemaphoreType.DMA((14,)),
            pltpu.SemaphoreType.DMA((4, 2)),
        ]
        + bufs,
        compiler_params=pltpu.CompilerParams(
            collective_id=1, has_side_effects=True, vmem_limit_bytes=VMEM_LIMIT
        ),
        name="backward",
    )(length_of, partners.reshape(1, -1), firsts, *gains, *hbm)


def finish_kernel(count, *refs):
    wide, narrow, refs = refs[:count], refs[count : count + 3], refs[count + 3 :]
    wide_out, refs = refs[:count], refs[count:]
    vectors, (bias, loss), refs = refs[:-count - 4], refs[-count - 4 : -count - 2], refs[-count - 2 :]
    bufs, (in_sem, out_sem) = refs[:count], refs[count:]
    loads = [pltpu.make_async_copy(a, b, in_sem.at[i]) for i, (a, b) in enumerate(zip(wide, bufs))]
    stores = [pltpu.make_async_copy(b, a, out_sem.at[i]) for i, (a, b) in enumerate(zip(wide_out, bufs))]
    for c in loads:
        c.start()
    for j, ref in enumerate(vectors):
        ref[...] = narrow[0][j : j + 1, : ref.shape[1]]
    bias[...] = narrow[1][0:1, : bias.shape[1]]
    loss[...] = narrow[2][0:1, 0:1]
    for load, store in zip(loads, stores):
        load.wait()
        store.start()
    for c in stores:
        c.wait()


def finish(wide, narrow, sizes):
    vmem, anywhere = pl.BlockSpec(memory_space=pltpu.VMEM), pl.BlockSpec(memory_space=pl.ANY)
    shape, count = jax.ShapeDtypeStruct, len(wide)
    outs = pl.pallas_call(
        functools.partial(finish_kernel, count),
        out_shape=[shape(w.shape, w.dtype) for w in wide] + [shape((1, n), f32) for n in sizes] + [shape((1, 1), f32)],
        in_specs=[anywhere] * count + [vmem] * 3,
        out_specs=[anywhere] * count + [vmem] * (len(sizes) + 1),
        scratch_shapes=[pltpu.VMEM(w.shape, w.dtype) for w in wide] + [pltpu.SemaphoreType.DMA((count,))] * 2,
        name="results",
    )(*wide, *narrow)
    return outs[:count], [v.reshape(-1) for v in outs[count:-1]], outs[-1].reshape(())


def on_device(whole, grid, tokens, lengths, keep_attn, keep_ffn, partners, out_cot, *weights):
    (w_qkv, b_qv, w_out, b_out, ln1_gain, ln1_bias, w_up, b_up, w_down, b_down, ln2_gain, ln2_bias, w_pool, b_pool) = weights
    _, length, width = tokens.shape
    inner = w_up.shape[1]
    big = [w_qkv, w_out, w_up, w_down, w_pool]
    small = [b_qv, b_out, ln1_gain, ln1_bias, b_up, b_down, ln2_gain, ln2_bias, b_pool]
    shard_rows = w_qkv.shape[0]
    if not grid.with_fsdp:
        big = [lax.all_gather(w, "fsdp", axis=0, tiled=True) for w in big]
        small = [lax.all_gather(v, "fsdp", axis=0, tiled=True) for v in small]
    sizes = [v.shape[0] for v in small][:-1]
    flat = (length, width)
    keep_a, keep_f = keep_attn.reshape(flat), keep_ffn.reshape(flat)
    outs = run_forward(grid, lengths, tokens.reshape(flat), keep_a, keep_f, big, small)
    wq, wo, wu, wd, wp = (g.reshape(-1, g.shape[-1]) for g in outs[:5])
    qkv, context, lse, tokens_t, context_t, hidden_t, norm1, scale1, norm2, scale2, layer_out = outs[5:16]
    act_t, slope, firsts = outs[16:19]
    vectors = outs[19:]
    hbm = [
        out_cot.reshape(flat), keep_a, keep_f, norm1, scale1, norm2, scale2, act_t, slope, hidden_t, context_t,
        qkv, context, lse, tokens_t, wq, wo, wu, wd, wp,
    ]
    rq, ro, ru, rd, rs, pool_w, pool_b, loss, tokens_grad = run_backward(
        grid, whole, lengths, partners, firsts, [vectors[2], vectors[6]], hbm, length, width, inner, sizes, shard_rows
    )
    if grid.with_fsdp:
        wide, vectors, loss = finish([layer_out, tokens_grad, rq, ro, ru, rd, pool_w], [rs, pool_b, loss], sizes + [shard_rows])
        layer_out, tokens_grad, rq, ro, ru, rd, pool_w = wide
    else:
        owned = [rq, ro, ru, rd] + [rs[j, :n] for j, n in enumerate(sizes)]
        rq, ro, ru, rd, *vectors = [lax.psum_scatter(g, "fsdp", scatter_dimension=0, tiled=True) for g in owned]
        vectors, loss = vectors + [pool_b[0, :shard_rows]], loss[0, 0]
    s_qv, s_out, s_g1, s_b1, s_up, s_down, s_g2, s_b2, s_pool = vectors
    return (
        layer_out.reshape(tokens.shape), tokens_grad.reshape(tokens.shape), rq, s_qv, ro, s_out, s_g1, s_b1, ru, s_up,
        rd, s_down, s_g2, s_b2, pool_w, s_pool, loss,
    )


def solution(mesh):
    rows, vector, matrix = P(AXES, None, None), P(AXES), P(AXES, None)
    weights = (matrix, vector, matrix, vector, vector, vector, matrix, vector, matrix, vector, vector, vector, matrix, vector)
    devices = mesh.shape["dp"] * mesh.shape["fsdp"]

    def step(*args):
        whole = Grid(mesh)
        grid = whole if (args[6].shape[0] // devices) % 8 == 0 else Grid(mesh, False)
        return jax.shard_map(
            functools.partial(on_device, whole, grid),
            mesh=mesh,
            in_specs=(rows, vector, rows, rows, P(), rows) + weights,
            out_specs=(rows, rows) + weights + (P(),),
            check_vma=False,
        )(*args)

    return step
```

```python
import functools
import math

import jax
import jax.numpy as jnp
from jax import lax
from jax.experimental import pallas as pl
from jax.experimental.pallas import tpu as pltpu
from jax.sharding import PartitionSpec as P

HEAD_DIM = 64
LANES = 128
f32, bf16 = jnp.float32, jnp.bfloat16
MESH = pl.DeviceIdType.MESH
AXES = ("dp", "fsdp")
eps_norm = 1e-05
keep_scale = 1.0 / 0.9
logit_divisor = 0.05
neg_fill = -1000000000.0
VMEM_LIMIT = 67043328
DIMS = ("z", "c", "y", "x")
SPACING = 4
SHARES = (0.56, 0.64, 0.88)
GATHER_ORDERS = (("z", "x", "y", "c"), ("z", "y", "x", "c"))
SCATTER_ORDERS = (("c", "y", "x", "z"), ("c", "x", "y", "z"))


class Grid:
    def __init__(self, mesh, with_fsdp=True):
        dp, fsdp = mesh.shape["dp"], mesh.shape["fsdp"]
        cores = 2 if dp % 2 == 0 else 1
        side = math.isqrt(fsdp)
        if side * side != fsdp:
            side = fsdp
        self.with_fsdp = with_fsdp
        self.size = {
            "z": dp // cores,
            "c": cores,
            "y": fsdp // side if with_fsdp else 1,
            "x": side if with_fsdp else 1,
        }
        self.shape = tuple(self.size[d] for d in DIMS)
        self.count = math.prod(self.shape)
        self.slots = sum(n - 1 for n in self.shape)

    def me(self):
        dp, fsdp = lax.axis_index("dp"), lax.axis_index("fsdp")
        at = {"z": lax.div(dp, self.size["c"]), "c": lax.rem(dp, self.size["c"])}
        if self.with_fsdp:
            at["y"], at["x"] = lax.div(fsdp, self.size["x"]), lax.rem(fsdp, self.size["x"])
        else:
            at["y"], at["x"] = 0, 0
        return at

    def device(self, at):
        fsdp = at["y"] * self.size["x"] + at["x"] if self.with_fsdp else lax.axis_index("fsdp")
        return (at["z"] * self.size["c"] + at["c"], fsdp)

    def peer(self, at, dim, j):
        other = dict(at)
        other[dim] = lax.rem(at[dim] + j, self.size[dim])
        return other

    def slot(self, dim, j):
        base = 0
        for d in DIMS:
            if d == dim:
                return base + j - 1
            base += self.size[d] - 1

    def order(self, order):
        return tuple(d for d in order if self.size[d] > 1)

    def straight(self):
        return [{d: j} for d in DIMS for j in range(1, self.size[d])]

    def around(self, dims):
        offsets = [{}]
        for d in dims:
            offsets = [{**o, d: j} if j else o for o in offsets for j in range(self.size[d])]
        return [o for o in offsets if o]

    def moved(self, at, offset):
        return {d: lax.rem(at[d] + offset[d], self.size[d]) if d in offset else at[d] for d in DIMS}

    def barrier(self, offsets):
        at, sem = self.me(), pltpu.get_barrier_semaphore()
        for offset in offsets:
            pl.semaphore_signal(
                sem, inc=1, device_id=self.device(self.moved(at, offset)), device_id_type=MESH
            )
        pl.semaphore_wait(sem, len(offsets))


class Exchange:
    def __init__(self, grid, ref, send, recv):
        self.grid, self.ref, self.send, self.recv, self.at = grid, ref, send, recv, grid.me()
        self.groups = [("z", "c"), ("y", "x")]

    def copies(self, stage):
        done = self.groups[0] if stage else ()
        view = self.ref.at[tuple(slice(None) if d in done else self.at[d] for d in DIMS)]
        first = len(self.grid.around(self.groups[0])) if stage else 0
        for j, offset in enumerate(self.grid.around(self.groups[stage])):
            yield pltpu.make_async_remote_copy(
                src_ref=view,
                dst_ref=view,
                send_sem=self.send.at[first + j],
                recv_sem=self.recv.at[first + j],
                device_id=self.grid.device(self.grid.moved(self.at, offset)),
                device_id_type=MESH,
            )

    def start(self, stage):
        for copy in self.copies(stage):
            copy.start()

    def wait(self, stage):
        for copy in self.copies(stage):
            copy.wait_recv()

    def finish(self):
        for stage in range(2):
            for copy in self.copies(stage):
                copy.wait_send()


class Gather:
    def __init__(self, grid, pieces, send, recv, window=3, lag=3):
        self.grid, self.send, self.recv, self.at = grid, send, recv, grid.me()
        self.pieces = [(ref, sub, grid.order(order)) for ref, sub, order in pieces]
        self.stages, self.window, self.now = len(self.pieces[0][2]), window, 0
        self.events = [
            (step - stage * lag, stage)
            for step in range(len(pieces) + (self.stages - 1) * lag)
            for stage in range(self.stages)
            if 0 <= step - stage * lag < len(pieces)
        ]
        self.whole = [self.events.index((i, self.stages - 1)) + 1 for i in range(len(pieces))]

    def copies(self, i, stage):
        ref, sub, order = self.pieces[i]
        dim, done = order[stage], order[:stage]
        index = tuple(slice(None) if d in done else self.at[d] for d in DIMS)
        view = ref.at[index + sub]
        for j in range(1, self.grid.size[dim]):
            slot = self.grid.slot(dim, j)
            yield pltpu.make_async_remote_copy(
                src_ref=view,
                dst_ref=view,
                send_sem=self.send.at[i, slot],
                recv_sem=self.recv.at[i, slot],
                device_id=self.grid.device(self.grid.peer(self.at, dim, j)),
                device_id_type=MESH,
            )

    def start(self, i, stage):
        for copy in self.copies(i, stage):
            copy.start()

    def begin(self):
        for i in range(min(self.window, len(self.pieces))):
            self.start(i, 0)

    def run(self, first, last):
        for i, stage in self.events[first:last]:
            for copy in self.copies(i, stage):
                copy.wait_recv()
            if stage == 0 and i + self.window < len(self.pieces):
                self.start(i + self.window, 0)
            if stage < self.stages - 1:
                self.start(i, stage + 1)

    def until(self, last):
        self.run(self.now, max(self.now, last))
        self.now = max(self.now, last)

    def finish(self):
        self.until(len(self.events))
        for i in range(len(self.pieces)):
            for stage in range(self.stages):
                for copy in self.copies(i, stage):
                    copy.wait_send()

    def loop(self, count, marks, body):
        marks = [max(self.now, m) for m in marks]
        starts = [self.now] + marks[:-1]

        def step(t, _):
            for k in range(count):
                if marks[k] > starts[k]:

                    @pl.when(t == k)
                    def _():
                        self.run(starts[k], marks[k])

            body(t)
            return 0

        lax.fori_loop(0, count, step, 0)
        self.now = marks[-1]


class Scatter:
    def __init__(self, grid, pieces, send, recv):
        self.grid, self.send, self.recv, self.at = grid, send, recv, grid.me()
        self.pieces = [(src, sub, grid.order(order), bufs, out) for src, sub, order, bufs, out in pieces]
        self.stages = len(self.pieces[0][2])

    def pick(self, i, stage, where):
        src, sub, order, bufs, _ = self.pieces[i]
        left = tuple(d for d in DIMS if d not in order[:stage])
        index = tuple(where if d == order[stage] else slice(None) for d in left)
        if stage == 0:
            return src.at[index + sub]
        return bufs[stage - 1].at[(0,) + index]

    def copies(self, i, stage):
        _, _, order, bufs, _ = self.pieces[i]
        dim = order[stage]
        for j in range(1, self.grid.size[dim]):
            other = self.grid.peer(self.at, dim, j)
            slot = self.grid.slot(dim, j)
            yield pltpu.make_async_remote_copy(
                src_ref=self.pick(i, stage, other[dim]),
                dst_ref=bufs[stage].at[j - 1],
                send_sem=self.send.at[i, slot],
                recv_sem=self.recv.at[i, slot],
                device_id=self.grid.device(other),
                device_id_type=MESH,
            )

    def begin(self, i):
        for copy in self.copies(i, 0):
            copy.start()

    def run(self, events):
        for i, stage in events:
            self.add(i, stage)
            if stage < self.stages - 1:
                for copy in self.copies(i, stage + 1):
                    copy.start()

    def add(self, i, stage):
        _, _, order, bufs, out = self.pieces[i]
        for copy in self.copies(i, stage):
            copy.wait_recv()
        buf = bufs[stage]
        own = self.pick(i, stage, self.at[order[stage]])[...]
        if stage < self.stages - 1 and self.grid.size[order[stage]] == 2:
            buf[0] = own + buf[0]
            return
        total = own.astype(f32)
        for j in range(self.grid.size[order[stage]] - 1):
            total = total + buf[j].astype(f32)
        if stage == self.stages - 1:
            out[...] = total.reshape(out.shape)
        else:
            buf[0] = total.astype(buf.dtype)

    def finish(self):
        for i in range(len(self.pieces)):
            for stage in range(self.stages):
                for copy in self.copies(i, stage):
                    copy.wait_send()


def scatter_buffers(grid, order, rows, columns, dtype):
    shapes, left = [], list(DIMS)
    for d in grid.order(order):
        left.remove(d)
        shapes.append((grid.size[d] - 1,) + tuple(grid.size[e] for e in left) + (rows, columns))
    return [pltpu.VMEM(s, dtype) for s in shapes]


def cuts(total, parts, unit):
    while parts > 1 and total % (parts * unit):
        parts -= 1
    return [(j * (total // parts), total // parts) for j in range(parts)]


def dotg(a, b, ca, cb, precision=None):
    return lax.dot_general(
        a, b, (((ca,), (cb,)), ((), ())), preferred_element_type=f32, precision=precision
    )


def iota(shape, dim):
    return lax.broadcasted_iota(jnp.int32, shape, dim)


def three_parts(x):
    high = x.astype(bf16).astype(f32)
    mid = (x - high).astype(bf16).astype(f32)
    return high, mid, x - high - mid


def spread_vector(rows, n):
    shards, width = rows.shape
    total = shards * n
    place = (iota((width, total), 1) % n == iota((width, total), 0)).astype(f32).astype(bf16)
    wide = dotg(rows, place, 1, 0)
    keep = iota((shards, total), 1) // n == iota((shards, total), 0)
    return jnp.sum(jnp.where(keep, wide, 0.0), axis=0, keepdims=True)


def fold_vector(vector, shards, n, width):
    total = shards * n
    keep = iota((shards, total), 1) // n == iota((shards, total), 0)
    place = (iota((total, width), 0) % n == iota((total, width), 1)).astype(f32).astype(bf16)
    parts = [jnp.where(keep, part, 0.0).astype(bf16) for part in three_parts(vector)]
    return sum(dotg(part, place, 1, 0) for part in parts)


def attend_prepare(qkv_ref, prep, live, pair):
    length, width = qkv_ref.shape[0], qkv_ref.shape[1] // 3
    k = qkv_ref[:, pl.ds(pl.multiple_of(width + pair * LANES, LANES), LANES)].astype(f32)
    v = qkv_ref[:, pl.ds(pl.multiple_of(2 * width + pair * LANES, LANES), LANES)].astype(f32)
    lane, row = iota((length, LANES), 1), iota((length, LANES), 0)
    bias = jnp.where(row < live, 0.0, neg_fill)
    k = k * (1.0 / math.sqrt(HEAD_DIM))
    for h in range(2):
        mine, spare = lane // HEAD_DIM == h, HEAD_DIM * (1 - h)
        prep[h, 0] = jnp.where(mine, k, jnp.where(lane == spare, bias, 0.0)).astype(bf16)
        prep[h, 1] = jnp.where(mine, v, 1.0).astype(bf16)


def attend(qkv_ref, context_ref, lse_ref, prep, pair, rows, block):
    out = pl.ds(pl.multiple_of(pair * LANES, LANES), LANES)
    q = qkv_ref[rows, out].astype(f32)
    lane = iota((block, LANES), 1)
    low = lane < HEAD_DIM
    sums, tops = [], []
    for h in range(2):
        spare = HEAD_DIM * (1 - h)
        query = jnp.where(lane // HEAD_DIM == h, q, jnp.where(lane == spare, 1.0, 0.0)).astype(bf16)
        scores = dotg(query, prep[h, 0], 1, 1)
        top = jnp.max(scores, axis=1, keepdims=True)
        weights = jnp.exp(scores - top).astype(bf16)
        sums.append(dotg(weights, prep[h, 1], 1, 0))
        tops.append(top)
    num = jnp.where(low, sums[0], sums[1])
    den = pltpu.roll(jnp.where(low, sums[1], sums[0]), HEAD_DIM, 1)
    context_ref[rows, out] = (num / den).astype(bf16)
    total = jnp.where(low, tops[0], tops[1]) + jnp.log(den)
    other = pltpu.roll(total, HEAD_DIM, 1)
    kept = jnp.where(lane == 2 * pair + 1, other, lse_ref[rows, :])
    lse_ref[rows, :] = jnp.where(lane == 2 * pair, total, kept)


def gelu_parts(x):
    cdf = 0.5 * (1.0 + lax.erf(x * (1.0 / math.sqrt(2.0))))
    return cdf, jnp.exp(-0.5 * x * x) * (1.0 / math.sqrt(2.0 * math.pi))


def normalize(values):
    center = values - jnp.mean(values, axis=-1, keepdims=True)
    scale = lax.rsqrt(jnp.mean(center * center, axis=-1, keepdims=True) + eps_norm)
    return center * scale, scale


def gather_plan(shapes):
    plan, every = [("s", ())], slice(None)
    width = shapes["o"][1]
    for a, n in cuts(width, 3, LANES):
        plan += [("q", (every, pl.ds(part * width + a, n))) for part in range(3)]
    for name, parts in (("o", 2), ("u", 6), ("p", 2), ("d", 3)):
        rows, columns = shapes[name]
        for a, n in cuts(columns, parts, LANES):
            for b, m in cuts(rows, 2 if name == "d" else 1, 8):
                plan.append((name, (pl.ds(b, m) if name == "d" else every, pl.ds(a, n))))
    return [(name, sub, GATHER_ORDERS[i % len(GATHER_ORDERS)]) for i, (name, sub) in enumerate(plan)]


def forward_kernel(grid, plan, sizes, *refs):
    (len_ref, tokens_ref, keep_a, keep_f, wq, wo, wu, wd, wp), refs = refs[:9], refs[9:]
    count = len(sizes)
    small_in, refs = refs[:count], refs[count:]
    kept_hbm, (act_t, slope), refs = refs[:16], refs[16:18], refs[18:]
    firsts, small_out, refs = refs[0], refs[1 : 1 + count], refs[1 + count :]
    kept, refs = refs[:16], refs[16:]
    (gq, go, gu, gd, gp, qkv_ref, context, lse, tokens_t, context_t, hidden_t, norm1, scale1, norm2, scale2, layer_out) = kept
    (gs, keep, hidden, hidden_low, act, act_buf, slope_buf, prep, bias), refs = refs[:9], refs[9:]
    send, recv, own_sem, keep_sem, act_sem, slope_sem, out_sem = refs
    length, width = context.shape
    b_qv, b_out, g1, b1, b_up, b_down, g2, b2, b_pool = small_out
    outs = [pltpu.make_async_copy(src, dst, out_sem.at[i]) for i, (src, dst) in enumerate(zip(kept, kept_hbm))]

    def put(*which):
        for i, ref in enumerate(kept):
            if any(ref is w for w in which):
                outs[i].start()

    at = grid.me()
    own = tuple(at[d] for d in DIMS)
    load = pltpu.make_async_copy(keep_a, keep, keep_sem)
    load.start()
    to_own = []
    for i, (src, dst) in enumerate(((wq, gq), (wo, go), (wu, gu), (wd, gd), (wp, gp))):
        to_own.append(pltpu.make_async_copy(src, dst.at[own], own_sem.at[i]))
        to_own[-1].start()
    mine = gs.at[own]
    mine[...] = jnp.zeros(mine.shape, bf16)
    for i, (ref, n) in enumerate(zip(small_in, sizes)):
        mine[i : i + 1, 0:n] = ref[...]
    where = dict(q=gq, o=go, u=gu, d=gd, p=gp, s=gs)
    gather = Gather(grid, [(where[name], sub, order) for name, sub, order in plan], send, recv)
    number = {}
    for i, (name, _, _) in enumerate(plan):
        number.setdefault(name, []).append(i)
    end = {name: [gather.whole[i] for i in numbers] for name, numbers in number.items()}
    grid.barrier(grid.straight())
    for copy in to_own:
        copy.wait()
    gather.begin()
    tokens_t[...] = tokens_ref[...].T
    lse[...] = jnp.zeros_like(lse)
    put(tokens_t)
    gather.until(end["s"][0])
    rows = gs[...].reshape((grid.count,) + gs.shape[-2:])
    for i, (ref, n) in enumerate(zip(small_out, sizes)):
        ref[...] = spread_vector(rows[:, i, :], n)
    bias[:, :width] = b_qv[:, :width]
    bias[:, width : 2 * width] = jnp.zeros((1, width), f32)
    bias[:, 2 * width :] = b_qv[:, width:]

    groups = len(number["q"]) // 3
    part = width // groups
    pairs, block = part // LANES, min(512, length)
    blocks, live = length // block, len_ref[0]
    each = pairs * blocks

    def attention(t):
        @pl.when(t % each == 0)
        def _():
            for j in range(3):
                cols = pl.ds(pl.multiple_of(j * width + t // each * part, part), part)
                out = dotg(tokens_ref[...], gq[:, :, :, :, :, cols].reshape(width, part), 1, 0)
                qkv_ref[:, cols] = (out + bias[:, cols]).astype(bf16)

        @pl.when(t % blocks == 0)
        def _():
            attend_prepare(qkv_ref, prep, live, t // blocks)

        rows = pl.ds(pl.multiple_of((t % blocks) * block, block), block)
        attend(qkv_ref, context, lse, prep, t // blocks, rows, block)

    slots = groups * each
    first, total = end["q"][2], len(gather.events)

    def by_then(share):
        return first + int(share * (total - first))

    gather.loop(
        slots,
        [max(end["q"][3 * (t // each) + 2], by_then(SHARES[0] * t / slots)) for t in range(slots)],
        attention,
    )
    put(gq, qkv_ref, context, lse)

    load.wait()
    block = min(512, length)
    blocks = length // block

    def row_block(t):
        return pl.ds(pl.multiple_of(t * block, block), block)

    gather.until(end["o"][-1])

    def project(t):
        here = row_block(t)
        attended = dotg(context[here, :], go[...].reshape(width, width), 1, 0) + b_out[...]
        total = tokens_ref[here, :].astype(f32) + attended * (keep[here, :].astype(f32) * keep_scale)
        norm, scale = normalize(total)
        out = norm * g1[...] + b1[...]
        hidden[here, :] = out
        hidden_low[here, :] = out.astype(bf16)
        hidden_t[:, here] = out.astype(bf16).T
        context_t[:, here] = context[here, :].T
        norm1[here, :] = norm.astype(bf16)
        scale1[here, :] = jnp.broadcast_to(scale, (block, LANES))

    gather.loop(blocks, [by_then(SHARES[0] + (SHARES[1] - SHARES[0]) * t / blocks) for t in range(blocks)], project)
    load = pltpu.make_async_copy(keep_f, keep, keep_sem)
    load.start()
    put(go, hidden_t, context_t, norm1, scale1)

    parts = len(end["u"])
    step = gu.shape[-1] // parts
    strip = min(128, length)

    def saved(t, cols):
        yield pltpu.make_async_copy(act_buf.at[t % 2], act_t.at[cols, :], act_sem.at[t % 2])
        yield pltpu.make_async_copy(slope_buf.at[t % 2], slope.at[:, cols], slope_sem.at[t % 2])

    def up(t):
        cols = pl.ds(pl.multiple_of(t * step, step), step)
        weight = gu[:, :, :, :, :, cols].reshape(width, step)

        @pl.when(t >= 2)
        def _():
            for copy in saved(t, cols):
                copy.wait()

        for i in range(length // strip):
            here = slice(i * strip, (i + 1) * strip)
            pre = dotg(hidden_low[here, :], weight, 1, 0) + b_up[:, cols]
            cdf, pdf = gelu_parts(pre)
            out = (pre * cdf).astype(bf16)
            act[here, cols] = out
            act_buf[t % 2, :, here] = out.T
            slope_buf[t % 2, here, :] = (cdf + pre * pdf).astype(bf16)
        for copy in saved(t, cols):
            copy.start()

    gather.loop(parts, [max(end["u"][t], by_then(SHARES[1] + (SHARES[2] - SHARES[1]) * t / parts)) for t in range(parts)], up)
    for t in range(max(0, parts - 2), parts):
        for copy in saved(t, pl.ds(0, step)):
            copy.wait()

    load.wait()
    put(gu)
    halves = len(cuts(gd.shape[-2], 2, 8))
    ends = end["d"][halves - 1 :: halves]
    parts = len(ends)
    step = width // parts

    def down(t):
        cols = pl.ds(pl.multiple_of(t * step, step), step)
        out = dotg(act[...], gd[:, :, :, :, :, cols].reshape(-1, step), 1, 0) + b_down[:, cols]
        hidden[:, cols] += out * (keep[:, cols].astype(f32) * keep_scale)

    gather.loop(parts, ends, down)
    put(gd, gp)
    block = min(256, length)
    blocks = length // block

    def norm(t):
        here = row_block(t)
        value, scale = normalize(hidden[here, :])
        out = value * g2[...] + b2[...]
        norm2[here, :] = value.astype(bf16)
        scale2[here, :] = jnp.broadcast_to(scale, (block, LANES))
        layer_out[here, :] = out.astype(bf16)

        @pl.when(t == 0)
        def _():
            first = out[0:8].astype(bf16)
            pooled = jnp.tanh(dotg(first, gp[...].reshape(width, width), 1, 0) + b_pool[...])
            firsts[0:1, :] = pooled[0:1]
            firsts[1:2, :] = first[0:1].astype(f32)

    gather.loop(blocks, [gather.now] * blocks, norm)
    put(norm2, scale2, layer_out)
    gather.finish()
    for copy in outs:
        copy.wait()


def run_forward(grid, length_of, tokens, keep_a, keep_f, big, small):
    length, width = tokens.shape
    names = ("q", "o", "u", "d", "p")
    shapes = {k: w.shape for k, w in zip(names, big)}
    inner = shapes["u"][1]
    sizes = [v.shape[0] for v in small]
    plan = gather_plan(shapes)
    pad = -(-max(sizes) // LANES) * LANES
    step = inner // sum(p[0] == "u" for p in plan)
    vmem, anywhere = pl.BlockSpec(memory_space=pltpu.VMEM), pl.BlockSpec(memory_space=pl.ANY)
    shape = jax.ShapeDtypeStruct
    kept = [(grid.shape + shapes[k], bf16) for k in names] + [
        ((length, 3 * width), bf16),
        ((length, width), bf16),
        ((length, LANES), f32),
        ((width, length), bf16),
        ((width, length), bf16),
        ((width, length), bf16),
        ((length, width), bf16),
        ((length, LANES), f32),
        ((length, width), bf16),
        ((length, LANES), f32),
        ((length, width), bf16),
    ]
    return pl.pallas_call(
        functools.partial(forward_kernel, grid, plan, sizes),
        out_shape=[shape(*k) for k in kept]
        + [shape((inner, length), bf16), shape((length, inner), bf16), shape((2, width), f32)]
        + [shape((1, grid.count * n), f32) for n in sizes],
        in_specs=[pl.BlockSpec(memory_space=pltpu.SMEM), vmem, anywhere, anywhere] + [vmem] * (5 + len(small)),
        out_specs=[anywhere] * 18 + [vmem] * (1 + len(small)),
        scratch_shapes=[pltpu.VMEM(*k) for k in kept]
        + [
            pltpu.VMEM(grid.shape + (16, pad), bf16),
            pltpu.VMEM((length, width), jnp.int32),
            pltpu.VMEM((length, width), f32),
            pltpu.VMEM((length, width), bf16),
            pltpu.VMEM((length, inner), bf16),
            pltpu.VMEM((2, step, length), bf16),
            pltpu.VMEM((2, length, step), bf16),
            pltpu.VMEM((2, 2, length, LANES), bf16),
            pltpu.VMEM((1, 3 * width), f32),
            pltpu.SemaphoreType.DMA((len(plan), grid.slots)),
            pltpu.SemaphoreType.DMA((len(plan), grid.slots)),
            pltpu.SemaphoreType.DMA((5,)),
            pltpu.SemaphoreType.DMA,
            pltpu.SemaphoreType.DMA((2,)),
            pltpu.SemaphoreType.DMA((2,)),
            pltpu.SemaphoreType.DMA((16,)),
        ],
        compiler_params=pltpu.CompilerParams(
            collective_id=0, has_side_effects=True, vmem_limit_bytes=VMEM_LIMIT
        ),
        name="forward",
    )(length_of, tokens, keep_a, keep_f, *big, *[v.reshape(1, -1) for v in small])


def pool_and_loss(views, partners_ref, wp, here, shard_rows, unit_ref, work, cls_grad, pool_w, pool_b, loss):
    high = lax.Precision.HIGHEST
    count, width = math.prod(views.shape[:4]), views.shape[-1]
    each = count // views.shape[0]

    def pooled_rows(z):
        rows = views[z].reshape((each,) + views.shape[-2:])
        pooled = rows[:, 0, :]
        scale = lax.rsqrt(jnp.sum(pooled * pooled, axis=1, keepdims=True) + 1e-06)
        return slice(z * each, (z + 1) * each), pooled, scale, rows[:, 1, :]

    for z in range(views.shape[0]):
        at, pooled, scale, cls = pooled_rows(z)
        unit_ref[at, :] = pooled * scale
        work[count + z * each : count + (z + 1) * each, :] = cls.astype(bf16)
    unit = unit_ref[0:count, :]
    sims = dotg(unit, unit, 1, 1, high) / logit_divisor
    column, row = iota((count, count), 1), iota((count, count), 0)
    others = jnp.where(row == column, neg_fill, sims)
    top = jnp.max(others, axis=1, keepdims=True)
    weights = jnp.exp(others - top)
    total = jnp.sum(weights, axis=1, keepdims=True)
    partner = row == partners_ref[...]
    target = jnp.sum(jnp.where(partner, sims, 0.0), axis=1, keepdims=True)
    lost = jnp.sum(top + jnp.log(total) - target, axis=0, keepdims=True) / count
    loss[...] = jnp.broadcast_to(lost, loss.shape)
    pull = weights / total - jnp.where(partner, 1.0, 0.0)
    pull = pull + dotg(pull, (row == column).astype(f32), 0, 0, high)
    for z in range(views.shape[0]):
        at, pooled, scale, _ = pooled_rows(z)
        unit_grad = dotg(pull[at], unit, 1, 0, high) / logit_divisor
        along = jnp.sum(pooled * unit_grad, axis=1, keepdims=True)
        pooled_grad = scale * unit_grad - pooled * (scale * scale * scale * along)
        work[at, :] = (pooled_grad * (1.0 - pooled * pooled)).astype(bf16)
    pre, cls = work[0:count, :], work[count : 2 * count, :]
    mine = jnp.sum(jnp.where(iota((count, width), 0) == here, pre.astype(f32), 0.0), axis=0, keepdims=True)
    cls_grad[...] = dotg(jnp.broadcast_to(mine, (8, width)).astype(bf16), wp, 1, 1)
    place = (iota((width, LANES), 0) == here * shard_rows + iota((width, LANES), 1)).astype(f32).astype(bf16)
    cls_rows = dotg(cls, place, 1, 0).astype(bf16)
    pool_w[...] = dotg(cls_rows, pre, 0, 0)[:shard_rows]
    sums = jnp.broadcast_to(jnp.sum(pre.astype(f32), axis=0, keepdims=True), (8, width))
    pool_b[...] = sum(dotg(part.astype(bf16), place, 1, 0) for part in three_parts(sums))


def attend_back(qkv_ref, context, dcontext, lse, live, pair, prep):
    length, width = qkv_ref.shape[0], context.shape[1]
    scale = 1.0 / math.sqrt(HEAD_DIM)
    one = pl.ds(pl.multiple_of(pair * LANES, LANES), LANES)

    def col(part):
        return pl.ds(pl.multiple_of(part * width + pair * LANES, LANES), LANES)

    q, k, v = (qkv_ref[:, col(j)].astype(f32) for j in range(3))
    d = dcontext[:, one].astype(f32)
    lane, row = iota((length, LANES), 1), iota((length, LANES), 0)
    bias = jnp.where(row < live, 0.0, neg_fill)
    mine, place = lane // HEAD_DIM, lane % HEAD_DIM
    source, target = iota((LANES, LANES), 0), iota((LANES, LANES), 1)
    swap = (source // HEAD_DIM != target // HEAD_DIM).astype(f32).astype(bf16)
    both = d * context[:, one].astype(f32)
    inner = sum(dotg(part.astype(bf16), swap, 1, 0) for part in three_parts(both))
    d0, d1, d2 = three_parts(-inner)
    extra_d = jnp.where(place == 0, d0, jnp.where(place == 1, d1, jnp.where(place == 2, d2, 0.0)))
    extra_q = jnp.where(place == 0, 1.0, 0.0)
    for j, part in enumerate(three_parts(-lse[...])):
        head = jnp.where(target < HEAD_DIM, 2 * pair + 1, 2 * pair)
        pick = ((source == head) & (target % HEAD_DIM == j + 1)).astype(f32).astype(bf16)
        extra_q = extra_q + dotg(part.astype(bf16), pick, 1, 0)
    extra_k = jnp.where(place == 0, bias, jnp.where(place < 4, 1.0, 0.0))
    extra_v = jnp.where(place < 3, 1.0, 0.0)
    q = q * scale
    for h in range(2):
        here = mine == h
        prep[h, 0] = jnp.where(here, q, extra_q).astype(bf16)
        prep[h, 1] = jnp.where(here, k, extra_k).astype(bf16)
        prep[h, 2] = jnp.where(here, d, extra_d).astype(bf16)
        prep[h, 3] = jnp.where(here, v, extra_v).astype(bf16)
        prep[h, 4] = jnp.where(here, k * scale, 0.0).astype(bf16)
    return q.astype(bf16).T, d.astype(bf16).T


def scatter_plan(grid, shapes):
    plan, every = [], slice(None)
    width = shapes["o"][1]
    rows, columns = shapes["d"]
    plan += [("d", (pl.ds(a, n), every), n, columns) for a, n in cuts(rows, 6, 8)]
    for name, parts in (("u", 6), ("o", 2)):
        rows, columns = shapes[name]
        plan += [(name, (every, pl.ds(a, n)), rows, n) for a, n in cuts(columns, parts, LANES)]
    for a, n in cuts(width, 3, LANES):
        plan += [("q", (every, pl.ds(part * width + a, n)), shapes["q"][0], n) for part in range(3)]
    plan.append(("s", (), 16, shapes["s"]))
    return [(p[0], p[1], SCATTER_ORDERS[i % 2]) + p[2:] for i, p in enumerate(plan)]


def backward_kernel(grid, whole, plan, sizes, shard_rows, *refs):
    (len_ref, partners_ref, firsts, g1, g2), refs = refs[:5], refs[5:]
    (h_cot, h_keep_a, h_keep_f, h_norm1, h_scale1, h_norm2, h_scale2, h_act, h_slope, h_hidden, h_context_t), refs = refs[:11], refs[11:]
    (h_qkv, h_context, h_lse, h_tokens, h_wq, h_wo, h_wu, h_wd, h_wp), refs = refs[:9], refs[9:]
    (rq, ro, ru, rd, rs, pool_w, pool_b, loss, h_tokens_grad), refs = refs[:9], refs[9:]
    (dd, du, do, dsmall, grad, gctx, low, norm, keep, scale, vec, cls_grad, views, wp), refs = refs[:14], refs[14:]
    (send, recv, view_send, view_recv, sems, pair_sems), bufs = refs[:6], list(refs[6:])
    length, width = grad.shape
    inner = vec.shape[1]
    sources, results = dict(d=dd, u=du, o=do, s=dsmall), dict(d=rd, u=ru, o=ro, q=rq, s=rs)
    number = {}
    for i, p in enumerate(plan):
        number.setdefault(p[0], []).append(i)
    cot = low

    def copy(k, src, dst):
        return pltpu.make_async_copy(src, dst, sems.at[k])

    first_loads = [copy(0, h_cot, cot), copy(1, h_norm2, norm), copy(2, h_scale2, scale), copy(3, h_keep_f, keep), copy(4, h_wp, wp)]
    for c in first_loads:
        c.start()
    at_all = whole.me()
    views[tuple(at_all[d] for d in DIMS)] = firsts[...]
    exchange = Exchange(whole, views, view_send, view_recv)
    whole.barrier(whole.straight() + [o for o in whole.around(("z", "c")) + whole.around(("y", "x")) if len(o) > 1])
    exchange.start(0)
    vec[...] = jnp.zeros_like(vec)
    for c in first_loads:
        c.wait()
    strip = min(128, length)
    strips = length // strip

    def strip_of(t):
        return pl.ds(pl.multiple_of(t * strip, strip), strip)

    def add_row(j, x):
        vec[j : j + 1, : x.shape[1]] += jnp.sum(x, axis=0, keepdims=True)

    def norm_back(here, up, gain, slot):
        value = norm[here, :].astype(f32)
        scaled = up * gain[...]
        along = jnp.mean(scaled * value, axis=1, keepdims=True)
        back = scale[here, 0:1] * (scaled - jnp.mean(scaled, axis=1, keepdims=True) - value * along)
        add_row(slot, up * value)
        add_row(slot + 1, up)
        grad[here, :] = back
        out = (back * (keep[here, :].astype(f32) * keep_scale)).astype(bf16)
        low[here, :] = out
        return out.astype(f32)

    def second_norm(t, extra):
        here = strip_of(t)
        up = cot[here, :].astype(f32)
        if extra is not None:
            up = up + jnp.where(iota((strip, width), 0) + t * strip == 0, extra, 0.0)
        add_row(5, norm_back(here, up, g2, 6))
        return 0

    held = -(-math.prod(whole.shape) // strip)
    def rest_of_norm(t, _):
        @pl.when(t == (held + strips) // 2)
        def _():
            exchange.wait(0)
            exchange.start(1)

        return second_norm(t, None)

    lax.fori_loop(held, strips, rest_of_norm, 0)
    exchange.wait(1)
    here = lax.axis_index("dp") * (whole.size["y"] * whole.size["x"]) + lax.axis_index("fsdp")
    pool_and_loss(views, partners_ref, wp[...], here, shard_rows, grad, gctx, cls_grad, pool_w, pool_b, loss)
    lax.fori_loop(0, held, lambda t, _: second_norm(t, cls_grad[0:1, :]), 0)
    wo = wp
    second_loads = [copy(1, h_norm1, norm), copy(2, h_scale1, scale), copy(3, h_keep_a, keep), copy(6, h_wo, wo)]
    for c in second_loads:
        c.start()

    pieces, left = [], bufs
    for name, sub, order, _, _ in plan:
        n = len(grid.order(order))
        pieces.append([sources.get(name), sub, order, left[:n], results[name].at[sub] if sub else results[name]])
        left = left[n:]
    groups = len(number["q"]) // 3
    early, last = len(plan) - 1 - len(number["q"]), len(plan) - 1
    scatter = Scatter(grid, pieces, send, recv)
    stages, lag = scatter.stages, 4
    steps = [
        [(j - stage * lag, stage) for stage in range(stages) if 0 <= j - stage * lag < early]
        for j in range(early + (stages - 1) * lag)
    ]

    def feed_forward(act, slope, wd, wu, gup, turned):
        third = [copy(5, h_hidden, turned), copy(7, h_context_t, turned)]
        third[0].start()
        block = min(256, length)
        chunk, part = act.shape[1], slope.shape[2]
        chunks, parts = inner // chunk, inner // part
        slab = wu.shape[1]

        def act_load(t):
            return pltpu.make_async_copy(h_act.at[pl.ds(pl.multiple_of(t * chunk, chunk), chunk), :], act.at[t % 2], pair_sems.at[0, t % 2])

        def part_loads(t):
            cols = pl.ds(pl.multiple_of(t * part, part), part)
            yield pltpu.make_async_copy(h_slope.at[:, cols], slope.at[t % 2], pair_sems.at[1, t % 2])
            yield pltpu.make_async_copy(h_wd.at[cols, :], wd.at[t % 2], pair_sems.at[2, t % 2])

        def slab_load(t):
            return pltpu.make_async_copy(h_wu.at[pl.ds(pl.multiple_of(t * slab, slab), slab), :], wu.at[t % 2], pair_sems.at[3, t % 2])

        act_load(0).start()
        for c in part_loads(0):
            c.start()
        slab_load(0).start()
        across = grid.size["y"] * grid.size["x"]

        def down_weight(t, _):
            @pl.when(t + 1 < chunks)
            def _():
                act_load(t + 1).start()

            act_load(t).wait()
            out = dotg(act[t % 2], low[...], 1, 0).astype(bf16)
            dd[t // grid.size["c"], t % grid.size["c"]] = out.reshape(dd.shape[2:])
            return 0

        lax.fori_loop(0, chunks, down_weight, 0)
        for i in number["d"]:
            scatter.begin(i)
        third[0].wait()

        def up_part(t, _):
            cols = pl.ds(pl.multiple_of(t * part, part), part)

            @pl.when(t + 1 < parts)
            def _():
                for c in part_loads(t + 1):
                    c.start()

            for c in part_loads(t):
                c.wait()
            for i in range(length // block):
                rows = slice(i * block, (i + 1) * block)
                out = dotg(low[rows, :], wd[t % 2], 1, 1) * slope[t % 2, rows, :].astype(f32)
                gup[rows, cols] = out.astype(bf16)
            vec[4:5, cols] = jnp.sum(gup[:, cols].astype(f32), axis=0, keepdims=True)
            out = dotg(turned[...], gup[:, cols], 1, 0).astype(bf16)
            du[:, :, :, :, :, cols] = out.reshape(grid.shape + (-1, part))
            for k, i in enumerate(number["u"]):

                @pl.when(t == k)
                def _():
                    scatter.begin(i)
                    scatter.run(steps[k])

            return 0

        lax.fori_loop(0, parts, up_part, 0)
        third[1].start()

        def hidden_part(t, _):
            cols = pl.ds(pl.multiple_of(t * slab, slab), slab)

            @pl.when(t + 1 < width // slab)
            def _():
                slab_load(t + 1).start()

            slab_load(t).wait()
            grad[:, cols] += dotg(gup[...], wu[t % 2], 1, 1)
            for k in range(width // slab):

                @pl.when(t == k)
                def _():
                    scatter.run(steps[parts + k])

            return 0

        lax.fori_loop(0, width // slab, hidden_part, 0)
        for c in second_loads:
            c.wait()

        def first_norm(t, _):
            add_row(1, norm_back(strip_of(t), grad[strip_of(t), :], g1, 2))
            return 0

        lax.fori_loop(0, strips, first_norm, 0)
        for c in (copy(9, h_context, norm), copy(10, h_lse, scale)):
            c.start()
        third[1].wait()
        for i in number["o"]:
            cols = plan[i][1][1]
            out = dotg(turned[...], low[:, cols], 1, 0).astype(bf16)
            do[:, :, :, :, :, cols] = out.reshape(grid.shape + (-1, cols.size))
            scatter.begin(i)
        for i in range(length // block):
            rows = slice(i * block, (i + 1) * block)
            gctx[rows, :] = dotg(low[rows, :], wo[...], 1, 1).astype(bf16)
        scatter.run(steps[parts + width // slab])
        return parts + width // slab + 1

    chunk, part, slab = inner // (grid.size["z"] * grid.size["c"]), inner // len(number["u"]), width // 3
    done = []

    def first_scope(*refs):
        done.append(feed_forward(*refs))

    pl.run_scoped(
        first_scope,
        pltpu.VMEM((2, chunk, length), bf16),
        pltpu.VMEM((2, length, part), bf16),
        pltpu.VMEM((2, part, width), bf16),
        pltpu.VMEM((2, slab, inner), bf16),
        pltpu.VMEM((length, inner), bf16),
        pltpu.VMEM((width, length), bf16),
    )
    step = done[0]

    def attention(qkv, tokens_t, wq, dq, prep, turned, acc):
        context, lse = norm, scale
        block = min(256, length) if grid.with_fsdp else min(128, length)
        blocks = length // block

        def rows_of(t):
            return pl.ds(pl.multiple_of(t * block, block), block)

        for i in number["q"]:
            scatter.pieces[i] = (dq,) + scatter.pieces[i][1:]
        span = width // groups

        def group_loads(g):
            for j in range(3):
                cols = pl.ds(j * width + g * span, span)
                yield pltpu.make_async_copy(h_qkv.at[:, cols], qkv.at[:, cols], pair_sems.at[j, g % 2])

        for g in range(min(2, groups)):
            for c in group_loads(g):
                c.start()
        loads = [copy(11, h_tokens, tokens_t), copy(12, h_wq.at[:, 0:width], wp)]
        loads += [copy(6, h_wq.at[:, width : 2 * width], wq.at[0]), copy(7, h_wq.at[:, 2 * width :], wq.at[1])]
        for c in loads:
            c.start()
        for c in (copy(9, h_context, norm), copy(10, h_lse, scale)):
            c.wait()
        each = span // LANES * blocks
        slots = groups * each
        live = len_ref[0]
        head = [slice(h * HEAD_DIM, (h + 1) * HEAD_DIM) for h in range(2)]
        due, late = [[] for _ in range(slots)], []
        for j, events in enumerate(steps[step:]):
            due[j * (slots - each // 2) // (len(steps) - step)] += events
        for g in range(groups - 1):
            for stage in range(stages):
                at, events = each * (g + 1) - 1 + SPACING * (stage + 1), [(i, stage) for i in number["q"][3 * g : 3 * g + 3]]
                if at < slots:
                    due[at] += events
                else:
                    late.append(events)
        tail = [late[j] if j < len(late) else [] for j in range(max(stages, len(late)))]
        for stage in range(stages):
            tail[len(tail) - stages + stage] += [(i, stage) for i in number["q"][-3:] + [last]]

        def slot(t, _):
            pair, b = t // blocks, t % blocks
            rows = rows_of(b)
            one = pl.ds(pl.multiple_of(pair * LANES, LANES), LANES)

            for g in range(groups):

                @pl.when(t == g * each)
                def _():
                    for c in group_loads(g):
                        c.wait()
                    if g + 2 < groups:
                        for c in group_loads(g + 2):
                            c.start()

            @pl.when(b == 0)
            def _():
                turned[0], turned[1] = attend_back(qkv, context, gctx, lse, live, pair, prep)
                acc[...] = jnp.zeros_like(acc)

            dq_rows = jnp.zeros((block, LANES), f32)
            for h in range(2):
                p = jnp.exp(dotg(prep[h, 0, rows, :], prep[h, 1], 1, 1))
                dp = dotg(prep[h, 2, rows, :], prep[h, 3], 1, 1)
                ds = (p * dp).astype(bf16)
                acc[0, head[h], :] += dotg(turned[1, head[h], rows], p.astype(bf16), 1, 0)
                acc[1, head[h], :] += dotg(turned[0, head[h], rows], ds, 1, 0)
                dq_rows = dq_rows + dotg(ds, prep[h, 4], 1, 0)
            qkv[rows, one] = dq_rows.astype(bf16)

            @pl.when(b == blocks - 1)
            def _():
                qkv[:, pl.ds(pl.multiple_of(width + pair * LANES, LANES), LANES)] = acc[1].astype(bf16).T
                qkv[:, pl.ds(pl.multiple_of(2 * width + pair * LANES, LANES), LANES)] = acc[0].astype(bf16).T

            for k in range(slots):
                if due[k]:

                    @pl.when(t == k)
                    def _():
                        scatter.run(due[k])

            @pl.when(t == each - 1)
            def _():
                loads[0].wait()

            @pl.when(t % each == each - 1)
            def _():
                for j in range(3):
                    cols = pl.ds(pl.multiple_of(j * width + t // each * span, LANES), span)
                    out = dotg(tokens_t[...], qkv[:, cols], 1, 0).astype(bf16)
                    dq[:, :, :, :, :, cols] = out.reshape(grid.shape + (-1, span))
                for g in range(groups):

                    @pl.when(t == each * (g + 1) - 1)
                    def _():
                        for i in number["q"][3 * g : 3 * g + 3]:
                            scatter.begin(i)

            return 0

        lax.fori_loop(0, slots, slot, 0)
        sums = dotg(jnp.ones((8, length), bf16), qkv[...], 1, 0)[0:1]
        vec[0:1, :width] = sums[:, :width]
        vec[0:1, width : 2 * width] = sums[:, 2 * width :]
        pad = dsmall.shape[-1]
        dsmall[...] = jnp.zeros_like(dsmall)
        for j, n in enumerate(sizes):
            folded = fold_vector(vec[j : j + 1, : grid.count * n], grid.count, n, pad)
            dsmall[:, :, :, :, j, :] = folded.reshape(grid.shape + (pad,))
        scatter.begin(number["s"][0])
        for c in loads[1:]:
            c.wait()
        rows = length // len(tail)
        for i, events in enumerate(tail):
            here = slice(i * rows, (i + 1) * rows)
            total = grad[here, :] + dotg(qkv[here, :width], wp[...], 1, 1)
            for j in range(2):
                total = total + dotg(qkv[here, (j + 1) * width : (j + 2) * width], wq[j], 1, 1)
            low[here, :] = total.astype(bf16)
            scatter.run(events)
        out = copy(13, low, h_tokens_grad)
        out.start()
        scatter.finish()
        exchange.finish()
        out.wait()

    pl.run_scoped(
        attention,
        pltpu.VMEM((length, 3 * width), bf16),
        pltpu.VMEM((width, length), bf16),
        pltpu.VMEM((2, width, width), bf16),
        pltpu.VMEM(grid.shape + (width // grid.count, 3 * width), bf16),
        pltpu.VMEM((2, 5, length, LANES), bf16),
        pltpu.VMEM((2, LANES, length), bf16),
        pltpu.VMEM((2, LANES, length), f32),
    )


def run_backward(grid, whole, length_of, partners, firsts, gains, hbm, length, width, inner, sizes, shard_rows):
    rows = width // grid.count
    pad = -(-max(sizes) // LANES) * LANES
    shapes = {"q": (rows, 3 * width), "o": (rows, width), "u": (rows, inner), "d": (inner // grid.count, width), "s": pad}
    plan = scatter_plan(grid, shapes)
    bufs = []
    for name, _, order, r, c in plan:
        bufs += scatter_buffers(grid, order, r, c, f32 if name == "s" else bf16)
    views_count = len(whole.around(("z", "c"))) + len(whole.around(("y", "x")))
    vmem, anywhere = pl.BlockSpec(memory_space=pltpu.VMEM), pl.BlockSpec(memory_space=pl.ANY)
    shape = jax.ShapeDtypeStruct
    return pl.pallas_call(
        functools.partial(backward_kernel, grid, whole, plan, sizes, shard_rows),
        out_shape=[shape(shapes[k], f32) for k in ("q", "o", "u", "d")]
        + [
            shape((16, pad), f32),
            shape((shard_rows, width), f32),
            shape((8, LANES), f32),
            shape((8, LANES), f32),
            shape((length, width), bf16),
        ],
        in_specs=[pl.BlockSpec(memory_space=pltpu.SMEM)] + [vmem] * 4 + [anywhere] * len(hbm),
        out_specs=[vmem] * 8 + [anywhere],
        scratch_shapes=[pltpu.VMEM(grid.shape + shapes[k], bf16) for k in ("d", "u", "o")]
        + [
            pltpu.VMEM(grid.shape + (16, pad), f32),
            pltpu.VMEM((length, width), f32),
            pltpu.VMEM((length, width), bf16),
            pltpu.VMEM((length, width), bf16),
            pltpu.VMEM((length, width), bf16),
            pltpu.VMEM((length, width), jnp.int32),
            pltpu.VMEM((length, LANES), f32),
            pltpu.VMEM((16, inner), f32),
            pltpu.VMEM((8, width), f32),
            pltpu.VMEM(whole.shape + (2, width), f32),
            pltpu.VMEM((width, width), bf16),
            pltpu.SemaphoreType.DMA((len(plan), grid.slots)),
            pltpu.SemaphoreType.DMA((len(plan), grid.slots)),
            pltpu.SemaphoreType.DMA((views_count,)),
            pltpu.SemaphoreType.DMA((views_count,)),
            pltpu.SemaphoreType.DMA((14,)),
            pltpu.SemaphoreType.DMA((4, 2)),
        ]
        + bufs,
        compiler_params=pltpu.CompilerParams(
            collective_id=1, has_side_effects=True, vmem_limit_bytes=VMEM_LIMIT
        ),
        name="backward",
    )(length_of, partners.reshape(1, -1), firsts, *gains, *hbm)


def finish_kernel(count, *refs):
    wide, narrow, refs = refs[:count], refs[count : count + 3], refs[count + 3 :]
    wide_out, refs = refs[:count], refs[count:]
    vectors, (bias, loss), refs = refs[:-count - 4], refs[-count - 4 : -count - 2], refs[-count - 2 :]
    bufs, (in_sem, out_sem) = refs[:count], refs[count:]
    loads = [pltpu.make_async_copy(a, b, in_sem.at[i]) for i, (a, b) in enumerate(zip(wide, bufs))]
    stores = [pltpu.make_async_copy(b, a, out_sem.at[i]) for i, (a, b) in enumerate(zip(wide_out, bufs))]
    for c in loads:
        c.start()
    for j, ref in enumerate(vectors):
        ref[...] = narrow[0][j : j + 1, : ref.shape[1]]
    bias[...] = narrow[1][0:1, : bias.shape[1]]
    loss[...] = narrow[2][0:1, 0:1]
    for load, store in zip(loads, stores):
        load.wait()
        store.start()
    for c in stores:
        c.wait()


def finish(wide, narrow, sizes):
    vmem, anywhere = pl.BlockSpec(memory_space=pltpu.VMEM), pl.BlockSpec(memory_space=pl.ANY)
    shape, count = jax.ShapeDtypeStruct, len(wide)
    outs = pl.pallas_call(
        functools.partial(finish_kernel, count),
        out_shape=[shape(w.shape, w.dtype) for w in wide] + [shape((1, n), f32) for n in sizes] + [shape((1, 1), f32)],
        in_specs=[anywhere] * count + [vmem] * 3,
        out_specs=[anywhere] * count + [vmem] * (len(sizes) + 1),
        scratch_shapes=[pltpu.VMEM(w.shape, w.dtype) for w in wide] + [pltpu.SemaphoreType.DMA((count,))] * 2,
        name="results",
    )(*wide, *narrow)
    return outs[:count], [v.reshape(-1) for v in outs[count:-1]], outs[-1].reshape(())


def on_device(whole, grid, tokens, lengths, keep_attn, keep_ffn, partners, out_cot, *weights):
    (w_qkv, b_qv, w_out, b_out, ln1_gain, ln1_bias, w_up, b_up, w_down, b_down, ln2_gain, ln2_bias, w_pool, b_pool) = weights
    _, length, width = tokens.shape
    inner = w_up.shape[1]
    big = [w_qkv, w_out, w_up, w_down, w_pool]
    small = [b_qv, b_out, ln1_gain, ln1_bias, b_up, b_down, ln2_gain, ln2_bias, b_pool]
    shard_rows = w_qkv.shape[0]
    if not grid.with_fsdp:
        big = [lax.all_gather(w, "fsdp", axis=0, tiled=True) for w in big]
        small = [lax.all_gather(v, "fsdp", axis=0, tiled=True) for v in small]
    sizes = [v.shape[0] for v in small][:-1]
    flat = (length, width)
    keep_a, keep_f = keep_attn.reshape(flat), keep_ffn.reshape(flat)
    outs = run_forward(grid, lengths, tokens.reshape(flat), keep_a, keep_f, big, small)
    wq, wo, wu, wd, wp = (g.reshape(-1, g.shape[-1]) for g in outs[:5])
    qkv, context, lse, tokens_t, context_t, hidden_t, norm1, scale1, norm2, scale2, layer_out = outs[5:16]
    act_t, slope, firsts = outs[16:19]
    vectors = outs[19:]
    hbm = [
        out_cot.reshape(flat), keep_a, keep_f, norm1, scale1, norm2, scale2, act_t, slope, hidden_t, context_t,
        qkv, context, lse, tokens_t, wq, wo, wu, wd, wp,
    ]
    rq, ro, ru, rd, rs, pool_w, pool_b, loss, tokens_grad = run_backward(
        grid, whole, lengths, partners, firsts, [vectors[2], vectors[6]], hbm, length, width, inner, sizes, shard_rows
    )
    if grid.with_fsdp:
        wide, vectors, loss = finish([layer_out, tokens_grad, rq, ro, ru, rd, pool_w], [rs, pool_b, loss], sizes + [shard_rows])
        layer_out, tokens_grad, rq, ro, ru, rd, pool_w = wide
    else:
        owned = [rq, ro, ru, rd] + [rs[j, :n] for j, n in enumerate(sizes)]
        rq, ro, ru, rd, *vectors = [lax.psum_scatter(g, "fsdp", scatter_dimension=0, tiled=True) for g in owned]
        vectors, loss = vectors + [pool_b[0, :shard_rows]], loss[0, 0]
    s_qv, s_out, s_g1, s_b1, s_up, s_down, s_g2, s_b2, s_pool = vectors
    return (
        layer_out.reshape(tokens.shape), tokens_grad.reshape(tokens.shape), rq, s_qv, ro, s_out, s_g1, s_b1, ru, s_up,
        rd, s_down, s_g2, s_b2, pool_w, s_pool, loss,
    )


def solution(mesh):
    rows, vector, matrix = P(AXES, None, None), P(AXES), P(AXES, None)
    weights = (matrix, vector, matrix, vector, vector, vector, matrix, vector, matrix, vector, vector, vector, matrix, vector)
    devices = mesh.shape["dp"] * mesh.shape["fsdp"]

    def step(*args):
        whole = Grid(mesh)
        grid = whole if (args[6].shape[0] // devices) % 8 == 0 else Grid(mesh, False)
        return jax.shard_map(
            functools.partial(on_device, whole, grid),
            mesh=mesh,
            in_specs=(rows, vector, rows, rows, P(), rows) + weights,
            out_specs=(rows, rows) + weights + (P(),),
            check_vma=False,
        )(*args)

    return step
```

```python
import functools
import math

import jax
import jax.numpy as jnp
from jax import lax
from jax.experimental import pallas as pl
from jax.experimental.pallas import tpu as pltpu
from jax.sharding import PartitionSpec as P

HEAD_DIM = 64
LANES = 128
f32, bf16 = jnp.float32, jnp.bfloat16
MESH = pl.DeviceIdType.MESH
AXES = ("dp", "fsdp")
eps_norm = 1e-05
keep_scale = 1.0 / 0.9
logit_divisor = 0.05
neg_fill = -1000000000.0
VMEM_LIMIT = 67043328
DIMS = ("z", "c", "y", "x")
SPACING = 4
SHARES = (0.56, 0.64, 0.88)
GATHER_ORDERS = (("z", "x", "y", "c"), ("z", "y", "x", "c"))
SCATTER_ORDERS = (("c", "y", "x", "z"), ("c", "x", "y", "z"))


class Grid:
    def __init__(self, mesh, with_fsdp=True):
        dp, fsdp = mesh.shape["dp"], mesh.shape["fsdp"]
        cores = 2 if dp % 2 == 0 else 1
        side = math.isqrt(fsdp)
        if side * side != fsdp:
            side = fsdp
        self.with_fsdp = with_fsdp
        self.size = {
            "z": dp // cores,
            "c": cores,
            "y": fsdp // side if with_fsdp else 1,
            "x": side if with_fsdp else 1,
        }
        self.shape = tuple(self.size[d] for d in DIMS)
        self.count = math.prod(self.shape)
        self.slots = sum(n - 1 for n in self.shape)

    def me(self):
        dp, fsdp = lax.axis_index("dp"), lax.axis_index("fsdp")
        at = {"z": lax.div(dp, self.size["c"]), "c": lax.rem(dp, self.size["c"])}
        if self.with_fsdp:
            at["y"], at["x"] = lax.div(fsdp, self.size["x"]), lax.rem(fsdp, self.size["x"])
        else:
            at["y"], at["x"] = 0, 0
        return at

    def device(self, at):
        fsdp = at["y"] * self.size["x"] + at["x"] if self.with_fsdp else lax.axis_index("fsdp")
        return (at["z"] * self.size["c"] + at["c"], fsdp)

    def peer(self, at, dim, j):
        other = dict(at)
        other[dim] = lax.rem(at[dim] + j, self.size[dim])
        return other

    def slot(self, dim, j):
        base = 0
        for d in DIMS:
            if d == dim:
                return base + j - 1
            base += self.size[d] - 1

    def order(self, order):
        return tuple(d for d in order if self.size[d] > 1)

    def straight(self):
        return [{d: j} for d in DIMS for j in range(1, self.size[d])]

    def around(self, dims):
        offsets = [{}]
        for d in dims:
            offsets = [{**o, d: j} if j else o for o in offsets for j in range(self.size[d])]
        return [o for o in offsets if o]

    def moved(self, at, offset):
        return {d: lax.rem(at[d] + offset[d], self.size[d]) if d in offset else at[d] for d in DIMS}

    def barrier(self, offsets):
        at, sem = self.me(), pltpu.get_barrier_semaphore()
        for offset in offsets:
            pl.semaphore_signal(
                sem, inc=1, device_id=self.device(self.moved(at, offset)), device_id_type=MESH
            )
        pl.semaphore_wait(sem, len(offsets))


class Exchange:
    def __init__(self, grid, ref, send, recv):
        self.grid, self.ref, self.send, self.recv, self.at = grid, ref, send, recv, grid.me()
        self.groups = [("z", "c"), ("y", "x")]

    def copies(self, stage):
        done = self.groups[0] if stage else ()
        view = self.ref.at[tuple(slice(None) if d in done else self.at[d] for d in DIMS)]
        first = len(self.grid.around(self.groups[0])) if stage else 0
        for j, offset in enumerate(self.grid.around(self.groups[stage])):
            yield pltpu.make_async_remote_copy(
                src_ref=view,
                dst_ref=view,
                send_sem=self.send.at[first + j],
                recv_sem=self.recv.at[first + j],
                device_id=self.grid.device(self.grid.moved(self.at, offset)),
                device_id_type=MESH,
            )

    def start(self, stage):
        for copy in self.copies(stage):
            copy.start()

    def wait(self, stage):
        for copy in self.copies(stage):
            copy.wait_recv()

    def finish(self):
        for stage in range(2):
            for copy in self.copies(stage):
                copy.wait_send()


class Gather:
    def __init__(self, grid, pieces, send, recv, window=3, lag=3):
        self.grid, self.send, self.recv, self.at = grid, send, recv, grid.me()
        self.pieces = [(ref, sub, grid.order(order)) for ref, sub, order in pieces]
        self.stages, self.window, self.now = len(self.pieces[0][2]), window, 0
        self.events = [
            (step - stage * lag, stage)
            for step in range(len(pieces) + (self.stages - 1) * lag)
            for stage in range(self.stages)
            if 0 <= step - stage * lag < len(pieces)
        ]
        self.whole = [self.events.index((i, self.stages - 1)) + 1 for i in range(len(pieces))]

    def copies(self, i, stage):
        ref, sub, order = self.pieces[i]
        dim, done = order[stage], order[:stage]
        index = tuple(slice(None) if d in done else self.at[d] for d in DIMS)
        view = ref.at[index + sub]
        for j in range(1, self.grid.size[dim]):
            slot = self.grid.slot(dim, j)
            yield pltpu.make_async_remote_copy(
                src_ref=view,
                dst_ref=view,
                send_sem=self.send.at[i, slot],
                recv_sem=self.recv.at[i, slot],
                device_id=self.grid.device(self.grid.peer(self.at, dim, j)),
                device_id_type=MESH,
            )

    def start(self, i, stage):
        for copy in self.copies(i, stage):
            copy.start()

    def begin(self):
        for i in range(min(self.window, len(self.pieces))):
            self.start(i, 0)

    def run(self, first, last):
        for i, stage in self.events[first:last]:
            for copy in self.copies(i, stage):
                copy.wait_recv()
            if stage == 0 and i + self.window < len(self.pieces):
                self.start(i + self.window, 0)
            if stage < self.stages - 1:
                self.start(i, stage + 1)

    def until(self, last):
        self.run(self.now, max(self.now, last))
        self.now = max(self.now, last)

    def finish(self):
        self.until(len(self.events))
        for i in range(len(self.pieces)):
            for stage in range(self.stages):
                for copy in self.copies(i, stage):
                    copy.wait_send()

    def loop(self, count, marks, body):
        marks = [max(self.now, m) for m in marks]
        starts = [self.now] + marks[:-1]

        def step(t, _):
            for k in range(count):
                if marks[k] > starts[k]:

                    @pl.when(t == k)
                    def _():
                        self.run(starts[k], marks[k])

            body(t)
            return 0

        lax.fori_loop(0, count, step, 0)
        self.now = marks[-1]


class Scatter:
    def __init__(self, grid, pieces, send, recv):
        self.grid, self.send, self.recv, self.at = grid, send, recv, grid.me()
        self.pieces = [(src, sub, grid.order(order), bufs, out) for src, sub, order, bufs, out in pieces]
        self.stages = len(self.pieces[0][2])

    def pick(self, i, stage, where):
        src, sub, order, bufs, _ = self.pieces[i]
        left = tuple(d for d in DIMS if d not in order[:stage])
        index = tuple(where if d == order[stage] else slice(None) for d in left)
        if stage == 0:
            return src.at[index + sub]
        return bufs[stage - 1].at[(0,) + index]

    def copies(self, i, stage):
        _, _, order, bufs, _ = self.pieces[i]
        dim = order[stage]
        for j in range(1, self.grid.size[dim]):
            other = self.grid.peer(self.at, dim, j)
            slot = self.grid.slot(dim, j)
            yield pltpu.make_async_remote_copy(
                src_ref=self.pick(i, stage, other[dim]),
                dst_ref=bufs[stage].at[j - 1],
                send_sem=self.send.at[i, slot],
                recv_sem=self.recv.at[i, slot],
                device_id=self.grid.device(other),
                device_id_type=MESH,
            )

    def begin(self, i):
        for copy in self.copies(i, 0):
            copy.start()

    def run(self, events):
        for i, stage in events:
            self.add(i, stage)
            if stage < self.stages - 1:
                for copy in self.copies(i, stage + 1):
                    copy.start()

    def add(self, i, stage):
        _, _, order, bufs, out = self.pieces[i]
        for copy in self.copies(i, stage):
            copy.wait_recv()
        buf = bufs[stage]
        own = self.pick(i, stage, self.at[order[stage]])[...]
        if stage < self.stages - 1 and self.grid.size[order[stage]] == 2:
            buf[0] = own + buf[0]
            return
        total = own.astype(f32)
        for j in range(self.grid.size[order[stage]] - 1):
            total = total + buf[j].astype(f32)
        if stage == self.stages - 1:
            out[...] = total.reshape(out.shape)
        else:
            buf[0] = total.astype(buf.dtype)

    def finish(self):
        for i in range(len(self.pieces)):
            for stage in range(self.stages):
                for copy in self.copies(i, stage):
                    copy.wait_send()


def scatter_buffers(grid, order, rows, columns, dtype):
    shapes, left = [], list(DIMS)
    for d in grid.order(order):
        left.remove(d)
        shapes.append((grid.size[d] - 1,) + tuple(grid.size[e] for e in left) + (rows, columns))
    return [pltpu.VMEM(s, dtype) for s in shapes]


def cuts(total, parts, unit):
    while parts > 1 and total % (parts * unit):
        parts -= 1
    return [(j * (total // parts), total // parts) for j in range(parts)]


def dotg(a, b, ca, cb, precision=None):
    return lax.dot_general(
        a, b, (((ca,), (cb,)), ((), ())), preferred_element_type=f32, precision=precision
    )


def iota(shape, dim):
    return lax.broadcasted_iota(jnp.int32, shape, dim)


def three_parts(x):
    high = x.astype(bf16).astype(f32)
    mid = (x - high).astype(bf16).astype(f32)
    return high, mid, x - high - mid


def spread_vector(rows, n):
    shards, width = rows.shape
    total = shards * n
    place = (iota((width, total), 1) % n == iota((width, total), 0)).astype(f32).astype(bf16)
    wide = dotg(rows, place, 1, 0)
    keep = iota((shards, total), 1) // n == iota((shards, total), 0)
    return jnp.sum(jnp.where(keep, wide, 0.0), axis=0, keepdims=True)


def fold_vector(vector, shards, n, width):
    total = shards * n
    keep = iota((shards, total), 1) // n == iota((shards, total), 0)
    place = (iota((total, width), 0) % n == iota((total, width), 1)).astype(f32).astype(bf16)
    parts = [jnp.where(keep, part, 0.0).astype(bf16) for part in three_parts(vector)]
    return sum(dotg(part, place, 1, 0) for part in parts)


def attend_prepare(qkv_ref, prep, live, pair):
    length, width = qkv_ref.shape[0], qkv_ref.shape[1] // 3
    k = qkv_ref[:, pl.ds(pl.multiple_of(width + pair * LANES, LANES), LANES)].astype(f32)
    v = qkv_ref[:, pl.ds(pl.multiple_of(2 * width + pair * LANES, LANES), LANES)].astype(f32)
    lane, row = iota((length, LANES), 1), iota((length, LANES), 0)
    bias = jnp.where(row < live, 0.0, neg_fill)
    k = k * (1.0 / math.sqrt(HEAD_DIM))
    for h in range(2):
        mine, spare = lane // HEAD_DIM == h, HEAD_DIM * (1 - h)
        prep[h, 0] = jnp.where(mine, k, jnp.where(lane == spare, bias, 0.0)).astype(bf16)
        prep[h, 1] = jnp.where(mine, v, 1.0).astype(bf16)


def attend(qkv_ref, context_ref, lse_ref, prep, pair, rows, block):
    out = pl.ds(pl.multiple_of(pair * LANES, LANES), LANES)
    q = qkv_ref[rows, out].astype(f32)
    lane = iota((block, LANES), 1)
    low = lane < HEAD_DIM
    sums, tops = [], []
    for h in range(2):
        spare = HEAD_DIM * (1 - h)
        query = jnp.where(lane // HEAD_DIM == h, q, jnp.where(lane == spare, 1.0, 0.0)).astype(bf16)
        scores = dotg(query, prep[h, 0], 1, 1)
        top = jnp.max(scores, axis=1, keepdims=True)
        weights = jnp.exp(scores - top).astype(bf16)
        sums.append(dotg(weights, prep[h, 1], 1, 0))
        tops.append(top)
    num = jnp.where(low, sums[0], sums[1])
    den = pltpu.roll(jnp.where(low, sums[1], sums[0]), HEAD_DIM, 1)
    context_ref[rows, out] = (num / den).astype(bf16)
    total = jnp.where(low, tops[0], tops[1]) + jnp.log(den)
    other = pltpu.roll(total, HEAD_DIM, 1)
    kept = jnp.where(lane == 2 * pair + 1, other, lse_ref[rows, :])
    lse_ref[rows, :] = jnp.where(lane == 2 * pair, total, kept)


def gelu_parts(x):
    cdf = 0.5 * (1.0 + lax.erf(x * (1.0 / math.sqrt(2.0))))
    return cdf, jnp.exp(-0.5 * x * x) * (1.0 / math.sqrt(2.0 * math.pi))


def normalize(values):
    center = values - jnp.mean(values, axis=-1, keepdims=True)
    scale = lax.rsqrt(jnp.mean(center * center, axis=-1, keepdims=True) + eps_norm)
    return center * scale, scale


def gather_plan(shapes):
    plan, every = [("s", ())], slice(None)
    width = shapes["o"][1]
    for a, n in cuts(width, 3, LANES):
        plan += [("q", (every, pl.ds(part * width + a, n))) for part in range(3)]
    for name, parts in (("o", 2), ("u", 6), ("p", 2), ("d", 3)):
        rows, columns = shapes[name]
        for a, n in cuts(columns, parts, LANES):
            for b, m in cuts(rows, 2 if name == "d" else 1, 8):
                plan.append((name, (pl.ds(b, m) if name == "d" else every, pl.ds(a, n))))
    return [(name, sub, GATHER_ORDERS[i % len(GATHER_ORDERS)]) for i, (name, sub) in enumerate(plan)]


def forward_kernel(grid, plan, sizes, *refs):
    (len_ref, h_tokens, keep_a, keep_f, wq, wo, wu, wd, wp), refs = refs[:9], refs[9:]
    count = len(sizes)
    small_in, refs = refs[:count], refs[count:]
    kept_hbm, (act_t, slope), refs = refs[:16], refs[16:18], refs[18:]
    firsts, small_out, refs = refs[0], refs[1 : 1 + count], refs[1 + count :]
    kept, refs = refs[:16], refs[16:]
    (gq, go, gu, gd, gp, qkv_ref, context, lse, tokens_t, context_t, hidden_t, norm1, scale1, norm2, scale2, layer_out) = kept
    (gs, tokens_ref, keep, hidden, hidden_low, act, act_buf, slope_buf, prep, bias), refs = refs[:10], refs[10:]
    send, recv, own_sem, keep_sem, act_sem, slope_sem, out_sem, norm_sem = refs
    length, width = context.shape
    b_qv, b_out, g1, b1, b_up, b_down, g2, b2, b_pool = small_out
    outs = [pltpu.make_async_copy(src, dst, out_sem.at[i]) for i, (src, dst) in enumerate(zip(kept, kept_hbm))]

    def put(*which):
        for i, ref in enumerate(kept):
            if any(ref is w for w in which):
                outs[i].start()

    at = grid.me()
    own = tuple(at[d] for d in DIMS)
    to_own = []
    for i, (src, dst) in enumerate(((wq, gq), (wo, go), (wu, gu), (wd, gd), (wp, gp))):
        to_own.append(pltpu.make_async_copy(src, dst.at[own], own_sem.at[i]))
        to_own[-1].start()
    to_tokens = pltpu.make_async_copy(h_tokens, tokens_ref, own_sem.at[5])
    to_tokens.start()
    mine = gs.at[own]
    mine[...] = jnp.zeros(mine.shape, bf16)
    for i, (ref, n) in enumerate(zip(small_in, sizes)):
        mine[i : i + 1, 0:n] = ref[...]
    where = dict(q=gq, o=go, u=gu, d=gd, p=gp, s=gs)
    gather = Gather(grid, [(where[name], sub, order) for name, sub, order in plan], send, recv)
    number = {}
    for i, (name, _, _) in enumerate(plan):
        number.setdefault(name, []).append(i)
    end = {name: [gather.whole[i] for i in numbers] for name, numbers in number.items()}
    grid.barrier(grid.straight())
    for copy in to_own:
        copy.wait()
    gather.begin()
    load = pltpu.make_async_copy(keep_a, keep, keep_sem)
    load.start()
    to_tokens.wait()
    tokens_t[...] = tokens_ref[...].T
    lse[...] = jnp.zeros_like(lse)
    put(tokens_t)
    gather.until(end["s"][0])
    rows = gs[...].reshape((grid.count,) + gs.shape[-2:])
    for i, (ref, n) in enumerate(zip(small_out, sizes)):
        ref[...] = spread_vector(rows[:, i, :], n)
    bias[:, :width] = b_qv[:, :width]
    bias[:, width : 2 * width] = jnp.zeros((1, width), f32)
    bias[:, 2 * width :] = b_qv[:, width:]

    groups = len(number["q"]) // 3
    part = width // groups
    pairs, block = part // LANES, min(512, length)
    blocks, live = length // block, len_ref[0]
    each = pairs * blocks

    def attention(t):
        @pl.when(t % each == 0)
        def _():
            for j in range(3):
                cols = pl.ds(pl.multiple_of(j * width + t // each * part, part), part)
                out = dotg(tokens_ref[...], gq[:, :, :, :, :, cols].reshape(width, part), 1, 0)
                qkv_ref[:, cols] = (out + bias[:, cols]).astype(bf16)

        @pl.when(t % blocks == 0)
        def _():
            attend_prepare(qkv_ref, prep, live, t // blocks)

        rows = pl.ds(pl.multiple_of((t % blocks) * block, block), block)
        attend(qkv_ref, context, lse, prep, t // blocks, rows, block)

    slots = groups * each
    first, total = end["q"][2], len(gather.events)

    def by_then(share):
        return first + int(share * (total - first))

    gather.loop(
        slots,
        [max(end["q"][3 * (t // each) + 2], by_then(SHARES[0] * t / slots)) for t in range(slots)],
        attention,
    )
    put(gq, qkv_ref, context, lse)

    load.wait()
    block = min(512, length)
    blocks = length // block

    def row_block(t):
        return pl.ds(pl.multiple_of(t * block, block), block)

    gather.until(end["o"][-1])

    def project(t):
        here = row_block(t)
        attended = dotg(context[here, :], go[...].reshape(width, width), 1, 0) + b_out[...]
        total = tokens_ref[here, :].astype(f32) + attended * (keep[here, :].astype(f32) * keep_scale)
        norm, scale = normalize(total)
        out = norm * g1[...] + b1[...]
        hidden[here, :] = out
        hidden_low[here, :] = out.astype(bf16)
        hidden_t[:, here] = out.astype(bf16).T
        context_t[:, here] = context[here, :].T
        norm1[here, :] = norm.astype(bf16)
        scale1[here, :] = jnp.broadcast_to(scale, (block, LANES))

    gather.loop(blocks, [by_then(SHARES[0] + (SHARES[1] - SHARES[0]) * t / blocks) for t in range(blocks)], project)
    load = pltpu.make_async_copy(keep_f, keep, keep_sem)
    load.start()
    put(go, hidden_t, context_t, norm1, scale1)

    parts = len(end["u"])
    step = gu.shape[-1] // parts
    strip = min(128, length)

    def saved(t, cols):
        yield pltpu.make_async_copy(act_buf.at[t % 2], act_t.at[cols, :], act_sem.at[t % 2])
        yield pltpu.make_async_copy(slope_buf.at[t % 2], slope.at[:, cols], slope_sem.at[t % 2])

    def up(t):
        cols = pl.ds(pl.multiple_of(t * step, step), step)
        weight = gu[:, :, :, :, :, cols].reshape(width, step)

        @pl.when(t >= 2)
        def _():
            for copy in saved(t, cols):
                copy.wait()

        for i in range(length // strip):
            here = slice(i * strip, (i + 1) * strip)
            pre = dotg(hidden_low[here, :], weight, 1, 0) + b_up[:, cols]
            cdf, pdf = gelu_parts(pre)
            out = (pre * cdf).astype(bf16)
            act[here, cols] = out
            act_buf[t % 2, :, here] = out.T
            slope_buf[t % 2, here, :] = (cdf + pre * pdf).astype(bf16)
        for copy in saved(t, cols):
            copy.start()

    gather.loop(parts, [max(end["u"][t], by_then(SHARES[1] + (SHARES[2] - SHARES[1]) * t / parts)) for t in range(parts)], up)
    for t in range(max(0, parts - 2), parts):
        for copy in saved(t, pl.ds(0, step)):
            copy.wait()

    load.wait()
    put(gu)
    halves = len(cuts(gd.shape[-2], 2, 8))
    ends = end["d"][halves - 1 :: halves]
    parts = len(ends)
    step = width // parts

    def down(t):
        cols = pl.ds(pl.multiple_of(t * step, step), step)
        out = dotg(act[...], gd[:, :, :, :, :, cols].reshape(-1, step), 1, 0) + b_down[:, cols]
        hidden[:, cols] += out * (keep[:, cols].astype(f32) * keep_scale)

    gather.loop(parts, ends, down)
    put(gd, gp)
    block = min(256, length)
    blocks = length // block

    def left(t):
        for j, i in enumerate((13, 14, 15)):
            yield pltpu.make_async_copy(kept[i].at[row_block(t)], kept_hbm[i].at[row_block(t)], norm_sem.at[j, t])

    def norm(t):
        here = row_block(t)
        value, scale = normalize(hidden[here, :])
        out = value * g2[...] + b2[...]
        norm2[here, :] = value.astype(bf16)
        scale2[here, :] = jnp.broadcast_to(scale, (block, LANES))
        layer_out[here, :] = out.astype(bf16)
        for c in left(t):
            c.start()

        @pl.when(t == 0)
        def _():
            first = out[0:8].astype(bf16)
            pooled = jnp.tanh(dotg(first, gp[...].reshape(width, width), 1, 0) + b_pool[...])
            firsts[0:1, :] = pooled[0:1]
            firsts[1:2, :] = first[0:1].astype(f32)

    gather.loop(blocks, [gather.now] * blocks, norm)
    gather.finish()
    for copy in outs[:13]:
        copy.wait()
    for t in range(blocks):
        for c in left(t):
            c.wait()


def run_forward(grid, length_of, tokens, keep_a, keep_f, big, small):
    length, width = tokens.shape
    names = ("q", "o", "u", "d", "p")
    shapes = {k: w.shape for k, w in zip(names, big)}
    inner = shapes["u"][1]
    sizes = [v.shape[0] for v in small]
    plan = gather_plan(shapes)
    pad = -(-max(sizes) // LANES) * LANES
    step = inner // sum(p[0] == "u" for p in plan)
    vmem, anywhere = pl.BlockSpec(memory_space=pltpu.VMEM), pl.BlockSpec(memory_space=pl.ANY)
    shape = jax.ShapeDtypeStruct
    kept = [(grid.shape + shapes[k], bf16) for k in names] + [
        ((length, 3 * width), bf16),
        ((length, width), bf16),
        ((length, LANES), f32),
        ((width, length), bf16),
        ((width, length), bf16),
        ((width, length), bf16),
        ((length, width), bf16),
        ((length, LANES), f32),
        ((length, width), bf16),
        ((length, LANES), f32),
        ((length, width), bf16),
    ]
    return pl.pallas_call(
        functools.partial(forward_kernel, grid, plan, sizes),
        out_shape=[shape(*k) for k in kept]
        + [shape((inner, length), bf16), shape((length, inner), bf16), shape((2, width), f32)]
        + [shape((1, grid.count * n), f32) for n in sizes],
        in_specs=[pl.BlockSpec(memory_space=pltpu.SMEM)] + [anywhere] * 8 + [vmem] * len(small),
        out_specs=[anywhere] * 18 + [vmem] * (1 + len(small)),
        scratch_shapes=[pltpu.VMEM(*k) for k in kept]
        + [
            pltpu.VMEM(grid.shape + (16, pad), bf16),
            pltpu.VMEM((length, width), bf16),
            pltpu.VMEM((length, width), jnp.int32),
            pltpu.VMEM((length, width), f32),
            pltpu.VMEM((length, width), bf16),
            pltpu.VMEM((length, inner), bf16),
            pltpu.VMEM((2, step, length), bf16),
            pltpu.VMEM((2, length, step), bf16),
            pltpu.VMEM((2, 2, length, LANES), bf16),
            pltpu.VMEM((1, 3 * width), f32),
            pltpu.SemaphoreType.DMA((len(plan), grid.slots)),
            pltpu.SemaphoreType.DMA((len(plan), grid.slots)),
            pltpu.SemaphoreType.DMA((6,)),
            pltpu.SemaphoreType.DMA,
            pltpu.SemaphoreType.DMA((2,)),
            pltpu.SemaphoreType.DMA((2,)),
            pltpu.SemaphoreType.DMA((16,)),
            pltpu.SemaphoreType.DMA((3, length // min(256, length))),
        ],
        compiler_params=pltpu.CompilerParams(
            collective_id=0, has_side_effects=True, vmem_limit_bytes=VMEM_LIMIT
        ),
        name="forward",
    )(length_of, tokens, keep_a, keep_f, *big, *[v.reshape(1, -1) for v in small])


def pool_and_loss(views, partners_ref, wp, here, shard_rows, unit_ref, work, cls_grad, pool_w, pool_b, loss):
    high = lax.Precision.HIGHEST
    count, width = math.prod(views.shape[:4]), views.shape[-1]
    each = count // views.shape[0]

    def pooled_rows(z):
        rows = views[z].reshape((each,) + views.shape[-2:])
        pooled = rows[:, 0, :]
        scale = lax.rsqrt(jnp.sum(pooled * pooled, axis=1, keepdims=True) + 1e-06)
        return slice(z * each, (z + 1) * each), pooled, scale, rows[:, 1, :]

    for z in range(views.shape[0]):
        at, pooled, scale, cls = pooled_rows(z)
        unit_ref[at, :] = pooled * scale
        work[count + z * each : count + (z + 1) * each, :] = cls.astype(bf16)
    unit = unit_ref[0:count, :]
    sims = dotg(unit, unit, 1, 1, high) / logit_divisor
    column, row = iota((count, count), 1), iota((count, count), 0)
    others = jnp.where(row == column, neg_fill, sims)
    top = jnp.max(others, axis=1, keepdims=True)
    weights = jnp.exp(others - top)
    total = jnp.sum(weights, axis=1, keepdims=True)
    partner = row == partners_ref[...]
    target = jnp.sum(jnp.where(partner, sims, 0.0), axis=1, keepdims=True)
    lost = jnp.sum(top + jnp.log(total) - target, axis=0, keepdims=True) / count
    loss[...] = jnp.broadcast_to(lost, loss.shape)
    pull = weights / total - jnp.where(partner, 1.0, 0.0)
    pull = pull + dotg(pull, (row == column).astype(f32), 0, 0, high)
    for z in range(views.shape[0]):
        at, pooled, scale, _ = pooled_rows(z)
        unit_grad = dotg(pull[at], unit, 1, 0, high) / logit_divisor
        along = jnp.sum(pooled * unit_grad, axis=1, keepdims=True)
        pooled_grad = scale * unit_grad - pooled * (scale * scale * scale * along)
        work[at, :] = (pooled_grad * (1.0 - pooled * pooled)).astype(bf16)
    pre, cls = work[0:count, :], work[count : 2 * count, :]
    mine = jnp.sum(jnp.where(iota((count, width), 0) == here, pre.astype(f32), 0.0), axis=0, keepdims=True)
    cls_grad[...] = dotg(jnp.broadcast_to(mine, (8, width)).astype(bf16), wp, 1, 1)
    place = (iota((width, LANES), 0) == here * shard_rows + iota((width, LANES), 1)).astype(f32).astype(bf16)
    cls_rows = dotg(cls, place, 1, 0).astype(bf16)
    pool_w[...] = dotg(cls_rows, pre, 0, 0)[:shard_rows]
    sums = jnp.broadcast_to(jnp.sum(pre.astype(f32), axis=0, keepdims=True), (8, width))
    pool_b[...] = sum(dotg(part.astype(bf16), place, 1, 0) for part in three_parts(sums))


def attend_back(qkv_ref, context, dcontext, lse, live, pair, prep):
    length, width = qkv_ref.shape[0], context.shape[1]
    scale = 1.0 / math.sqrt(HEAD_DIM)
    one = pl.ds(pl.multiple_of(pair * LANES, LANES), LANES)

    def col(part):
        return pl.ds(pl.multiple_of(part * width + pair * LANES, LANES), LANES)

    q, k, v = (qkv_ref[:, col(j)].astype(f32) for j in range(3))
    d = dcontext[:, one].astype(f32)
    lane, row = iota((length, LANES), 1), iota((length, LANES), 0)
    bias = jnp.where(row < live, 0.0, neg_fill)
    mine, place = lane // HEAD_DIM, lane % HEAD_DIM
    source, target = iota((LANES, LANES), 0), iota((LANES, LANES), 1)
    swap = (source // HEAD_DIM != target // HEAD_DIM).astype(f32).astype(bf16)
    both = d * context[:, one].astype(f32)
    inner = sum(dotg(part.astype(bf16), swap, 1, 0) for part in three_parts(both))
    d0, d1, d2 = three_parts(-inner)
    extra_d = jnp.where(place == 0, d0, jnp.where(place == 1, d1, jnp.where(place == 2, d2, 0.0)))
    extra_q = jnp.where(place == 0, 1.0, 0.0)
    for j, part in enumerate(three_parts(-lse[...])):
        head = jnp.where(target < HEAD_DIM, 2 * pair + 1, 2 * pair)
        pick = ((source == head) & (target % HEAD_DIM == j + 1)).astype(f32).astype(bf16)
        extra_q = extra_q + dotg(part.astype(bf16), pick, 1, 0)
    extra_k = jnp.where(place == 0, bias, jnp.where(place < 4, 1.0, 0.0))
    extra_v = jnp.where(place < 3, 1.0, 0.0)
    q = q * scale
    for h in range(2):
        here = mine == h
        prep[h, 0] = jnp.where(here, q, extra_q).astype(bf16)
        prep[h, 1] = jnp.where(here, k, extra_k).astype(bf16)
        prep[h, 2] = jnp.where(here, d, extra_d).astype(bf16)
        prep[h, 3] = jnp.where(here, v, extra_v).astype(bf16)
        prep[h, 4] = jnp.where(here, k * scale, 0.0).astype(bf16)
    return q.astype(bf16).T, d.astype(bf16).T


def scatter_plan(grid, shapes):
    plan, every = [], slice(None)
    width = shapes["o"][1]
    rows, columns = shapes["d"]
    plan += [("d", (pl.ds(a, n), every), n, columns) for a, n in cuts(rows, 6, 8)]
    for name, parts in (("u", 6), ("o", 2)):
        rows, columns = shapes[name]
        plan += [(name, (every, pl.ds(a, n)), rows, n) for a, n in cuts(columns, parts, LANES)]
    for a, n in cuts(width, 3, LANES):
        plan += [("q", (every, pl.ds(part * width + a, n)), shapes["q"][0], n) for part in range(3)]
    plan.append(("s", (), 16, shapes["s"]))
    return [(p[0], p[1], SCATTER_ORDERS[i % 2]) + p[2:] for i, p in enumerate(plan)]


def backward_kernel(grid, whole, plan, sizes, shard_rows, *refs):
    (len_ref, partners_ref, firsts, g1, g2), refs = refs[:5], refs[5:]
    (h_cot, h_keep_a, h_keep_f, h_norm1, h_scale1, h_norm2, h_scale2, h_act, h_slope, h_hidden, h_context_t), refs = refs[:11], refs[11:]
    (h_qkv, h_context, h_lse, h_tokens, h_wq, h_wo, h_wu, h_wd, h_wp), refs = refs[:9], refs[9:]
    (rq, ro, ru, rd, rs, pool_w, pool_b, loss, h_tokens_grad), refs = refs[:9], refs[9:]
    (dd, du, do, dsmall, grad, gctx, low, norm, keep, scale, vec, cls_grad, views, wp), refs = refs[:14], refs[14:]
    (send, recv, view_send, view_recv, sems, pair_sems), bufs = refs[:6], list(refs[6:])
    length, width = grad.shape
    inner = vec.shape[1]
    sources, results = dict(d=dd, u=du, o=do, s=dsmall), dict(d=rd, u=ru, o=ro, q=rq, s=rs)
    number = {}
    for i, p in enumerate(plan):
        number.setdefault(p[0], []).append(i)
    cot = low

    def copy(k, src, dst):
        return pltpu.make_async_copy(src, dst, sems.at[k])

    first_loads = [copy(0, h_cot, cot), copy(1, h_norm2, norm), copy(2, h_scale2, scale), copy(3, h_keep_f, keep), copy(4, h_wp, wp)]
    for c in first_loads:
        c.start()
    at_all = whole.me()
    views[tuple(at_all[d] for d in DIMS)] = firsts[...]
    exchange = Exchange(whole, views, view_send, view_recv)
    whole.barrier(whole.straight() + [o for o in whole.around(("z", "c")) + whole.around(("y", "x")) if len(o) > 1])
    exchange.start(0)
    vec[...] = jnp.zeros_like(vec)
    for c in first_loads:
        c.wait()
    strip = min(128, length)
    strips = length // strip

    def strip_of(t):
        return pl.ds(pl.multiple_of(t * strip, strip), strip)

    def add_row(j, x):
        vec[j : j + 1, : x.shape[1]] += jnp.sum(x, axis=0, keepdims=True)

    def norm_back(here, up, gain, slot):
        value = norm[here, :].astype(f32)
        scaled = up * gain[...]
        along = jnp.mean(scaled * value, axis=1, keepdims=True)
        back = scale[here, 0:1] * (scaled - jnp.mean(scaled, axis=1, keepdims=True) - value * along)
        add_row(slot, up * value)
        add_row(slot + 1, up)
        grad[here, :] = back
        out = (back * (keep[here, :].astype(f32) * keep_scale)).astype(bf16)
        low[here, :] = out
        return out.astype(f32)

    def second_norm(t, extra):
        here = strip_of(t)
        up = cot[here, :].astype(f32)
        if extra is not None:
            up = up + jnp.where(iota((strip, width), 0) + t * strip == 0, extra, 0.0)
        add_row(5, norm_back(here, up, g2, 6))
        return 0

    held = -(-math.prod(whole.shape) // strip)
    def rest_of_norm(t, _):
        @pl.when(t == (held + strips) // 2)
        def _():
            exchange.wait(0)
            exchange.start(1)

        return second_norm(t, None)

    lax.fori_loop(held, strips, rest_of_norm, 0)
    exchange.wait(1)
    here = lax.axis_index("dp") * (whole.size["y"] * whole.size["x"]) + lax.axis_index("fsdp")
    pool_and_loss(views, partners_ref, wp[...], here, shard_rows, grad, gctx, cls_grad, pool_w, pool_b, loss)
    lax.fori_loop(0, held, lambda t, _: second_norm(t, cls_grad[0:1, :]), 0)
    wo = wp
    second_loads = [copy(1, h_norm1, norm), copy(2, h_scale1, scale), copy(3, h_keep_a, keep), copy(6, h_wo, wo)]
    for c in second_loads:
        c.start()

    pieces, left = [], bufs
    for name, sub, order, _, _ in plan:
        n = len(grid.order(order))
        pieces.append([sources.get(name), sub, order, left[:n], results[name].at[sub] if sub else results[name]])
        left = left[n:]
    groups = len(number["q"]) // 3
    early, last = len(plan) - 1 - len(number["q"]), len(plan) - 1
    scatter = Scatter(grid, pieces, send, recv)
    stages, lag = scatter.stages, 4
    steps = [
        [(j - stage * lag, stage) for stage in range(stages) if 0 <= j - stage * lag < early]
        for j in range(early + (stages - 1) * lag)
    ]

    def feed_forward(act, slope, wd, wu, gup, turned):
        third = [copy(5, h_hidden, turned), copy(7, h_context_t, turned)]
        third[0].start()
        block = min(256, length)
        chunk, part = act.shape[1], slope.shape[2]
        chunks, parts = inner // chunk, inner // part
        slab = wu.shape[1]

        def act_load(t):
            return pltpu.make_async_copy(h_act.at[pl.ds(pl.multiple_of(t * chunk, chunk), chunk), :], act.at[t % 2], pair_sems.at[0, t % 2])

        def part_loads(t):
            cols = pl.ds(pl.multiple_of(t * part, part), part)
            yield pltpu.make_async_copy(h_slope.at[:, cols], slope.at[t % 2], pair_sems.at[1, t % 2])
            yield pltpu.make_async_copy(h_wd.at[cols, :], wd.at[t % 2], pair_sems.at[2, t % 2])

        def slab_load(t):
            return pltpu.make_async_copy(h_wu.at[pl.ds(pl.multiple_of(t * slab, slab), slab), :], wu.at[t % 2], pair_sems.at[3, t % 2])

        act_load(0).start()
        for c in part_loads(0):
            c.start()
        slab_load(0).start()
        across = grid.size["y"] * grid.size["x"]

        def down_weight(t, _):
            @pl.when(t + 1 < chunks)
            def _():
                act_load(t + 1).start()

            act_load(t).wait()
            out = dotg(act[t % 2], low[...], 1, 0).astype(bf16)
            dd[t // grid.size["c"], t % grid.size["c"]] = out.reshape(dd.shape[2:])
            return 0

        lax.fori_loop(0, chunks, down_weight, 0)
        for i in number["d"]:
            scatter.begin(i)
        third[0].wait()

        def up_part(t, _):
            cols = pl.ds(pl.multiple_of(t * part, part), part)

            @pl.when(t + 1 < parts)
            def _():
                for c in part_loads(t + 1):
                    c.start()

            for c in part_loads(t):
                c.wait()
            for i in range(length // block):
                rows = slice(i * block, (i + 1) * block)
                out = dotg(low[rows, :], wd[t % 2], 1, 1) * slope[t % 2, rows, :].astype(f32)
                gup[rows, cols] = out.astype(bf16)
            vec[4:5, cols] = jnp.sum(gup[:, cols].astype(f32), axis=0, keepdims=True)
            out = dotg(turned[...], gup[:, cols], 1, 0).astype(bf16)
            du[:, :, :, :, :, cols] = out.reshape(grid.shape + (-1, part))
            for k, i in enumerate(number["u"]):

                @pl.when(t == k)
                def _():
                    scatter.begin(i)
                    scatter.run(steps[k])

            return 0

        lax.fori_loop(0, parts, up_part, 0)
        third[1].start()

        def hidden_part(t, _):
            cols = pl.ds(pl.multiple_of(t * slab, slab), slab)

            @pl.when(t + 1 < width // slab)
            def _():
                slab_load(t + 1).start()

            slab_load(t).wait()
            grad[:, cols] += dotg(gup[...], wu[t % 2], 1, 1)
            for k in range(width // slab):

                @pl.when(t == k)
                def _():
                    scatter.run(steps[parts + k])

            return 0

        lax.fori_loop(0, width // slab, hidden_part, 0)
        for c in second_loads:
            c.wait()

        def first_norm(t, _):
            add_row(1, norm_back(strip_of(t), grad[strip_of(t), :], g1, 2))
            return 0

        lax.fori_loop(0, strips, first_norm, 0)
        for c in (copy(9, h_context, norm), copy(10, h_lse, scale)):
            c.start()
        third[1].wait()
        for i in number["o"]:
            cols = plan[i][1][1]
            out = dotg(turned[...], low[:, cols], 1, 0).astype(bf16)
            do[:, :, :, :, :, cols] = out.reshape(grid.shape + (-1, cols.size))
            scatter.begin(i)
        for i in range(length // block):
            rows = slice(i * block, (i + 1) * block)
            gctx[rows, :] = dotg(low[rows, :], wo[...], 1, 1).astype(bf16)
        scatter.run(steps[parts + width // slab])
        return parts + width // slab + 1

    chunk, part, slab = inner // (grid.size["z"] * grid.size["c"]), inner // len(number["u"]), width // 3
    done = []

    def first_scope(*refs):
        done.append(feed_forward(*refs))

    pl.run_scoped(
        first_scope,
        pltpu.VMEM((2, chunk, length), bf16),
        pltpu.VMEM((2, length, part), bf16),
        pltpu.VMEM((2, part, width), bf16),
        pltpu.VMEM((2, slab, inner), bf16),
        pltpu.VMEM((length, inner), bf16),
        pltpu.VMEM((width, length), bf16),
    )
    step = done[0]

    def attention(qkv, tokens_t, wq, dq, prep, turned, acc):
        context, lse = norm, scale
        block = min(256, length) if grid.with_fsdp else min(128, length)
        blocks = length // block

        def rows_of(t):
            return pl.ds(pl.multiple_of(t * block, block), block)

        for i in number["q"]:
            scatter.pieces[i] = (dq,) + scatter.pieces[i][1:]
        span = width // groups

        def group_loads(g):
            for j in range(3):
                cols = pl.ds(j * width + g * span, span)
                yield pltpu.make_async_copy(h_qkv.at[:, cols], qkv.at[:, cols], pair_sems.at[j, g % 2])

        for g in range(min(2, groups)):
            for c in group_loads(g):
                c.start()
        loads = [copy(11, h_tokens, tokens_t), copy(12, h_wq.at[:, 0:width], wp)]
        loads += [copy(6, h_wq.at[:, width : 2 * width], wq.at[0]), copy(7, h_wq.at[:, 2 * width :], wq.at[1])]
        for c in loads:
            c.start()
        for c in (copy(9, h_context, norm), copy(10, h_lse, scale)):
            c.wait()
        each = span // LANES * blocks
        slots = groups * each
        live = len_ref[0]
        head = [slice(h * HEAD_DIM, (h + 1) * HEAD_DIM) for h in range(2)]
        due, late = [[] for _ in range(slots)], []
        for j, events in enumerate(steps[step:]):
            due[j * (slots - each // 2) // (len(steps) - step)] += events
        for g in range(groups - 1):
            for stage in range(stages):
                at, events = each * (g + 1) - 1 + SPACING * (stage + 1), [(i, stage) for i in number["q"][3 * g : 3 * g + 3]]
                if at < slots:
                    due[at] += events
                else:
                    late.append(events)
        tail = [late[j] if j < len(late) else [] for j in range(max(stages, len(late)))]
        for stage in range(stages):
            tail[len(tail) - stages + stage] += [(i, stage) for i in number["q"][-3:] + [last]]

        def slot(t, _):
            pair, b = t // blocks, t % blocks
            rows = rows_of(b)
            one = pl.ds(pl.multiple_of(pair * LANES, LANES), LANES)

            for g in range(groups):

                @pl.when(t == g * each)
                def _():
                    for c in group_loads(g):
                        c.wait()
                    if g + 2 < groups:
                        for c in group_loads(g + 2):
                            c.start()

            @pl.when(b == 0)
            def _():
                turned[0], turned[1] = attend_back(qkv, context, gctx, lse, live, pair, prep)
                acc[...] = jnp.zeros_like(acc)

            dq_rows = jnp.zeros((block, LANES), f32)
            for h in range(2):
                p = jnp.exp(dotg(prep[h, 0, rows, :], prep[h, 1], 1, 1))
                dp = dotg(prep[h, 2, rows, :], prep[h, 3], 1, 1)
                ds = (p * dp).astype(bf16)
                acc[0, head[h], :] += dotg(turned[1, head[h], rows], p.astype(bf16), 1, 0)
                acc[1, head[h], :] += dotg(turned[0, head[h], rows], ds, 1, 0)
                dq_rows = dq_rows + dotg(ds, prep[h, 4], 1, 0)
            qkv[rows, one] = dq_rows.astype(bf16)

            @pl.when(b == blocks - 1)
            def _():
                qkv[:, pl.ds(pl.multiple_of(width + pair * LANES, LANES), LANES)] = acc[1].astype(bf16).T
                qkv[:, pl.ds(pl.multiple_of(2 * width + pair * LANES, LANES), LANES)] = acc[0].astype(bf16).T

            for k in range(slots):
                if due[k]:

                    @pl.when(t == k)
                    def _():
                        scatter.run(due[k])

            @pl.when(t == each - 1)
            def _():
                loads[0].wait()

            @pl.when(t % each == each - 1)
            def _():
                for j in range(3):
                    cols = pl.ds(pl.multiple_of(j * width + t // each * span, LANES), span)
                    out = dotg(tokens_t[...], qkv[:, cols], 1, 0).astype(bf16)
                    dq[:, :, :, :, :, cols] = out.reshape(grid.shape + (-1, span))
                for g in range(groups):

                    @pl.when(t == each * (g + 1) - 1)
                    def _():
                        for i in number["q"][3 * g : 3 * g + 3]:
                            scatter.begin(i)

            return 0

        lax.fori_loop(0, slots, slot, 0)
        sums = dotg(jnp.ones((8, length), bf16), qkv[...], 1, 0)[0:1]
        vec[0:1, :width] = sums[:, :width]
        vec[0:1, width : 2 * width] = sums[:, 2 * width :]
        pad = dsmall.shape[-1]
        dsmall[...] = jnp.zeros_like(dsmall)
        for j, n in enumerate(sizes):
            folded = fold_vector(vec[j : j + 1, : grid.count * n], grid.count, n, pad)
            dsmall[:, :, :, :, j, :] = folded.reshape(grid.shape + (pad,))
        scatter.begin(number["s"][0])
        for c in loads[1:]:
            c.wait()
        rows = length // len(tail)
        for i, events in enumerate(tail):
            here = slice(i * rows, (i + 1) * rows)
            total = grad[here, :] + dotg(qkv[here, :width], wp[...], 1, 1)
            for j in range(2):
                total = total + dotg(qkv[here, (j + 1) * width : (j + 2) * width], wq[j], 1, 1)
            low[here, :] = total.astype(bf16)
            scatter.run(events)
        out = copy(13, low, h_tokens_grad)
        out.start()
        scatter.finish()
        exchange.finish()
        out.wait()

    pl.run_scoped(
        attention,
        pltpu.VMEM((length, 3 * width), bf16),
        pltpu.VMEM((width, length), bf16),
        pltpu.VMEM((2, width, width), bf16),
        pltpu.VMEM(grid.shape + (width // grid.count, 3 * width), bf16),
        pltpu.VMEM((2, 5, length, LANES), bf16),
        pltpu.VMEM((2, LANES, length), bf16),
        pltpu.VMEM((2, LANES, length), f32),
    )


def run_backward(grid, whole, length_of, partners, firsts, gains, hbm, length, width, inner, sizes, shard_rows):
    rows = width // grid.count
    pad = -(-max(sizes) // LANES) * LANES
    shapes = {"q": (rows, 3 * width), "o": (rows, width), "u": (rows, inner), "d": (inner // grid.count, width), "s": pad}
    plan = scatter_plan(grid, shapes)
    bufs = []
    for name, _, order, r, c in plan:
        bufs += scatter_buffers(grid, order, r, c, f32 if name == "s" else bf16)
    views_count = len(whole.around(("z", "c"))) + len(whole.around(("y", "x")))
    vmem, anywhere = pl.BlockSpec(memory_space=pltpu.VMEM), pl.BlockSpec(memory_space=pl.ANY)
    shape = jax.ShapeDtypeStruct
    return pl.pallas_call(
        functools.partial(backward_kernel, grid, whole, plan, sizes, shard_rows),
        out_shape=[shape(shapes[k], f32) for k in ("q", "o", "u", "d")]
        + [
            shape((16, pad), f32),
            shape((shard_rows, width), f32),
            shape((8, LANES), f32),
            shape((8, LANES), f32),
            shape((length, width), bf16),
        ],
        in_specs=[pl.BlockSpec(memory_space=pltpu.SMEM)] + [vmem] * 4 + [anywhere] * len(hbm),
        out_specs=[vmem] * 8 + [anywhere],
        scratch_shapes=[pltpu.VMEM(grid.shape + shapes[k], bf16) for k in ("d", "u", "o")]
        + [
            pltpu.VMEM(grid.shape + (16, pad), f32),
            pltpu.VMEM((length, width), f32),
            pltpu.VMEM((length, width), bf16),
            pltpu.VMEM((length, width), bf16),
            pltpu.VMEM((length, width), bf16),
            pltpu.VMEM((length, width), jnp.int32),
            pltpu.VMEM((length, LANES), f32),
            pltpu.VMEM((16, inner), f32),
            pltpu.VMEM((8, width), f32),
            pltpu.VMEM(whole.shape + (2, width), f32),
            pltpu.VMEM((width, width), bf16),
            pltpu.SemaphoreType.DMA((len(plan), grid.slots)),
            pltpu.SemaphoreType.DMA((len(plan), grid.slots)),
            pltpu.SemaphoreType.DMA((views_count,)),
            pltpu.SemaphoreType.DMA((views_count,)),
            pltpu.SemaphoreType.DMA((14,)),
            pltpu.SemaphoreType.DMA((4, 2)),
        ]
        + bufs,
        compiler_params=pltpu.CompilerParams(
            collective_id=1, has_side_effects=True, vmem_limit_bytes=VMEM_LIMIT
        ),
        name="backward",
    )(length_of, partners.reshape(1, -1), firsts, *gains, *hbm)


def finish_kernel(count, *refs):
    wide, narrow, refs = refs[:count], refs[count : count + 3], refs[count + 3 :]
    wide_out, refs = refs[:count], refs[count:]
    vectors, (bias, loss), refs = refs[:-count - 4], refs[-count - 4 : -count - 2], refs[-count - 2 :]
    bufs, (in_sem, out_sem) = refs[:count], refs[count:]
    loads = [pltpu.make_async_copy(a, b, in_sem.at[i]) for i, (a, b) in enumerate(zip(wide, bufs))]
    stores = [pltpu.make_async_copy(b, a, out_sem.at[i]) for i, (a, b) in enumerate(zip(wide_out, bufs))]
    for c in loads:
        c.start()
    for j, ref in enumerate(vectors):
        ref[...] = narrow[0][j : j + 1, : ref.shape[1]]
    bias[...] = narrow[1][0:1, : bias.shape[1]]
    loss[...] = narrow[2][0:1, 0:1]
    for load, store in zip(loads, stores):
        load.wait()
        store.start()
    for c in stores:
        c.wait()


def finish(wide, narrow, sizes):
    vmem, anywhere = pl.BlockSpec(memory_space=pltpu.VMEM), pl.BlockSpec(memory_space=pl.ANY)
    shape, count = jax.ShapeDtypeStruct, len(wide)
    outs = pl.pallas_call(
        functools.partial(finish_kernel, count),
        out_shape=[shape(w.shape, w.dtype) for w in wide] + [shape((1, n), f32) for n in sizes] + [shape((1, 1), f32)],
        in_specs=[anywhere] * count + [vmem] * 3,
        out_specs=[anywhere] * count + [vmem] * (len(sizes) + 1),
        scratch_shapes=[pltpu.VMEM(w.shape, w.dtype) for w in wide] + [pltpu.SemaphoreType.DMA((count,))] * 2,
        name="results",
    )(*wide, *narrow)
    return outs[:count], [v.reshape(-1) for v in outs[count:-1]], outs[-1].reshape(())


def on_device(whole, grid, tokens, lengths, keep_attn, keep_ffn, partners, out_cot, *weights):
    (w_qkv, b_qv, w_out, b_out, ln1_gain, ln1_bias, w_up, b_up, w_down, b_down, ln2_gain, ln2_bias, w_pool, b_pool) = weights
    _, length, width = tokens.shape
    inner = w_up.shape[1]
    big = [w_qkv, w_out, w_up, w_down, w_pool]
    small = [b_qv, b_out, ln1_gain, ln1_bias, b_up, b_down, ln2_gain, ln2_bias, b_pool]
    shard_rows = w_qkv.shape[0]
    if not grid.with_fsdp:
        big = [lax.all_gather(w, "fsdp", axis=0, tiled=True) for w in big]
        small = [lax.all_gather(v, "fsdp", axis=0, tiled=True) for v in small]
    sizes = [v.shape[0] for v in small][:-1]
    flat = (length, width)
    keep_a, keep_f = keep_attn.reshape(flat), keep_ffn.reshape(flat)
    outs = run_forward(grid, lengths, tokens.reshape(flat), keep_a, keep_f, big, small)
    wq, wo, wu, wd, wp = (g.reshape(-1, g.shape[-1]) for g in outs[:5])
    qkv, context, lse, tokens_t, context_t, hidden_t, norm1, scale1, norm2, scale2, layer_out = outs[5:16]
    act_t, slope, firsts = outs[16:19]
    vectors = outs[19:]
    hbm = [
        out_cot.reshape(flat), keep_a, keep_f, norm1, scale1, norm2, scale2, act_t, slope, hidden_t, context_t,
        qkv, context, lse, tokens_t, wq, wo, wu, wd, wp,
    ]
    rq, ro, ru, rd, rs, pool_w, pool_b, loss, tokens_grad = run_backward(
        grid, whole, lengths, partners, firsts, [vectors[2], vectors[6]], hbm, length, width, inner, sizes, shard_rows
    )
    if grid.with_fsdp:
        wide, vectors, loss = finish([layer_out, tokens_grad, rq, ro, ru, rd, pool_w], [rs, pool_b, loss], sizes + [shard_rows])
        layer_out, tokens_grad, rq, ro, ru, rd, pool_w = wide
    else:
        owned = [rq, ro, ru, rd] + [rs[j, :n] for j, n in enumerate(sizes)]
        rq, ro, ru, rd, *vectors = [lax.psum_scatter(g, "fsdp", scatter_dimension=0, tiled=True) for g in owned]
        vectors, loss = vectors + [pool_b[0, :shard_rows]], loss[0, 0]
    s_qv, s_out, s_g1, s_b1, s_up, s_down, s_g2, s_b2, s_pool = vectors
    return (
        layer_out.reshape(tokens.shape), tokens_grad.reshape(tokens.shape), rq, s_qv, ro, s_out, s_g1, s_b1, ru, s_up,
        rd, s_down, s_g2, s_b2, pool_w, s_pool, loss,
    )


def solution(mesh):
    rows, vector, matrix = P(AXES, None, None), P(AXES), P(AXES, None)
    weights = (matrix, vector, matrix, vector, vector, vector, matrix, vector, matrix, vector, vector, vector, matrix, vector)
    devices = mesh.shape["dp"] * mesh.shape["fsdp"]

    def step(*args):
        whole = Grid(mesh)
        grid = whole if (args[6].shape[0] // devices) % 8 == 0 else Grid(mesh, False)
        return jax.shard_map(
            functools.partial(on_device, whole, grid),
            mesh=mesh,
            in_specs=(rows, vector, rows, rows, P(), rows) + weights,
            out_specs=(rows, rows) + weights + (P(),),
            check_vma=False,
        )(*args)

    return step
```

```python
import functools
import math

import jax
import jax.numpy as jnp
from jax import lax
from jax.experimental import pallas as pl
from jax.experimental.pallas import tpu as pltpu
from jax.sharding import PartitionSpec as P

HEAD_DIM = 64
LANES = 128
f32, bf16 = jnp.float32, jnp.bfloat16
MESH = pl.DeviceIdType.MESH
AXES = ("dp", "fsdp")
eps_norm = 1e-05
keep_scale = 1.0 / 0.9
logit_divisor = 0.05
neg_fill = -1000000000.0
VMEM_LIMIT = 67043328
DIMS = ("z", "c", "y", "x")
SPACING = 4
SHARES = (0.62, 0.68, 0.92)
GATHER_ORDERS = (("z", "x", "y", "c"), ("z", "y", "x", "c"))
SCATTER_ORDERS = (("c", "y", "x", "z"), ("c", "x", "y", "z"))


class Grid:
    def __init__(self, mesh, with_fsdp=True):
        dp, fsdp = mesh.shape["dp"], mesh.shape["fsdp"]
        cores = 2 if dp % 2 == 0 else 1
        side = math.isqrt(fsdp)
        if side * side != fsdp:
            side = fsdp
        self.with_fsdp = with_fsdp
        self.size = {
            "z": dp // cores,
            "c": cores,
            "y": fsdp // side if with_fsdp else 1,
            "x": side if with_fsdp else 1,
        }
        self.shape = tuple(self.size[d] for d in DIMS)
        self.count = math.prod(self.shape)
        self.slots = sum(n - 1 for n in self.shape)

    def me(self):
        dp, fsdp = lax.axis_index("dp"), lax.axis_index("fsdp")
        at = {"z": lax.div(dp, self.size["c"]), "c": lax.rem(dp, self.size["c"])}
        if self.with_fsdp:
            at["y"], at["x"] = lax.div(fsdp, self.size["x"]), lax.rem(fsdp, self.size["x"])
        else:
            at["y"], at["x"] = 0, 0
        return at

    def device(self, at):
        fsdp = at["y"] * self.size["x"] + at["x"] if self.with_fsdp else lax.axis_index("fsdp")
        return (at["z"] * self.size["c"] + at["c"], fsdp)

    def peer(self, at, dim, j):
        other = dict(at)
        other[dim] = lax.rem(at[dim] + j, self.size[dim])
        return other

    def slot(self, dim, j):
        base = 0
        for d in DIMS:
            if d == dim:
                return base + j - 1
            base += self.size[d] - 1

    def order(self, order):
        return tuple(d for d in order if self.size[d] > 1)

    def straight(self):
        return [{d: j} for d in DIMS for j in range(1, self.size[d])]

    def around(self, dims):
        offsets = [{}]
        for d in dims:
            offsets = [{**o, d: j} if j else o for o in offsets for j in range(self.size[d])]
        return [o for o in offsets if o]

    def moved(self, at, offset):
        return {d: lax.rem(at[d] + offset[d], self.size[d]) if d in offset else at[d] for d in DIMS}

    def barrier(self, offsets):
        at, sem = self.me(), pltpu.get_barrier_semaphore()
        for offset in offsets:
            pl.semaphore_signal(
                sem, inc=1, device_id=self.device(self.moved(at, offset)), device_id_type=MESH
            )
        pl.semaphore_wait(sem, len(offsets))


class Exchange:
    def __init__(self, grid, ref, send, recv):
        self.grid, self.ref, self.send, self.recv, self.at = grid, ref, send, recv, grid.me()
        self.groups = [("z", "c"), ("y", "x")]

    def copies(self, stage):
        done = self.groups[0] if stage else ()
        view = self.ref.at[tuple(slice(None) if d in done else self.at[d] for d in DIMS)]
        first = len(self.grid.around(self.groups[0])) if stage else 0
        for j, offset in enumerate(self.grid.around(self.groups[stage])):
            yield pltpu.make_async_remote_copy(
                src_ref=view,
                dst_ref=view,
                send_sem=self.send.at[first + j],
                recv_sem=self.recv.at[first + j],
                device_id=self.grid.device(self.grid.moved(self.at, offset)),
                device_id_type=MESH,
            )

    def start(self, stage):
        for copy in self.copies(stage):
            copy.start()

    def wait(self, stage):
        for copy in self.copies(stage):
            copy.wait_recv()

    def finish(self):
        for stage in range(2):
            for copy in self.copies(stage):
                copy.wait_send()


class Gather:
    def __init__(self, grid, pieces, send, recv, window=3, lag=3):
        self.grid, self.send, self.recv, self.at = grid, send, recv, grid.me()
        self.pieces = [(ref, sub, grid.order(order)) for ref, sub, order in pieces]
        self.stages, self.window, self.now = len(self.pieces[0][2]), window, 0
        self.events = [
            (step - stage * lag, stage)
            for step in range(len(pieces) + (self.stages - 1) * lag)
            for stage in range(self.stages)
            if 0 <= step - stage * lag < len(pieces)
        ]
        self.whole = [self.events.index((i, self.stages - 1)) + 1 for i in range(len(pieces))]

    def copies(self, i, stage):
        ref, sub, order = self.pieces[i]
        dim, done = order[stage], order[:stage]
        index = tuple(slice(None) if d in done else self.at[d] for d in DIMS)
        view = ref.at[index + sub]
        for j in range(1, self.grid.size[dim]):
            slot = self.grid.slot(dim, j)
            yield pltpu.make_async_remote_copy(
                src_ref=view,
                dst_ref=view,
                send_sem=self.send.at[i, slot],
                recv_sem=self.recv.at[i, slot],
                device_id=self.grid.device(self.grid.peer(self.at, dim, j)),
                device_id_type=MESH,
            )

    def start(self, i, stage):
        for copy in self.copies(i, stage):
            copy.start()

    def begin(self):
        for i in range(min(self.window, len(self.pieces))):
            self.start(i, 0)

    def run(self, first, last):
        for i, stage in self.events[first:last]:
            for copy in self.copies(i, stage):
                copy.wait_recv()
            if stage == 0 and i + self.window < len(self.pieces):
                self.start(i + self.window, 0)
            if stage < self.stages - 1:
                self.start(i, stage + 1)

    def until(self, last):
        self.run(self.now, max(self.now, last))
        self.now = max(self.now, last)

    def finish(self):
        self.until(len(self.events))
        for i in range(len(self.pieces)):
            for stage in range(self.stages):
                for copy in self.copies(i, stage):
                    copy.wait_send()

    def loop(self, count, marks, body):
        marks = [max(self.now, m) for m in marks]
        starts = [self.now] + marks[:-1]

        def step(t, _):
            for k in range(count):
                if marks[k] > starts[k]:

                    @pl.when(t == k)
                    def _():
                        self.run(starts[k], marks[k])

            body(t)
            return 0

        lax.fori_loop(0, count, step, 0)
        self.now = marks[-1]


class Scatter:
    def __init__(self, grid, pieces, send, recv):
        self.grid, self.send, self.recv, self.at = grid, send, recv, grid.me()
        self.pieces = [(src, sub, grid.order(order), bufs, out) for src, sub, order, bufs, out in pieces]
        self.stages = len(self.pieces[0][2])

    def pick(self, i, stage, where):
        src, sub, order, bufs, _ = self.pieces[i]
        left = tuple(d for d in DIMS if d not in order[:stage])
        index = tuple(where if d == order[stage] else slice(None) for d in left)
        if stage == 0:
            return src.at[index + sub]
        return bufs[stage - 1].at[(0,) + index]

    def copies(self, i, stage):
        _, _, order, bufs, _ = self.pieces[i]
        dim = order[stage]
        for j in range(1, self.grid.size[dim]):
            other = self.grid.peer(self.at, dim, j)
            slot = self.grid.slot(dim, j)
            yield pltpu.make_async_remote_copy(
                src_ref=self.pick(i, stage, other[dim]),
                dst_ref=bufs[stage].at[j - 1],
                send_sem=self.send.at[i, slot],
                recv_sem=self.recv.at[i, slot],
                device_id=self.grid.device(other),
                device_id_type=MESH,
            )

    def begin(self, i):
        for copy in self.copies(i, 0):
            copy.start()

    def run(self, events):
        for i, stage in events:
            self.add(i, stage)
            if stage < self.stages - 1:
                for copy in self.copies(i, stage + 1):
                    copy.start()

    def add(self, i, stage):
        _, _, order, bufs, out = self.pieces[i]
        for copy in self.copies(i, stage):
            copy.wait_recv()
        buf = bufs[stage]
        own = self.pick(i, stage, self.at[order[stage]])[...]
        if stage < self.stages - 1 and self.grid.size[order[stage]] == 2:
            buf[0] = own + buf[0]
            return
        total = own.astype(f32)
        for j in range(self.grid.size[order[stage]] - 1):
            total = total + buf[j].astype(f32)
        if stage == self.stages - 1:
            out[...] = total.reshape(out.shape)
        else:
            buf[0] = total.astype(buf.dtype)

    def finish(self):
        for i in range(len(self.pieces)):
            for stage in range(self.stages):
                for copy in self.copies(i, stage):
                    copy.wait_send()


def scatter_buffers(grid, order, rows, columns, dtype):
    shapes, left = [], list(DIMS)
    for d in grid.order(order):
        left.remove(d)
        shapes.append((grid.size[d] - 1,) + tuple(grid.size[e] for e in left) + (rows, columns))
    return [pltpu.VMEM(s, dtype) for s in shapes]


def cuts(total, parts, unit):
    while parts > 1 and total % (parts * unit):
        parts -= 1
    return [(j * (total // parts), total // parts) for j in range(parts)]


def dotg(a, b, ca, cb, precision=None):
    return lax.dot_general(
        a, b, (((ca,), (cb,)), ((), ())), preferred_element_type=f32, precision=precision
    )


def iota(shape, dim):
    return lax.broadcasted_iota(jnp.int32, shape, dim)


def three_parts(x):
    high = x.astype(bf16).astype(f32)
    mid = (x - high).astype(bf16).astype(f32)
    return high, mid, x - high - mid


def spread_vector(rows, n):
    shards, width = rows.shape
    total = shards * n
    place = (iota((width, total), 1) % n == iota((width, total), 0)).astype(f32).astype(bf16)
    wide = dotg(rows, place, 1, 0)
    keep = iota((shards, total), 1) // n == iota((shards, total), 0)
    return jnp.sum(jnp.where(keep, wide, 0.0), axis=0, keepdims=True)


def fold_vector(vector, shards, n, width):
    total = shards * n
    keep = iota((shards, total), 1) // n == iota((shards, total), 0)
    place = (iota((total, width), 0) % n == iota((total, width), 1)).astype(f32).astype(bf16)
    parts = [jnp.where(keep, part, 0.0).astype(bf16) for part in three_parts(vector)]
    return sum(dotg(part, place, 1, 0) for part in parts)


def attend_prepare(qkv_ref, prep, live, pair):
    length, width = qkv_ref.shape[0], qkv_ref.shape[1] // 3
    k = qkv_ref[:, pl.ds(pl.multiple_of(width + pair * LANES, LANES), LANES)].astype(f32)
    v = qkv_ref[:, pl.ds(pl.multiple_of(2 * width + pair * LANES, LANES), LANES)].astype(f32)
    lane, row = iota((length, LANES), 1), iota((length, LANES), 0)
    bias = jnp.where(row < live, 0.0, neg_fill)
    k = k * (1.0 / math.sqrt(HEAD_DIM))
    for h in range(2):
        mine, spare = lane // HEAD_DIM == h, HEAD_DIM * (1 - h)
        prep[h, 0] = jnp.where(mine, k, jnp.where(lane == spare, bias, 0.0)).astype(bf16)
        prep[h, 1] = jnp.where(mine, v, 1.0).astype(bf16)


def attend(qkv_ref, context_ref, lse_ref, prep, pair, rows, block):
    out = pl.ds(pl.multiple_of(pair * LANES, LANES), LANES)
    q = qkv_ref[rows, out].astype(f32)
    lane = iota((block, LANES), 1)
    low = lane < HEAD_DIM
    sums, tops = [], []
    for h in range(2):
        spare = HEAD_DIM * (1 - h)
        query = jnp.where(lane // HEAD_DIM == h, q, jnp.where(lane == spare, 1.0, 0.0)).astype(bf16)
        scores = dotg(query, prep[h, 0], 1, 1)
        top = jnp.max(scores, axis=1, keepdims=True)
        weights = jnp.exp(scores - top).astype(bf16)
        sums.append(dotg(weights, prep[h, 1], 1, 0))
        tops.append(top)
    num = jnp.where(low, sums[0], sums[1])
    den = pltpu.roll(jnp.where(low, sums[1], sums[0]), HEAD_DIM, 1)
    context_ref[rows, out] = (num / den).astype(bf16)
    total = jnp.where(low, tops[0], tops[1]) + jnp.log(den)
    other = pltpu.roll(total, HEAD_DIM, 1)
    kept = jnp.where(lane == 2 * pair + 1, other, lse_ref[rows, :])
    lse_ref[rows, :] = jnp.where(lane == 2 * pair, total, kept)


def gelu_parts(x):
    cdf = 0.5 * (1.0 + lax.erf(x * (1.0 / math.sqrt(2.0))))
    return cdf, jnp.exp(-0.5 * x * x) * (1.0 / math.sqrt(2.0 * math.pi))


def normalize(values):
    center = values - jnp.mean(values, axis=-1, keepdims=True)
    scale = lax.rsqrt(jnp.mean(center * center, axis=-1, keepdims=True) + eps_norm)
    return center * scale, scale


def gather_plan(shapes):
    plan, every = [("s", ())], slice(None)
    width = shapes["o"][1]
    for a, n in cuts(width, 3, LANES):
        plan += [("q", (every, pl.ds(part * width + a, n))) for part in range(3)]
    for name, parts in (("o", 2), ("u", 6), ("p", 2), ("d", 3)):
        rows, columns = shapes[name]
        for a, n in cuts(columns, parts, LANES):
            for b, m in cuts(rows, 2 if name == "d" else 1, 8):
                plan.append((name, (pl.ds(b, m) if name == "d" else every, pl.ds(a, n))))
    return [(name, sub, GATHER_ORDERS[i % len(GATHER_ORDERS)]) for i, (name, sub) in enumerate(plan)]


def forward_kernel(grid, plan, sizes, *refs):
    (len_ref, h_tokens, keep_a, keep_f, wq, wo, wu, wd, wp), refs = refs[:9], refs[9:]
    count = len(sizes)
    small_in, refs = refs[:count], refs[count:]
    kept_hbm, (act_t, slope), refs = refs[:16], refs[16:18], refs[18:]
    firsts, small_out, refs = refs[0], refs[1 : 1 + count], refs[1 + count :]
    kept, refs = refs[:16], refs[16:]
    (gq, go, gu, gd, gp, qkv_ref, context, lse, tokens_t, context_t, hidden_t, norm1, scale1, norm2, scale2, layer_out) = kept
    (gs, tokens_ref, keep, hidden, hidden_low, act, act_buf, slope_buf, prep, bias), refs = refs[:10], refs[10:]
    send, recv, own_sem, keep_sem, act_sem, slope_sem, out_sem, norm_sem = refs
    length, width = context.shape
    b_qv, b_out, g1, b1, b_up, b_down, g2, b2, b_pool = small_out
    outs = [pltpu.make_async_copy(src, dst, out_sem.at[i]) for i, (src, dst) in enumerate(zip(kept, kept_hbm))]

    def put(*which):
        for i, ref in enumerate(kept):
            if any(ref is w for w in which):
                outs[i].start()

    at = grid.me()
    own = tuple(at[d] for d in DIMS)
    to_own = []
    for i, (src, dst) in enumerate(((wq, gq), (wo, go), (wu, gu), (wd, gd), (wp, gp))):
        to_own.append(pltpu.make_async_copy(src, dst.at[own], own_sem.at[i]))
        to_own[-1].start()
    to_tokens = pltpu.make_async_copy(h_tokens, tokens_ref, own_sem.at[5])
    to_tokens.start()
    mine = gs.at[own]
    mine[...] = jnp.zeros(mine.shape, bf16)
    for i, (ref, n) in enumerate(zip(small_in, sizes)):
        mine[i : i + 1, 0:n] = ref[...]
    where = dict(q=gq, o=go, u=gu, d=gd, p=gp, s=gs)
    gather = Gather(grid, [(where[name], sub, order) for name, sub, order in plan], send, recv)
    number = {}
    for i, (name, _, _) in enumerate(plan):
        number.setdefault(name, []).append(i)
    end = {name: [gather.whole[i] for i in numbers] for name, numbers in number.items()}
    grid.barrier(grid.straight())
    for copy in to_own:
        copy.wait()
    gather.begin()
    load = pltpu.make_async_copy(keep_a, keep, keep_sem)
    load.start()
    to_tokens.wait()
    tokens_t[...] = tokens_ref[...].T
    lse[...] = jnp.zeros_like(lse)
    put(tokens_t)
    gather.until(end["s"][0])
    rows = gs[...].reshape((grid.count,) + gs.shape[-2:])
    for i, (ref, n) in enumerate(zip(small_out, sizes)):
        ref[...] = spread_vector(rows[:, i, :], n)
    bias[:, :width] = b_qv[:, :width]
    bias[:, width : 2 * width] = jnp.zeros((1, width), f32)
    bias[:, 2 * width :] = b_qv[:, width:]

    groups = len(number["q"]) // 3
    part = width // groups
    pairs, block = part // LANES, min(512, length)
    blocks, live = length // block, len_ref[0]
    each = pairs * blocks

    def attention(t):
        @pl.when(t % each == 0)
        def _():
            for j in range(3):
                cols = pl.ds(pl.multiple_of(j * width + t // each * part, part), part)
                out = dotg(tokens_ref[...], gq[:, :, :, :, :, cols].reshape(width, part), 1, 0)
                qkv_ref[:, cols] = (out + bias[:, cols]).astype(bf16)

        @pl.when(t % blocks == 0)
        def _():
            attend_prepare(qkv_ref, prep, live, t // blocks)

        rows = pl.ds(pl.multiple_of((t % blocks) * block, block), block)
        attend(qkv_ref, context, lse, prep, t // blocks, rows, block)

    slots = groups * each
    first, total = end["q"][2], len(gather.events)

    def by_then(share):
        return first + int(share * (total - first))

    gather.loop(
        slots,
        [max(end["q"][3 * (t // each) + 2], by_then(SHARES[0] * t / slots)) for t in range(slots)],
        attention,
    )
    put(gq, qkv_ref, context, lse)

    load.wait()
    block = min(512, length)
    blocks = length // block

    def row_block(t):
        return pl.ds(pl.multiple_of(t * block, block), block)

    gather.until(end["o"][-1])

    def project(t):
        here = row_block(t)
        attended = dotg(context[here, :], go[...].reshape(width, width), 1, 0) + b_out[...]
        total = tokens_ref[here, :].astype(f32) + attended * (keep[here, :].astype(f32) * keep_scale)
        norm, scale = normalize(total)
        out = norm * g1[...] + b1[...]
        hidden[here, :] = out
        hidden_low[here, :] = out.astype(bf16)
        hidden_t[:, here] = out.astype(bf16).T
        context_t[:, here] = context[here, :].T
        norm1[here, :] = norm.astype(bf16)
        scale1[here, :] = jnp.broadcast_to(scale, (block, LANES))

    gather.loop(blocks, [by_then(SHARES[0] + (SHARES[1] - SHARES[0]) * t / blocks) for t in range(blocks)], project)
    load = pltpu.make_async_copy(keep_f, keep, keep_sem)
    load.start()
    put(go, hidden_t, context_t, norm1, scale1)

    parts = len(end["u"])
    step = gu.shape[-1] // parts
    strip = min(128, length)

    def saved(t, cols):
        yield pltpu.make_async_copy(act_buf.at[t % 2], act_t.at[cols, :], act_sem.at[t % 2])
        yield pltpu.make_async_copy(slope_buf.at[t % 2], slope.at[:, cols], slope_sem.at[t % 2])

    def up(t):
        cols = pl.ds(pl.multiple_of(t * step, step), step)
        weight = gu[:, :, :, :, :, cols].reshape(width, step)

        @pl.when(t >= 2)
        def _():
            for copy in saved(t, cols):
                copy.wait()

        for i in range(length // strip):
            here = slice(i * strip, (i + 1) * strip)
            pre = dotg(hidden_low[here, :], weight, 1, 0) + b_up[:, cols]
            cdf, pdf = gelu_parts(pre)
            out = (pre * cdf).astype(bf16)
            act[here, cols] = out
            act_buf[t % 2, :, here] = out.T
            slope_buf[t % 2, here, :] = (cdf + pre * pdf).astype(bf16)
        for copy in saved(t, cols):
            copy.start()

    gather.loop(parts, [max(end["u"][t], by_then(SHARES[1] + (SHARES[2] - SHARES[1]) * t / parts)) for t in range(parts)], up)
    for t in range(max(0, parts - 2), parts):
        for copy in saved(t, pl.ds(0, step)):
            copy.wait()

    load.wait()
    put(gu)
    halves = len(cuts(gd.shape[-2], 2, 8))
    ends = end["d"][halves - 1 :: halves]
    parts = len(ends)
    step = width // parts

    def down(t):
        cols = pl.ds(pl.multiple_of(t * step, step), step)
        out = dotg(act[...], gd[:, :, :, :, :, cols].reshape(-1, step), 1, 0) + b_down[:, cols]
        hidden[:, cols] += out * (keep[:, cols].astype(f32) * keep_scale)

    gather.loop(parts, ends, down)
    put(gd, gp)
    block = min(256, length)
    blocks = length // block

    def left(t):
        for j, i in enumerate((13, 14, 15)):
            yield pltpu.make_async_copy(kept[i].at[row_block(t)], kept_hbm[i].at[row_block(t)], norm_sem.at[j, t])

    def norm(t):
        here = row_block(t)
        value, scale = normalize(hidden[here, :])
        out = value * g2[...] + b2[...]
        norm2[here, :] = value.astype(bf16)
        scale2[here, :] = jnp.broadcast_to(scale, (block, LANES))
        layer_out[here, :] = out.astype(bf16)
        for c in left(t):
            c.start()

        @pl.when(t == 0)
        def _():
            first = out[0:8].astype(bf16)
            pooled = jnp.tanh(dotg(first, gp[...].reshape(width, width), 1, 0) + b_pool[...])
            firsts[0:1, :] = pooled[0:1]
            firsts[1:2, :] = first[0:1].astype(f32)

    gather.loop(blocks, [gather.now] * blocks, norm)
    gather.finish()
    for copy in outs[:13]:
        copy.wait()
    for t in range(blocks):
        for c in left(t):
            c.wait()


def run_forward(grid, length_of, tokens, keep_a, keep_f, big, small):
    length, width = tokens.shape
    names = ("q", "o", "u", "d", "p")
    shapes = {k: w.shape for k, w in zip(names, big)}
    inner = shapes["u"][1]
    sizes = [v.shape[0] for v in small]
    plan = gather_plan(shapes)
    pad = -(-max(sizes) // LANES) * LANES
    step = inner // sum(p[0] == "u" for p in plan)
    vmem, anywhere = pl.BlockSpec(memory_space=pltpu.VMEM), pl.BlockSpec(memory_space=pl.ANY)
    shape = jax.ShapeDtypeStruct
    kept = [(grid.shape + shapes[k], bf16) for k in names] + [
        ((length, 3 * width), bf16),
        ((length, width), bf16),
        ((length, LANES), f32),
        ((width, length), bf16),
        ((width, length), bf16),
        ((width, length), bf16),
        ((length, width), bf16),
        ((length, LANES), f32),
        ((length, width), bf16),
        ((length, LANES), f32),
        ((length, width), bf16),
    ]
    return pl.pallas_call(
        functools.partial(forward_kernel, grid, plan, sizes),
        out_shape=[shape(*k) for k in kept]
        + [shape((inner, length), bf16), shape((length, inner), bf16), shape((2, width), f32)]
        + [shape((1, grid.count * n), f32) for n in sizes],
        in_specs=[pl.BlockSpec(memory_space=pltpu.SMEM)] + [anywhere] * 8 + [vmem] * len(small),
        out_specs=[anywhere] * 18 + [vmem] * (1 + len(small)),
        scratch_shapes=[pltpu.VMEM(*k) for k in kept]
        + [
            pltpu.VMEM(grid.shape + (16, pad), bf16),
            pltpu.VMEM((length, width), bf16),
            pltpu.VMEM((length, width), jnp.int32),
            pltpu.VMEM((length, width), f32),
            pltpu.VMEM((length, width), bf16),
            pltpu.VMEM((length, inner), bf16),
            pltpu.VMEM((2, step, length), bf16),
            pltpu.VMEM((2, length, step), bf16),
            pltpu.VMEM((2, 2, length, LANES), bf16),
            pltpu.VMEM((1, 3 * width), f32),
            pltpu.SemaphoreType.DMA((len(plan), grid.slots)),
            pltpu.SemaphoreType.DMA((len(plan), grid.slots)),
            pltpu.SemaphoreType.DMA((6,)),
            pltpu.SemaphoreType.DMA,
            pltpu.SemaphoreType.DMA((2,)),
            pltpu.SemaphoreType.DMA((2,)),
            pltpu.SemaphoreType.DMA((16,)),
            pltpu.SemaphoreType.DMA((3, length // min(256, length))),
        ],
        compiler_params=pltpu.CompilerParams(
            collective_id=0, has_side_effects=True, vmem_limit_bytes=VMEM_LIMIT
        ),
        name="forward",
    )(length_of, tokens, keep_a, keep_f, *big, *[v.reshape(1, -1) for v in small])


def pool_and_loss(views, partners_ref, wp, here, shard_rows, unit_ref, work, cls_grad, pool_w, pool_b, loss):
    high = lax.Precision.HIGHEST
    count, width = math.prod(views.shape[:4]), views.shape[-1]
    each = count // views.shape[0]

    def pooled_rows(z):
        rows = views[z].reshape((each,) + views.shape[-2:])
        pooled = rows[:, 0, :]
        scale = lax.rsqrt(jnp.sum(pooled * pooled, axis=1, keepdims=True) + 1e-06)
        return slice(z * each, (z + 1) * each), pooled, scale, rows[:, 1, :]

    for z in range(views.shape[0]):
        at, pooled, scale, cls = pooled_rows(z)
        unit_ref[at, :] = pooled * scale
        work[count + z * each : count + (z + 1) * each, :] = cls.astype(bf16)
    unit = unit_ref[0:count, :]
    sims = dotg(unit, unit, 1, 1, high) / logit_divisor
    column, row = iota((count, count), 1), iota((count, count), 0)
    others = jnp.where(row == column, neg_fill, sims)
    top = jnp.max(others, axis=1, keepdims=True)
    weights = jnp.exp(others - top)
    total = jnp.sum(weights, axis=1, keepdims=True)
    partner = row == partners_ref[...]
    target = jnp.sum(jnp.where(partner, sims, 0.0), axis=1, keepdims=True)
    lost = jnp.sum(top + jnp.log(total) - target, axis=0, keepdims=True) / count
    loss[...] = jnp.broadcast_to(lost, loss.shape)
    pull = weights / total - jnp.where(partner, 1.0, 0.0)
    pull = pull + dotg(pull, (row == column).astype(f32), 0, 0, high)
    for z in range(views.shape[0]):
        at, pooled, scale, _ = pooled_rows(z)
        unit_grad = dotg(pull[at], unit, 1, 0, high) / logit_divisor
        along = jnp.sum(pooled * unit_grad, axis=1, keepdims=True)
        pooled_grad = scale * unit_grad - pooled * (scale * scale * scale * along)
        work[at, :] = (pooled_grad * (1.0 - pooled * pooled)).astype(bf16)
    pre, cls = work[0:count, :], work[count : 2 * count, :]
    mine = jnp.sum(jnp.where(iota((count, width), 0) == here, pre.astype(f32), 0.0), axis=0, keepdims=True)
    cls_grad[...] = dotg(jnp.broadcast_to(mine, (8, width)).astype(bf16), wp, 1, 1)
    place = (iota((width, LANES), 0) == here * shard_rows + iota((width, LANES), 1)).astype(f32).astype(bf16)
    cls_rows = dotg(cls, place, 1, 0).astype(bf16)
    pool_w[...] = dotg(cls_rows, pre, 0, 0)[:shard_rows]
    sums = jnp.broadcast_to(jnp.sum(pre.astype(f32), axis=0, keepdims=True), (8, width))
    pool_b[...] = sum(dotg(part.astype(bf16), place, 1, 0) for part in three_parts(sums))


def attend_back(qkv_ref, context, dcontext, lse, live, pair, prep):
    length, width = qkv_ref.shape[0], context.shape[1]
    scale = 1.0 / math.sqrt(HEAD_DIM)
    one = pl.ds(pl.multiple_of(pair * LANES, LANES), LANES)

    def col(part):
        return pl.ds(pl.multiple_of(part * width + pair * LANES, LANES), LANES)

    q, k, v = (qkv_ref[:, col(j)].astype(f32) for j in range(3))
    d = dcontext[:, one].astype(f32)
    lane, row = iota((length, LANES), 1), iota((length, LANES), 0)
    bias = jnp.where(row < live, 0.0, neg_fill)
    mine, place = lane // HEAD_DIM, lane % HEAD_DIM
    source, target = iota((LANES, LANES), 0), iota((LANES, LANES), 1)
    swap = (source // HEAD_DIM != target // HEAD_DIM).astype(f32).astype(bf16)
    both = d * context[:, one].astype(f32)
    inner = sum(dotg(part.astype(bf16), swap, 1, 0) for part in three_parts(both))
    d0, d1, d2 = three_parts(-inner)
    extra_d = jnp.where(place == 0, d0, jnp.where(place == 1, d1, jnp.where(place == 2, d2, 0.0)))
    extra_q = jnp.where(place == 0, 1.0, 0.0)
    for j, part in enumerate(three_parts(-lse[...])):
        head = jnp.where(target < HEAD_DIM, 2 * pair + 1, 2 * pair)
        pick = ((source == head) & (target % HEAD_DIM == j + 1)).astype(f32).astype(bf16)
        extra_q = extra_q + dotg(part.astype(bf16), pick, 1, 0)
    extra_k = jnp.where(place == 0, bias, jnp.where(place < 4, 1.0, 0.0))
    extra_v = jnp.where(place < 3, 1.0, 0.0)
    q = q * scale
    for h in range(2):
        here = mine == h
        prep[h, 0] = jnp.where(here, q, extra_q).astype(bf16)
        prep[h, 1] = jnp.where(here, k, extra_k).astype(bf16)
        prep[h, 2] = jnp.where(here, d, extra_d).astype(bf16)
        prep[h, 3] = jnp.where(here, v, extra_v).astype(bf16)
        prep[h, 4] = jnp.where(here, k * scale, 0.0).astype(bf16)
    return q.astype(bf16).T, d.astype(bf16).T


def scatter_plan(grid, shapes):
    plan, every = [], slice(None)
    width = shapes["o"][1]
    rows, columns = shapes["d"]
    plan += [("d", (pl.ds(a, n), every), n, columns) for a, n in cuts(rows, 6, 8)]
    for name, parts in (("u", 6), ("o", 2)):
        rows, columns = shapes[name]
        plan += [(name, (every, pl.ds(a, n)), rows, n) for a, n in cuts(columns, parts, LANES)]
    for a, n in cuts(width, 3, LANES):
        plan += [("q", (every, pl.ds(part * width + a, n)), shapes["q"][0], n) for part in range(3)]
    plan.append(("s", (), 16, shapes["s"]))
    return [(p[0], p[1], SCATTER_ORDERS[i % 2]) + p[2:] for i, p in enumerate(plan)]


def backward_kernel(grid, whole, plan, sizes, shard_rows, *refs):
    (len_ref, partners_ref, firsts, g1, g2), refs = refs[:5], refs[5:]
    (h_cot, h_keep_a, h_keep_f, h_norm1, h_scale1, h_norm2, h_scale2, h_act, h_slope, h_hidden, h_context_t), refs = refs[:11], refs[11:]
    (h_qkv, h_context, h_lse, h_tokens, h_wq, h_wo, h_wu, h_wd, h_wp), refs = refs[:9], refs[9:]
    (rq, ro, ru, rd, rs, pool_w, pool_b, loss, h_tokens_grad), refs = refs[:9], refs[9:]
    (dd, du, do, dsmall, grad, gctx, low, norm, keep, scale, vec, cls_grad, views, wp), refs = refs[:14], refs[14:]
    (send, recv, view_send, view_recv, sems, pair_sems), bufs = refs[:6], list(refs[6:])
    length, width = grad.shape
    inner = vec.shape[1]
    sources, results = dict(d=dd, u=du, o=do, s=dsmall), dict(d=rd, u=ru, o=ro, q=rq, s=rs)
    number = {}
    for i, p in enumerate(plan):
        number.setdefault(p[0], []).append(i)
    cot = low

    def copy(k, src, dst):
        return pltpu.make_async_copy(src, dst, sems.at[k])

    first_loads = [copy(0, h_cot, cot), copy(1, h_norm2, norm), copy(2, h_scale2, scale), copy(3, h_keep_f, keep), copy(4, h_wp, wp)]
    for c in first_loads:
        c.start()
    at_all = whole.me()
    views[tuple(at_all[d] for d in DIMS)] = firsts[...]
    exchange = Exchange(whole, views, view_send, view_recv)
    whole.barrier(whole.straight() + [o for o in whole.around(("z", "c")) + whole.around(("y", "x")) if len(o) > 1])
    exchange.start(0)
    vec[...] = jnp.zeros_like(vec)
    for c in first_loads:
        c.wait()
    strip = min(128, length)
    strips = length // strip

    def strip_of(t):
        return pl.ds(pl.multiple_of(t * strip, strip), strip)

    def add_row(j, x):
        vec[j : j + 1, : x.shape[1]] += jnp.sum(x, axis=0, keepdims=True)

    def norm_back(here, up, gain, slot):
        value = norm[here, :].astype(f32)
        scaled = up * gain[...]
        along = jnp.mean(scaled * value, axis=1, keepdims=True)
        back = scale[here, 0:1] * (scaled - jnp.mean(scaled, axis=1, keepdims=True) - value * along)
        add_row(slot, up * value)
        add_row(slot + 1, up)
        grad[here, :] = back
        out = (back * (keep[here, :].astype(f32) * keep_scale)).astype(bf16)
        low[here, :] = out
        return out.astype(f32)

    def second_norm(t, extra):
        here = strip_of(t)
        up = cot[here, :].astype(f32)
        if extra is not None:
            up = up + jnp.where(iota((strip, width), 0) + t * strip == 0, extra, 0.0)
        add_row(5, norm_back(here, up, g2, 6))
        return 0

    held = -(-math.prod(whole.shape) // strip)
    def rest_of_norm(t, _):
        @pl.when(t == (held + strips) // 2)
        def _():
            exchange.wait(0)
            exchange.start(1)

        return second_norm(t, None)

    lax.fori_loop(held, strips, rest_of_norm, 0)
    exchange.wait(1)
    here = lax.axis_index("dp") * (whole.size["y"] * whole.size["x"]) + lax.axis_index("fsdp")
    pool_and_loss(views, partners_ref, wp[...], here, shard_rows, grad, gctx, cls_grad, pool_w, pool_b, loss)
    lax.fori_loop(0, held, lambda t, _: second_norm(t, cls_grad[0:1, :]), 0)
    wo = wp
    second_loads = [copy(1, h_norm1, norm), copy(2, h_scale1, scale), copy(3, h_keep_a, keep), copy(6, h_wo, wo)]
    for c in second_loads:
        c.start()

    pieces, left = [], bufs
    for name, sub, order, _, _ in plan:
        n = len(grid.order(order))
        pieces.append([sources.get(name), sub, order, left[:n], results[name].at[sub] if sub else results[name]])
        left = left[n:]
    groups = len(number["q"]) // 3
    early, last = len(plan) - 1 - len(number["q"]), len(plan) - 1
    scatter = Scatter(grid, pieces, send, recv)
    stages, lag = scatter.stages, 4
    steps = [
        [(j - stage * lag, stage) for stage in range(stages) if 0 <= j - stage * lag < early]
        for j in range(early + (stages - 1) * lag)
    ]

    def feed_forward(act, slope, wd, wu, gup, turned):
        third = [copy(5, h_hidden, turned), copy(7, h_context_t, turned)]
        third[0].start()
        block = min(256, length)
        chunk, part = act.shape[1], slope.shape[2]
        chunks, parts = inner // chunk, inner // part
        slab = wu.shape[1]

        def act_load(t):
            return pltpu.make_async_copy(h_act.at[pl.ds(pl.multiple_of(t * chunk, chunk), chunk), :], act.at[t % 2], pair_sems.at[0, t % 2])

        def part_loads(t):
            cols = pl.ds(pl.multiple_of(t * part, part), part)
            yield pltpu.make_async_copy(h_slope.at[:, cols], slope.at[t % 2], pair_sems.at[1, t % 2])
            yield pltpu.make_async_copy(h_wd.at[cols, :], wd.at[t % 2], pair_sems.at[2, t % 2])

        def slab_load(t):
            return pltpu.make_async_copy(h_wu.at[pl.ds(pl.multiple_of(t * slab, slab), slab), :], wu.at[t % 2], pair_sems.at[3, t % 2])

        act_load(0).start()
        for c in part_loads(0):
            c.start()
        slab_load(0).start()
        across = grid.size["y"] * grid.size["x"]

        def down_weight(t, _):
            @pl.when(t + 1 < chunks)
            def _():
                act_load(t + 1).start()

            act_load(t).wait()
            out = dotg(act[t % 2], low[...], 1, 0).astype(bf16)
            dd[t // grid.size["c"], t % grid.size["c"]] = out.reshape(dd.shape[2:])
            return 0

        lax.fori_loop(0, chunks, down_weight, 0)
        for i in number["d"]:
            scatter.begin(i)
        third[0].wait()

        def up_part(t, _):
            cols = pl.ds(pl.multiple_of(t * part, part), part)

            @pl.when(t + 1 < parts)
            def _():
                for c in part_loads(t + 1):
                    c.start()

            for c in part_loads(t):
                c.wait()
            for i in range(length // block):
                rows = slice(i * block, (i + 1) * block)
                out = dotg(low[rows, :], wd[t % 2], 1, 1) * slope[t % 2, rows, :].astype(f32)
                gup[rows, cols] = out.astype(bf16)
            vec[4:5, cols] = jnp.sum(gup[:, cols].astype(f32), axis=0, keepdims=True)
            out = dotg(turned[...], gup[:, cols], 1, 0).astype(bf16)
            du[:, :, :, :, :, cols] = out.reshape(grid.shape + (-1, part))
            for k, i in enumerate(number["u"]):

                @pl.when(t == k)
                def _():
                    scatter.begin(i)
                    scatter.run(steps[k])

            return 0

        lax.fori_loop(0, parts, up_part, 0)
        third[1].start()

        def hidden_part(t, _):
            cols = pl.ds(pl.multiple_of(t * slab, slab), slab)

            @pl.when(t + 1 < width // slab)
            def _():
                slab_load(t + 1).start()

            slab_load(t).wait()
            grad[:, cols] += dotg(gup[...], wu[t % 2], 1, 1)
            for k in range(width // slab):

                @pl.when(t == k)
                def _():
                    scatter.run(steps[parts + k])

            return 0

        lax.fori_loop(0, width // slab, hidden_part, 0)
        for c in second_loads:
            c.wait()

        def first_norm(t, _):
            add_row(1, norm_back(strip_of(t), grad[strip_of(t), :], g1, 2))
            return 0

        lax.fori_loop(0, strips, first_norm, 0)
        for c in (copy(9, h_context, norm), copy(10, h_lse, scale)):
            c.start()
        third[1].wait()
        for i in number["o"]:
            cols = plan[i][1][1]
            out = dotg(turned[...], low[:, cols], 1, 0).astype(bf16)
            do[:, :, :, :, :, cols] = out.reshape(grid.shape + (-1, cols.size))
            scatter.begin(i)
        for i in range(length // block):
            rows = slice(i * block, (i + 1) * block)
            gctx[rows, :] = dotg(low[rows, :], wo[...], 1, 1).astype(bf16)
        scatter.run(steps[parts + width // slab])
        return parts + width // slab + 1

    chunk, part, slab = inner // (grid.size["z"] * grid.size["c"]), inner // len(number["u"]), width // 3
    done = []

    def first_scope(*refs):
        done.append(feed_forward(*refs))

    pl.run_scoped(
        first_scope,
        pltpu.VMEM((2, chunk, length), bf16),
        pltpu.VMEM((2, length, part), bf16),
        pltpu.VMEM((2, part, width), bf16),
        pltpu.VMEM((2, slab, inner), bf16),
        pltpu.VMEM((length, inner), bf16),
        pltpu.VMEM((width, length), bf16),
    )
    step = done[0]

    def attention(qkv, tokens_t, wq, dq, prep, turned, acc):
        context, lse = norm, scale
        block = min(256, length) if grid.with_fsdp else min(128, length)
        blocks = length // block

        def rows_of(t):
            return pl.ds(pl.multiple_of(t * block, block), block)

        for i in number["q"]:
            scatter.pieces[i] = (dq,) + scatter.pieces[i][1:]
        span = width // groups

        def group_loads(g):
            for j in range(3):
                cols = pl.ds(j * width + g * span, span)
                yield pltpu.make_async_copy(h_qkv.at[:, cols], qkv.at[:, cols], pair_sems.at[j, g % 2])

        for g in range(min(2, groups)):
            for c in group_loads(g):
                c.start()
        loads = [copy(11, h_tokens, tokens_t), copy(12, h_wq.at[:, 0:width], wp)]
        loads += [copy(6, h_wq.at[:, width : 2 * width], wq.at[0]), copy(7, h_wq.at[:, 2 * width :], wq.at[1])]
        for c in loads:
            c.start()
        for c in (copy(9, h_context, norm), copy(10, h_lse, scale)):
            c.wait()
        each = span // LANES * blocks
        slots = groups * each
        live = len_ref[0]
        head = [slice(h * HEAD_DIM, (h + 1) * HEAD_DIM) for h in range(2)]
        due, late = [[] for _ in range(slots)], []
        for j, events in enumerate(steps[step:]):
            due[j * (slots - each // 2) // (len(steps) - step)] += events
        for g in range(groups - 1):
            for stage in range(stages):
                at, events = each * (g + 1) - 1 + SPACING * (stage + 1), [(i, stage) for i in number["q"][3 * g : 3 * g + 3]]
                if at < slots:
                    due[at] += events
                else:
                    late.append(events)
        tail = [late[j] if j < len(late) else [] for j in range(max(stages, len(late)))]
        for stage in range(stages):
            tail[len(tail) - stages + stage] += [(i, stage) for i in number["q"][-3:] + [last]]

        def slot(t, _):
            pair, b = t // blocks, t % blocks
            rows = rows_of(b)
            one = pl.ds(pl.multiple_of(pair * LANES, LANES), LANES)

            for g in range(groups):

                @pl.when(t == g * each)
                def _():
                    for c in group_loads(g):
                        c.wait()
                    if g + 2 < groups:
                        for c in group_loads(g + 2):
                            c.start()

            @pl.when(b == 0)
            def _():
                turned[0], turned[1] = attend_back(qkv, context, gctx, lse, live, pair, prep)
                acc[...] = jnp.zeros_like(acc)

            dq_rows = jnp.zeros((block, LANES), f32)
            for h in range(2):
                p = jnp.exp(dotg(prep[h, 0, rows, :], prep[h, 1], 1, 1))
                dp = dotg(prep[h, 2, rows, :], prep[h, 3], 1, 1)
                ds = (p * dp).astype(bf16)
                acc[0, head[h], :] += dotg(turned[1, head[h], rows], p.astype(bf16), 1, 0)
                acc[1, head[h], :] += dotg(turned[0, head[h], rows], ds, 1, 0)
                dq_rows = dq_rows + dotg(ds, prep[h, 4], 1, 0)
            qkv[rows, one] = dq_rows.astype(bf16)

            @pl.when(b == blocks - 1)
            def _():
                qkv[:, pl.ds(pl.multiple_of(width + pair * LANES, LANES), LANES)] = acc[1].astype(bf16).T
                qkv[:, pl.ds(pl.multiple_of(2 * width + pair * LANES, LANES), LANES)] = acc[0].astype(bf16).T

            for k in range(slots):
                if due[k]:

                    @pl.when(t == k)
                    def _():
                        scatter.run(due[k])

            @pl.when(t == each - 1)
            def _():
                loads[0].wait()

            @pl.when(t % each == each - 1)
            def _():
                for j in range(3):
                    cols = pl.ds(pl.multiple_of(j * width + t // each * span, LANES), span)
                    out = dotg(tokens_t[...], qkv[:, cols], 1, 0).astype(bf16)
                    dq[:, :, :, :, :, cols] = out.reshape(grid.shape + (-1, span))
                for g in range(groups):

                    @pl.when(t == each * (g + 1) - 1)
                    def _():
                        for i in number["q"][3 * g : 3 * g + 3]:
                            scatter.begin(i)

            return 0

        lax.fori_loop(0, slots, slot, 0)
        sums = dotg(jnp.ones((8, length), bf16), qkv[...], 1, 0)[0:1]
        vec[0:1, :width] = sums[:, :width]
        vec[0:1, width : 2 * width] = sums[:, 2 * width :]
        pad = dsmall.shape[-1]
        dsmall[...] = jnp.zeros_like(dsmall)
        for j, n in enumerate(sizes):
            folded = fold_vector(vec[j : j + 1, : grid.count * n], grid.count, n, pad)
            dsmall[:, :, :, :, j, :] = folded.reshape(grid.shape + (pad,))
        scatter.begin(number["s"][0])
        for c in loads[1:]:
            c.wait()
        rows = length // len(tail)
        for i, events in enumerate(tail):
            here = slice(i * rows, (i + 1) * rows)
            total = grad[here, :] + dotg(qkv[here, :width], wp[...], 1, 1)
            for j in range(2):
                total = total + dotg(qkv[here, (j + 1) * width : (j + 2) * width], wq[j], 1, 1)
            low[here, :] = total.astype(bf16)
            scatter.run(events)
        out = copy(13, low, h_tokens_grad)
        out.start()
        scatter.finish()
        exchange.finish()
        out.wait()

    pl.run_scoped(
        attention,
        pltpu.VMEM((length, 3 * width), bf16),
        pltpu.VMEM((width, length), bf16),
        pltpu.VMEM((2, width, width), bf16),
        pltpu.VMEM(grid.shape + (width // grid.count, 3 * width), bf16),
        pltpu.VMEM((2, 5, length, LANES), bf16),
        pltpu.VMEM((2, LANES, length), bf16),
        pltpu.VMEM((2, LANES, length), f32),
    )


def run_backward(grid, whole, length_of, partners, firsts, gains, hbm, length, width, inner, sizes, shard_rows):
    rows = width // grid.count
    pad = -(-max(sizes) // LANES) * LANES
    shapes = {"q": (rows, 3 * width), "o": (rows, width), "u": (rows, inner), "d": (inner // grid.count, width), "s": pad}
    plan = scatter_plan(grid, shapes)
    bufs = []
    for name, _, order, r, c in plan:
        bufs += scatter_buffers(grid, order, r, c, f32 if name == "s" else bf16)
    views_count = len(whole.around(("z", "c"))) + len(whole.around(("y", "x")))
    vmem, anywhere = pl.BlockSpec(memory_space=pltpu.VMEM), pl.BlockSpec(memory_space=pl.ANY)
    shape = jax.ShapeDtypeStruct
    return pl.pallas_call(
        functools.partial(backward_kernel, grid, whole, plan, sizes, shard_rows),
        out_shape=[shape(shapes[k], f32) for k in ("q", "o", "u", "d")]
        + [
            shape((16, pad), f32),
            shape((shard_rows, width), f32),
            shape((8, LANES), f32),
            shape((8, LANES), f32),
            shape((length, width), bf16),
        ],
        in_specs=[pl.BlockSpec(memory_space=pltpu.SMEM)] + [vmem] * 4 + [anywhere] * len(hbm),
        out_specs=[vmem] * 8 + [anywhere],
        scratch_shapes=[pltpu.VMEM(grid.shape + shapes[k], bf16) for k in ("d", "u", "o")]
        + [
            pltpu.VMEM(grid.shape + (16, pad), f32),
            pltpu.VMEM((length, width), f32),
            pltpu.VMEM((length, width), bf16),
            pltpu.VMEM((length, width), bf16),
            pltpu.VMEM((length, width), bf16),
            pltpu.VMEM((length, width), jnp.int32),
            pltpu.VMEM((length, LANES), f32),
            pltpu.VMEM((16, inner), f32),
            pltpu.VMEM((8, width), f32),
            pltpu.VMEM(whole.shape + (2, width), f32),
            pltpu.VMEM((width, width), bf16),
            pltpu.SemaphoreType.DMA((len(plan), grid.slots)),
            pltpu.SemaphoreType.DMA((len(plan), grid.slots)),
            pltpu.SemaphoreType.DMA((views_count,)),
            pltpu.SemaphoreType.DMA((views_count,)),
            pltpu.SemaphoreType.DMA((14,)),
            pltpu.SemaphoreType.DMA((4, 2)),
        ]
        + bufs,
        compiler_params=pltpu.CompilerParams(
            collective_id=1, has_side_effects=True, vmem_limit_bytes=VMEM_LIMIT
        ),
        name="backward",
    )(length_of, partners.reshape(1, -1), firsts, *gains, *hbm)


def finish_kernel(count, *refs):
    wide, narrow, refs = refs[:count], refs[count : count + 3], refs[count + 3 :]
    wide_out, refs = refs[:count], refs[count:]
    vectors, (bias, loss), refs = refs[:-count - 4], refs[-count - 4 : -count - 2], refs[-count - 2 :]
    bufs, (in_sem, out_sem) = refs[:count], refs[count:]
    loads = [pltpu.make_async_copy(a, b, in_sem.at[i]) for i, (a, b) in enumerate(zip(wide, bufs))]
    stores = [pltpu.make_async_copy(b, a, out_sem.at[i]) for i, (a, b) in enumerate(zip(wide_out, bufs))]
    for c in loads:
        c.start()
    for j, ref in enumerate(vectors):
        ref[...] = narrow[0][j : j + 1, : ref.shape[1]]
    bias[...] = narrow[1][0:1, : bias.shape[1]]
    loss[...] = narrow[2][0:1, 0:1]
    for load, store in zip(loads, stores):
        load.wait()
        store.start()
    for c in stores:
        c.wait()


def finish(wide, narrow, sizes):
    vmem, anywhere = pl.BlockSpec(memory_space=pltpu.VMEM), pl.BlockSpec(memory_space=pl.ANY)
    shape, count = jax.ShapeDtypeStruct, len(wide)
    outs = pl.pallas_call(
        functools.partial(finish_kernel, count),
        out_shape=[shape(w.shape, w.dtype) for w in wide] + [shape((1, n), f32) for n in sizes] + [shape((1, 1), f32)],
        in_specs=[anywhere] * count + [vmem] * 3,
        out_specs=[anywhere] * count + [vmem] * (len(sizes) + 1),
        scratch_shapes=[pltpu.VMEM(w.shape, w.dtype) for w in wide] + [pltpu.SemaphoreType.DMA((count,))] * 2,
        name="results",
    )(*wide, *narrow)
    return outs[:count], [v.reshape(-1) for v in outs[count:-1]], outs[-1].reshape(())


def on_device(whole, grid, tokens, lengths, keep_attn, keep_ffn, partners, out_cot, *weights):
    (w_qkv, b_qv, w_out, b_out, ln1_gain, ln1_bias, w_up, b_up, w_down, b_down, ln2_gain, ln2_bias, w_pool, b_pool) = weights
    _, length, width = tokens.shape
    inner = w_up.shape[1]
    big = [w_qkv, w_out, w_up, w_down, w_pool]
    small = [b_qv, b_out, ln1_gain, ln1_bias, b_up, b_down, ln2_gain, ln2_bias, b_pool]
    shard_rows = w_qkv.shape[0]
    if not grid.with_fsdp:
        big = [lax.all_gather(w, "fsdp", axis=0, tiled=True) for w in big]
        small = [lax.all_gather(v, "fsdp", axis=0, tiled=True) for v in small]
    sizes = [v.shape[0] for v in small][:-1]
    flat = (length, width)
    keep_a, keep_f = keep_attn.reshape(flat), keep_ffn.reshape(flat)
    outs = run_forward(grid, lengths, tokens.reshape(flat), keep_a, keep_f, big, small)
    wq, wo, wu, wd, wp = (g.reshape(-1, g.shape[-1]) for g in outs[:5])
    qkv, context, lse, tokens_t, context_t, hidden_t, norm1, scale1, norm2, scale2, layer_out = outs[5:16]
    act_t, slope, firsts = outs[16:19]
    vectors = outs[19:]
    hbm = [
        out_cot.reshape(flat), keep_a, keep_f, norm1, scale1, norm2, scale2, act_t, slope, hidden_t, context_t,
        qkv, context, lse, tokens_t, wq, wo, wu, wd, wp,
    ]
    rq, ro, ru, rd, rs, pool_w, pool_b, loss, tokens_grad = run_backward(
        grid, whole, lengths, partners, firsts, [vectors[2], vectors[6]], hbm, length, width, inner, sizes, shard_rows
    )
    if grid.with_fsdp:
        wide, vectors, loss = finish([layer_out, tokens_grad, rq, ro, ru, rd, pool_w], [rs, pool_b, loss], sizes + [shard_rows])
        layer_out, tokens_grad, rq, ro, ru, rd, pool_w = wide
    else:
        owned = [rq, ro, ru, rd] + [rs[j, :n] for j, n in enumerate(sizes)]
        rq, ro, ru, rd, *vectors = [lax.psum_scatter(g, "fsdp", scatter_dimension=0, tiled=True) for g in owned]
        vectors, loss = vectors + [pool_b[0, :shard_rows]], loss[0, 0]
    s_qv, s_out, s_g1, s_b1, s_up, s_down, s_g2, s_b2, s_pool = vectors
    return (
        layer_out.reshape(tokens.shape), tokens_grad.reshape(tokens.shape), rq, s_qv, ro, s_out, s_g1, s_b1, ru, s_up,
        rd, s_down, s_g2, s_b2, pool_w, s_pool, loss,
    )


def solution(mesh):
    rows, vector, matrix = P(AXES, None, None), P(AXES), P(AXES, None)
    weights = (matrix, vector, matrix, vector, vector, vector, matrix, vector, matrix, vector, vector, vector, matrix, vector)
    devices = mesh.shape["dp"] * mesh.shape["fsdp"]

    def step(*args):
        whole = Grid(mesh)
        grid = whole if (args[6].shape[0] // devices) % 8 == 0 else Grid(mesh, False)
        return jax.shard_map(
            functools.partial(on_device, whole, grid),
            mesh=mesh,
            in_specs=(rows, vector, rows, rows, P(), rows) + weights,
            out_specs=(rows, rows) + weights + (P(),),
            check_vma=False,
        )(*args)

    return step
```
